32 devices in a mesh: lat: 16 (over z, y, x), lon: 2 (over core).
Axes of the slice: x: 2, y: 2, z: 4, core: 2. Of those that a mesh axis runs over, the one named last changes fastest.
Arguments:
- elevation: float32 [1, 3072, 8640], P(None, 'lat', 'lon'), may hold values from -30 to 30
- velocity: float32 [1, 2, 3072, 8640], P(None, None, 'lat', 'lon'), may hold values from -3 to 3
- wind_forcing: float32 [2, 3072, 8640], P(None, 'lat', 'lon'), may hold values from -0.6 to 0.6
- ocean_depth: float32 [3072, 8640], P('lat', 'lon'), may hold values from 0.2 to 1
- wet_mask: int32 [3072, 8640], P('lat', 'lon'), may hold values from 0 to 1, as said below
- love_factor: float32 [1081], replicated, may hold values from 0.3 to 3
- wavenumbers: int32 [16], replicated, may hold values from 0 to 31, as said below
Outputs:
- new_elevation: float32 [1, 3072, 8640], P(None, 'lat', 'lon')
- new_velocity: float32 [1, 2, 3072, 8640], P(None, None, 'lat', 'lon')
- self_loading: float32 [1, 3072, 8640], P(None, 'lat', 'lon')
The draws below stay inside these ranges and needn't reach their ends.
Inputs may be any that keep to these rules, and one draw needn't show every extreme that they name: `wet_mask`: 0 in the 24 rows nearest each pole. `wavenumbers`: distinct.
All inputs are finite; a program needn't handle non-finite values.
Results may differ from the reference program's by a relative error of at most 0.0003.
Values sent between devices are 32-bit elements; how exact they have to be, the bound alone decides.
No kernel may reach another device: no remote copies, remote signals or barrier semaphores. Data moves between devices by JAX's collectives and lax.ppermute only.
A program may use at most 128 MiB of HBM per device.

```python
import math
import jax
import jax.numpy as jnp
from jax import lax

GRID_LAT = 3072
GRID_LON = 8640
DEGREES = 1081
MEMBERS = 1
TIME_STEPS = 1
WAVE_SET = 16


def window_numbers(key):
    pool_size = min(DEGREES, 2 * WAVE_SET)
    return jax.random.permutation(jax.random.fold_in(key, 7), pool_size)[:WAVE_SET].astype(jnp.int32)


def draw_elevation(key, part):
    keys = jax.random.split(key, 6)
    wave_orders = jax.random.randint(keys[0], (16,), 0, 16)
    lat_orders = jax.random.randint(keys[1], (16,), 0, 7)
    amplitude = jax.random.uniform(keys[2], (MEMBERS, 16), jnp.float32, -1.2, 1.2)
    phases = jax.random.uniform(keys[3], (MEMBERS, 16), jnp.float32, 0.0, 2.0 * jnp.pi)
    polar_angle = jnp.pi * (jnp.arange(GRID_LAT).astype(jnp.float32) + 0.5) / GRID_LAT
    longitude = 2.0 * jnp.pi * jnp.arange(GRID_LON).astype(jnp.float32) / GRID_LON
    profile = jnp.cos(lat_orders.astype(jnp.float32)[:, None] * polar_angle[None, :])
    cosines = jnp.cos(wave_orders.astype(jnp.float32)[:, None] * longitude[None, :])
    sines = jnp.sin(wave_orders.astype(jnp.float32)[:, None] * longitude[None, :])
    left_cos = (amplitude * jnp.cos(phases))[:, :, None] * profile[None]
    left_sin = (amplitude * jnp.sin(phases))[:, :, None] * profile[None]
    smooth = jnp.einsum('ecj,ck->ejk', left_cos, cosines) - jnp.einsum('ecj,ck->ejk', left_sin, sines)
    window = window_numbers(key)
    window_phase = window[:, None] * jnp.arange(GRID_LON, dtype=jnp.int32)[None, :] % GRID_LON
    window_angle = 2.0 * jnp.pi / GRID_LON * window_phase.astype(jnp.float32)
    window_cos = jnp.cos(window_angle)
    window_sin = jnp.sin(window_angle)
    shape = (MEMBERS, GRID_LAT, GRID_LON)
    profile_shape = (MEMBERS, 2, WAVE_SET, GRID_LAT)
    rows_rough = jax.random.truncated_normal(keys[5], -3.0, 3.0, profile_shape, jnp.float32)
    banded = jnp.einsum('ewj,wk->ejk', rows_rough[:, 0], window_cos) + jnp.einsum('ewj,wk->ejk', rows_rough[:, 1], window_sin)
    rough = 0.3 * jax.random.truncated_normal(keys[4], -3.0, 3.0, shape, jnp.float32)
    total = smooth + rough + banded
    return jnp.clip(total, -30.0, 30.0)


def draw_wet_mask(key, part):
    rows_index = jnp.arange(GRID_LAT, dtype=jnp.int32)[:, None]
    polar_cap = GRID_LAT // 128
    coins = jax.random.randint(key, (GRID_LAT, GRID_LON), 0, 5)
    wet = (coins < 4) & (rows_index >= polar_cap) & (rows_index < GRID_LAT - polar_cap)
    return wet.astype(jnp.int32)


def draw_wavenumbers(key, part):
    return window_numbers(key)


def level_of(key, shape, cuts, smallest, high):
    def one(dim, parts):
        draws = jax.random.uniform(jax.random.fold_in(jax.random.fold_in(key, 6), dim), (parts,), jnp.float32, smallest / len(cuts), high / len(cuts))
        return jnp.repeat(jnp.exp(draws), shape[dim] // parts).reshape((-1,) + (1,) * (len(shape) - dim - 1))

    level = one(*cuts[0])
    for cut in cuts[1:]:
        level = level * one(*cut)
    return level


def centred(stream_key, dims, width, limit, cuts=(), kind=jnp.bfloat16):
    drawn = width * jax.random.normal(stream_key, dims, jnp.float32)
    if cuts:
        drawn = drawn * level_of(stream_key, dims, cuts, -0.22, 0.18)
    return jnp.clip(drawn, -limit, limit).astype(kind)


def setup_inputs(seed: int = 0) -> dict:
    key_list = jax.random.split(jax.random.key(seed), 8)
    return {
        "elevation": draw_elevation(jax.random.fold_in(key_list[7], 71), 0),
        "velocity": centred(key_list[1], (MEMBERS, 2, GRID_LAT, GRID_LON), 0.5, 3.0, ((2, 16), (3, 2)), jnp.float32),
        "wind_forcing": centred(key_list[2], (2, GRID_LAT, GRID_LON), 0.1, 0.6, ((1, 16), (2, 2)), jnp.float32),
        "ocean_depth": jnp.clip(jnp.exp(math.log(1.0) - 1.609438 * jax.random.uniform(key_list[3], (GRID_LAT, GRID_LON), jnp.float32) ** level_of(key_list[3], (GRID_LAT, GRID_LON), ((0, 16), (1, 2)), -0.2, 0.2)), 0.2, 1.0),
        "wet_mask": draw_wet_mask(jax.random.fold_in(key_list[7], 71), 0),
        "love_factor": jnp.clip(jnp.exp(jax.random.uniform(key_list[5], (DEGREES,), jnp.float32, math.log(0.3), math.log(3.0))), 0.3, 3.0),
        "wavenumbers": draw_wavenumbers(jax.random.fold_in(key_list[7], 71), 0),
    }


friction_rate = 0.1
step_ratio = 0.05
highest = lax.Precision.HIGHEST

def colatitude(rows_index):
    return jnp.pi * (rows_index.astype(jnp.float32) + 0.5) / GRID_LAT

def legendre(orders, cosine, sine_row, length):
    real_type = cosine.dtype
    order_real = orders.astype(real_type)
    ladder = jnp.arange(2, length + 1).astype(real_type)
    summands = jnp.where(ladder[None, :] <= order_real, jnp.log((2.0 * ladder + 1.0) / (2.0 * ladder))[None, :], 0.0)
    log_start = 0.5 * (jnp.where(order_real > 0.0, jnp.log(3.0), 0.0) + lax.optimization_barrier(jnp.sum(summands, axis=1, keepdims=True))) + order_real * jnp.log(sine_row)
    current = jnp.ones(log_start.shape, real_type)
    previous = jnp.zeros(log_start.shape, real_type)

    def recur(carried, degree):
        current, previous, log_scale = carried
        degree_real = degree.astype(real_type)
        active = degree_real > order_real
        raising = jnp.sqrt(jnp.maximum(4.0 * degree_real * degree_real - 1.0, 0.0) / jnp.maximum(degree_real * degree_real - order_real * order_real, 1.0))
        lower_degree = degree_real - 1.0
        lowering = jnp.sqrt(jnp.maximum(lower_degree * lower_degree - order_real * order_real, 0.0) / jnp.maximum(4.0 * lower_degree * lower_degree - 1.0, 1.0))
        latest = raising * (cosine * current - lowering * previous)
        current_next = jnp.where(active, latest, current)
        previous_next = jnp.where(active, current, previous)
        result = jnp.where(degree_real >= order_real, current_next * jnp.exp(log_scale), 0.0)
        magnitude = jnp.abs(current_next) + jnp.abs(previous_next)
        return ((current_next / magnitude, previous_next / magnitude, log_scale + jnp.log(magnitude)), result)
    _, values = lax.scan(recur, (current, previous, log_start), jnp.arange(length, dtype=jnp.int32), unroll=8)
    return values

def fourier_tables(waves, columns):
    phase = waves[None, :] * columns[:, None] % GRID_LON
    angle = 2.0 * jnp.pi / GRID_LON * phase.astype(jnp.float32)
    cosines = jnp.cos(angle)
    sines = jnp.sin(angle)
    forward = jnp.stack([cosines, sines], axis=-1).reshape(columns.shape[0], 2 * waves.shape[0]) / GRID_LON
    inverse = jnp.stack([cosines.T, sines.T], axis=1).reshape(2 * waves.shape[0], columns.shape[0])
    return (forward, inverse)

def loading_field(elevation, wet_float, love_factor, wavenumbers):
    members = elevation.shape[0]
    wave_total = wavenumbers.shape[0]
    forward, inverse = fourier_tables(wavenumbers, jnp.arange(GRID_LON, dtype=jnp.int32))
    load_mass = wet_float[None] * elevation
    fourier = jnp.dot(load_mass.reshape(members * GRID_LAT, GRID_LON), forward, precision=highest).reshape(members, GRID_LAT, 2 * wave_total)
    polar_angle = colatitude(jnp.arange(GRID_LAT, dtype=jnp.int32))
    cosine = jnp.cos(polar_angle)
    sine_row = jnp.sin(polar_angle)
    weights = jnp.pi * sine_row / (2.0 * GRID_LAT)
    love_weight = love_factor / (2.0 * jnp.arange(DEGREES).astype(jnp.float32) + 1.0)

    def one_wave(position):
        orders = lax.dynamic_slice_in_dim(wavenumbers, position, 1).reshape(1, 1)
        tables = legendre(orders, cosine[None, :], sine_row[None, :], DEGREES)[:, 0, :]
        wave_slab = lax.dynamic_slice_in_dim(fourier, 2 * position, 2, axis=2) * weights[None, :, None]
        coeffs = jnp.einsum('lr,erc->ecl', tables, wave_slab, precision=highest)
        return jnp.einsum('lr,ecl->erc', tables, coeffs * love_weight, precision=highest)
    spectral = lax.map(one_wave, jnp.arange(wave_total, dtype=jnp.int32))
    spectral = jnp.transpose(spectral, (1, 2, 0, 3)).reshape(members * GRID_LAT, 2 * wave_total)
    return jnp.dot(spectral, inverse, precision=highest).reshape(members, GRID_LAT, GRID_LON)

def advance(elevation, velocity, wind_push, inverse_depth, ocean_depth, wet_float, loading):
    surface = elevation - loading
    sine_row = jnp.sin(colatitude(jnp.arange(GRID_LAT, dtype=jnp.int32)))
    zonal_step = (step_ratio / sine_row)[:, None]
    meridional = 0.1 * GRID_LAT / GRID_LON
    eastward = velocity[:, 0]
    southward = velocity[:, 1]
    zonal_change = jnp.roll(surface, -1, axis=2) - jnp.roll(surface, 1, axis=2)
    padded = jnp.pad(surface, ((0, 0), (1, 1), (0, 0)))
    merid_change = padded[:, 2:] - padded[:, :-2]
    damping = 1.0 + friction_rate * jnp.sqrt(eastward * eastward + southward * southward) * inverse_depth
    east_next = wet_float * (eastward + wind_push[0] - zonal_step * zonal_change) / damping
    south_next = wet_float * (southward + wind_push[1] - meridional * merid_change) / damping
    east_flux = ocean_depth * east_next
    south_flux = sine_row[:, None] * ocean_depth * south_next
    padded_flux = jnp.pad(south_flux, ((0, 0), (1, 1), (0, 0)))
    tendency = zonal_step * (jnp.roll(east_flux, -1, axis=2) - jnp.roll(east_flux, 1, axis=2)) + (meridional / sine_row)[:, None] * (padded_flux[:, 2:] - padded_flux[:, :-2])
    elevation_next = elevation - wet_float * tendency
    return (elevation_next, jnp.stack([east_next, south_next], axis=1))

def reference(elevation, velocity, wind_forcing, ocean_depth, wet_mask, love_factor, wavenumbers):
    wet_float = wet_mask.astype(jnp.float32)
    wind_push = wind_forcing / ocean_depth[None]
    inverse_depth = 1.0 / ocean_depth
    elevation_now = elevation
    velocity_now = velocity
    loading = jnp.zeros_like(elevation)
    for _ in range(TIME_STEPS):
        loading = loading_field(elevation_now, wet_float, love_factor, wavenumbers)
        elevation_now, velocity_now = advance(elevation_now, velocity_now, wind_push, inverse_depth, ocean_depth, wet_float, loading)
    return (elevation_now, velocity_now, loading)
```

```python
import math

import jax
import jax.numpy as jnp
from jax import lax
from jax.experimental import pallas as pl
from jax.experimental.pallas import tpu as pltpu
from jax.sharding import PartitionSpec as P

GRID_LAT = 3072
GRID_LON = 8640
DEGREES = 1081
LANES = 128

f32 = jnp.float32
bf16 = jnp.bfloat16
SMEM = pl.BlockSpec(memory_space=pltpu.SMEM)
VMEM = pl.BlockSpec(memory_space=pltpu.VMEM)
ANY = pl.BlockSpec(memory_space=pl.ANY)
HBM = pl.BlockSpec(memory_space=pltpu.HBM)
NT = (((1,), (1,)), ((), ()))
TN = (((0,), (0,)), ((), ()))


def round_up(value, step):
    return -(-value // step) * step


def sine_series(angle, orders=(13, 11, 9, 7, 5, 3, 1)):
    square = angle * angle
    series = None
    for order in orders:
        factor = (-1.0 if (order // 2) % 2 else 1.0) / math.factorial(order)
        series = jnp.full(angle.shape, factor, f32) if series is None else series * square + factor
    return angle * series


def cosine_of_units(units):
    turns = jnp.floor(units * (1.0 / GRID_LON) + 0.5)
    sine = sine_series((units - turns * GRID_LON) * (math.pi / GRID_LON))
    return 1.0 - 2.0 * sine * sine


def colatitude(row):
    return jnp.pi * (row.astype(f32) + 0.5) / GRID_LAT


def sine_of(angle):
    return sine_series(angle, (15, 13, 11, 9, 7, 5, 3, 1))


def split(value):
    high = value.astype(bf16)
    return high, (value - high.astype(f32)).astype(bf16)


def edge_kernel(rows, cols, width, lat, lon, waves, lane_rows):
    tail = cols % LANES or LANES

    def body(band_ref, sector_ref, waves_ref, elev, vel, wind, depth, wet,
             send, top, bottom, side, table, elev_v, wet_v, load_hi, load_lo,
             top_v, bottom_v, left_v, right_v, sems):
        band = band_ref[0]
        sector = sector_ref[0]
        first = pltpu.make_async_copy(elev.at[0], elev_v, sems.at[0])
        second = pltpu.make_async_copy(wet, wet_v, sems.at[1])
        first.start()
        second.start()
        fields = (vel.at[0, 0], vel.at[0, 1], wind.at[1], depth)
        copies = []
        for n, field in enumerate(fields):
            copies.append(pltpu.make_async_copy(field.at[pl.ds(0, 1), :], top_v.at[n], sems.at[2 + n]))
            copies.append(pltpu.make_async_copy(field.at[pl.ds(rows - 1, 1), :], bottom_v.at[n], sems.at[6 + n]))
        fields = (vel.at[0, 0], vel.at[0, 1], wind.at[0], depth)
        for n, field in enumerate(fields):
            copies.append(pltpu.make_async_copy(field.at[:, pl.ds(0, LANES)], left_v.at[n], sems.at[10 + n]))
            copies.append(pltpu.make_async_copy(
                field.at[:, pl.ds(cols - tail, tail)], right_v.at[n], sems.at[14 + n]))
        for copy in copies:
            copy.start()

        wave_row = lax.broadcasted_iota(jnp.int32, (2 * waves, LANES), 0)
        order = jnp.zeros((2 * waves, LANES), f32)
        for n in range(waves):
            order = jnp.where(wave_row // 2 == n, waves_ref[n].astype(f32), order)
        quarter = jnp.where(wave_row % 2 == 1, 0.25 * GRID_LON, 0.0)
        lane = lax.broadcasted_iota(jnp.int32, (2 * waves, LANES), 1)
        for tile in range(width // LANES):
            column = (sector * cols + (tile - 1) * LANES + lane).astype(f32)
            values = cosine_of_units(order * column - quarter)
            high, low = split(values)
            span = slice(tile * LANES, (tile + 1) * LANES)
            table[0 : 2 * waves, span] = high
            table[2 * waves : 4 * waves, span] = high
            table[4 * waves : 6 * waves, span] = low

        first.wait()
        second.wait()
        for start in range(0, rows, 8):
            here = slice(start, start + 8)
            high, low = split(elev_v[here, :] * wet_v[here, :].astype(f32))
            load_hi[here, :] = high
            load_lo[here, :] = low
        own = slice(LANES, LANES + cols)
        main_part = lax.dot_general(
            load_hi[...], table[2 * waves : 6 * waves, own], NT, preferred_element_type=f32)
        rest = lax.dot_general(load_lo[...], table[0 : 2 * waves, own], NT, preferred_element_type=f32)
        sums = (main_part[:, 0 : 2 * waves] + main_part[:, 2 * waves : 4 * waves] + rest) * (1.0 / GRID_LON)
        row = lax.broadcasted_iota(jnp.int32, (rows, lane_rows), 0)
        slot = lax.broadcasted_iota(jnp.int32, (rows, lane_rows), 1) - 2
        target = jnp.where(band < lat // 2, row, rows - 1 - row)
        pick = jnp.where(slot == target, 1.0, 0.0).astype(bf16)
        high, low = split(sums)
        lower = (sums - high.astype(f32) - low.astype(f32)).astype(bf16)
        turned = (
            lax.dot_general(high, pick, TN, preferred_element_type=f32)
            + lax.dot_general(low, pick, TN, preferred_element_type=f32)
            + lax.dot_general(lower, pick, TN, preferred_element_type=f32)
        )
        for n in range(waves):
            block = turned[2 * n : 2 * n + 2, :]
            for k in range(lon):
                send[n * lon + k, :, :] = block

        for copy in copies:
            copy.wait()
        top[0:2, :] = elev_v[0:2, :]
        bottom[0:2, :] = elev_v[rows - 2 : rows, :]
        for n in range(4):
            top[2 + n : 3 + n, :] = top_v[n]
            bottom[2 + n : 3 + n, :] = bottom_v[n]
        top[6:7, :] = wet_v[0:1, :].astype(f32)
        bottom[6:7, :] = wet_v[rows - 1 : rows, :].astype(f32)
        top[7:8, :] = jnp.zeros((1, cols), f32)
        bottom[7:8, :] = jnp.zeros((1, cols), f32)
        blank = jnp.zeros((8, LANES - tail), f32)
        for start in range(0, rows, 8):
            here = slice(start, start + 8)
            lane8 = lax.broadcasted_iota(jnp.int32, (8, LANES), 1)
            left = [elev_v[here, 0:LANES]] + [left_v[n, here, :] for n in range(4)]
            left.append(wet_v[here, 0:LANES].astype(f32))
            right = [elev_v[here, cols - tail : cols]] + [right_v[n, here, :] for n in range(4)]
            right.append(wet_v[here, cols - tail : cols].astype(f32))
            right = [jnp.concatenate([x, blank], axis=1) if tail < LANES else x for x in right]
            packed = jnp.zeros((8, LANES), f32)
            for n in range(6):
                moved = pltpu.roll(left[n], 4 * n, 1) if n else left[n]
                packed = jnp.where(lane8 // 2 == 2 * n, moved, packed)
                moved = pltpu.roll(right[n], (4 * n + 2 - (tail - 2)) % LANES, 1)
                packed = jnp.where(lane8 // 2 == 2 * n + 1, moved, packed)
            side[here, :] = packed

    return pl.pallas_call(
        body,
        out_shape=(
            jax.ShapeDtypeStruct((lat * lon, 2, lane_rows), f32),
            jax.ShapeDtypeStruct((8, cols), f32),
            jax.ShapeDtypeStruct((8, cols), f32),
            jax.ShapeDtypeStruct((rows, LANES), f32),
            jax.ShapeDtypeStruct((6 * waves, width), bf16),
        ),
        in_specs=[SMEM, SMEM, SMEM, ANY, ANY, ANY, ANY, ANY],
        out_specs=(VMEM, VMEM, VMEM, VMEM, VMEM),
        scratch_shapes=[
            pltpu.VMEM((rows, cols), f32),
            pltpu.VMEM((rows, cols), jnp.int32),
            pltpu.VMEM((rows, cols), bf16),
            pltpu.VMEM((rows, cols), bf16),
            pltpu.VMEM((4, 1, cols), f32),
            pltpu.VMEM((4, 1, cols), f32),
            pltpu.VMEM((4, rows, LANES), f32),
            pltpu.VMEM((4, rows, tail), f32),
            pltpu.SemaphoreType.DMA((18,)),
        ],
        name="edge_fourier",
    )


GROW = 2.0**40
SHRINK = 2.0**-96
SHRINK_LOG = 96.0 * math.log(2.0)


def legendre_kernel(bands, rows, lane_rows, steps):
    tile = (8, LANES)
    spots = [(r, t) for r in range(0, bands, 8) for t in range(0, lane_rows, LANES)]
    pairs = 8
    parts = 4
    share = steps // parts

    def body(band_ref, sector_ref, waves_ref, values_out, coef_a, coef_s, coef_t, values, sems):
        order = waves_ref[band_ref[0]]
        parity = sector_ref[0] % 2
        order_real = order.astype(f32)
        count = coef_a.shape[0]
        for start in range(0, count, 8):
            index = (lax.broadcasted_iota(jnp.int32, tile, 0) + start).astype(f32)
            index = jnp.maximum(index, 1.0)
            double = 2.0 * (index + order_real)
            above = index + 2.0 * order_real
            below = double - 1.0
            raising = jnp.sqrt(below * (double + 1.0) / (index * above))
            ratio = raising / below
            coef_a[start : start + 8, :] = raising
            coef_s[start : start + 8, :] = ratio * above
            coef_t[start : start + 8, :] = ratio * (index - 1.0)
        ladder_rows = round_up(DEGREES, 8 * LANES) // LANES
        ladder = (
            lax.broadcasted_iota(jnp.int32, (ladder_rows, LANES), 0) * LANES
            + lax.broadcasted_iota(jnp.int32, (ladder_rows, LANES), 1)
        ).astype(f32)
        used = (ladder >= 2.0) & (ladder <= order_real)
        safe = jnp.maximum(ladder, 1.0)
        total = jnp.sum(jnp.where(used, jnp.log((2.0 * safe + 1.0) / (2.0 * safe)), 0.0))
        total = 0.5 * (total + jnp.where(order > 0, math.log(3.0), 0.0))

        gap, level, now, slope = [], [], [], []
        for r, t in spots:
            row = (
                (lax.broadcasted_iota(jnp.int32, tile, 0) + r) * rows
                + lax.broadcasted_iota(jnp.int32, tile, 1) + (t - 2)
            )
            angle = colatitude(jnp.clip(row, 0, GRID_LAT // 2 + 1))
            half = sine_series(0.5 * angle)
            cosine = 1.0 - 2.0 * half * half
            gap.append(1.0 - cosine)
            log_start = total + order_real * jnp.log(sine_of(angle))
            rung = jnp.minimum(jnp.ceil((log_start - math.log(GROW)) / SHRINK_LOG), 0.0)
            level.append(rung)
            now.append(jnp.exp(log_start - rung * SHRINK_LOG))
            slope.append(jnp.zeros(tile, f32))

        def scale_of(level):
            return jnp.where(level == 0.0, 1.0, jnp.where(level == -1.0, SHRINK, 0.0))

        def advance(k, now, slope):
            a = jnp.broadcast_to(coef_a[pl.ds(k, 1), :], tile)
            s = jnp.broadcast_to(coef_s[pl.ds(k, 1), :], tile)
            t = jnp.broadcast_to(coef_t[pl.ds(k, 1), :], tile)
            drop = [a * h for h in gap]
            kept = [t * y for y in slope]
            slope = [y - c * x for x, y, c in zip(now, kept, drop)]
            return [(s - c) * x + y for x, y, c in zip(now, kept, drop)], slope

        odd = parity == 1
        next_now, next_slope = advance(1, now, slope)
        now = [jnp.where(odd, y, x) for x, y in zip(now, next_now)]
        slope = [jnp.where(odd, y, x) for x, y in zip(slope, next_slope)]

        def block(n, carry):
            now, slope, level = carry
            scale = [scale_of(x) for x in level]
            for q in range(pairs):
                j = n * pairs + q
                for (r, t), x, y in zip(spots, now, scale):
                    values[pl.ds(j, 1), r : r + 8, t : t + LANES] = (x * y)[None]
                k = 2 * j + parity + 1
                now, slope = advance(k, now, slope)
                now, slope = advance(k + 1, now, slope)
            large = [(jnp.maximum(jnp.abs(x), jnp.abs(y)) > GROW) & (z < 0.0)
                     for x, y, z in zip(now, slope, level)]
            factor = [jnp.where(x, SHRINK, 1.0) for x in large]
            level = [jnp.where(x, z + 1.0, z) for x, z in zip(large, level)]
            return [x * y for x, y in zip(now, factor)], [x * y for x, y in zip(slope, factor)], level

        state = (now, slope, level)
        copies = []
        for k in range(parts):
            state = lax.fori_loop(k * share // pairs, (k + 1) * share // pairs, block, state)
            here = pl.ds(k * share, share)
            copies.append(pltpu.make_async_copy(values.at[here], values_out.at[here], sems.at[k]))
            copies[k].start()
        for copy in copies:
            copy.wait()

    coefs = pltpu.VMEM((2 * steps + 8, LANES), f32)
    return pl.pallas_call(
        body,
        out_shape=pltpu.HBM((steps, bands, lane_rows), f32),
        in_specs=[SMEM, SMEM, SMEM],
        out_specs=HBM,
        scratch_shapes=[coefs, coefs, coefs, pltpu.VMEM((steps, bands, lane_rows), f32),
                        pltpu.SemaphoreType.DMA((parts,))],
        compiler_params=pltpu.CompilerParams(vmem_limit_bytes=16 << 20),
        cost_estimate=pl.CostEstimate(flops=12 * steps * bands * lane_rows, transcendentals=0,
                                      bytes_accessed=4 * steps * bands * lane_rows),
        name="legendre_values",
    )


def synthesis_kernel(bands, rows, lane_rows, steps, lat, lon):
    parts = 4
    share = steps // parts

    def body(band_ref, sector_ref, waves_ref, love, got, values_in, send, mass, totals, values, sems):
        copies = []
        for k in range(parts):
            here = pl.ds(k * share, share)
            copies.append(pltpu.make_async_copy(values_in.at[here], values.at[here], sems.at[k]))
            copies[k].start()
        order = waves_ref[band_ref[0]]
        parity = sector_ref[0] % 2
        sign = jnp.where(parity == 1, -1.0, 1.0)
        slot = lax.broadcasted_iota(jnp.int32, (1, lane_rows), 1)
        inside = (slot >= 2) & (slot < rows + 2)
        for b in range(bands):
            north = got[b * lon]
            south = got[(lat - 1 - b) * lon]
            for k in range(1, lon):
                north = north + got[b * lon + k]
                south = south + got[(lat - 1 - b) * lon + k]
            row = b * rows + slot - 2
            sine = sine_of(colatitude(jnp.clip(row, 0, GRID_LAT // 2 + 1)))
            weight = (jnp.pi / (2.0 * GRID_LAT)) * sine
            both = jnp.where(inside, (north + sign * south) * weight, 0.0)
            mass[0, b : b + 1, :] = both[0:1]
            mass[1, b : b + 1, :] = both[1:2]
        sub = lax.broadcasted_iota(jnp.int32, (8, LANES), 0)
        tiles = [(r, t) for r in range(0, bands, 8) for t in range(0, lane_rows, LANES)]

        def fold(parts, shift):
            half = len(parts) // 2
            lower = sub % (2 * shift) < shift
            out = []
            for x, y in zip(parts[:half], parts[half:]):
                out.append(jnp.where(lower, y + pltpu.roll(y, 8 - shift, 0), x + pltpu.roll(x, shift, 0)))
            return out

        def analyse(n, carry):
            for c in range(2):
                parts = []
                for q in (7, 6, 5, 4, 3, 2, 1, 0):
                    acc = None
                    for r, t in tiles:
                        term = mass[c, r : r + 8, t : t + LANES] * values[n * 8 + q, r : r + 8, t : t + LANES]
                        acc = term if acc is None else acc + term
                    parts.append(acc)
                for shift in (4, 2, 1):
                    parts = fold(parts, shift)
                totals[c, pl.ds(n * 8, 8), :] = parts[0]
            return carry

        for k in range(parts):
            copies[k].wait()
            lax.fori_loop(k * share // 8, (k + 1) * share // 8, analyse, 0)
        degree = order + parity + 2 * lax.broadcasted_iota(jnp.int32, (steps, LANES), 0)
        weight = jnp.where(degree < DEGREES, 1.0 / (2.0 * degree.astype(f32) + 1.0), 0.0)
        for c in range(2):
            totals[c] = jnp.sum(totals[c], axis=1, keepdims=True) * weight

        def synthesise(n, carry):
            carry = list(carry)
            for q in range(8):
                j = n * 8 + q
                weight = love[jnp.minimum(order + parity + 2 * j, DEGREES - 1)]
                factors = [jnp.broadcast_to(totals[c, pl.ds(j, 1), :], (8, LANES)) * weight for c in range(2)]
                for i, (r, t) in enumerate(tiles):
                    value = values[j, r : r + 8, t : t + LANES]
                    for c in range(2):
                        carry[2 * i + c] = carry[2 * i + c] + factors[c] * value
            return tuple(carry)

        zero = jnp.zeros((8, LANES), f32)
        found = lax.fori_loop(0, steps // 8, synthesise, (zero,) * (2 * len(tiles)))
        for b in range(bands):
            for t in range(0, lane_rows, LANES):
                i = tiles.index((b // 8 * 8, t))
                for c in range(2):
                    line = found[2 * i + c][b % 8 : b % 8 + 1, :]
                    for k in range(lon):
                        send[b * lon + k, c : c + 1, t : t + LANES] = line
                        send[(lat - 1 - b) * lon + k, c : c + 1, t : t + LANES] = line

    return pl.pallas_call(
        body,
        out_shape=jax.ShapeDtypeStruct((lat * lon, 2, lane_rows), f32),
        in_specs=[SMEM, SMEM, SMEM, SMEM, VMEM, HBM],
        out_specs=VMEM,
        scratch_shapes=[
            pltpu.VMEM((2, bands, lane_rows), f32),
            pltpu.VMEM((2, steps, LANES), f32),
            pltpu.VMEM((steps, bands, lane_rows), f32),
            pltpu.SemaphoreType.DMA((parts,)),
        ],
        compiler_params=pltpu.CompilerParams(vmem_limit_bytes=16 << 20),
        name="degree_sums",
    )


def step_kernel(rows, cols, width, lat, waves, lane_rows):
    tail = cols % LANES or LANES
    tiles = -(-cols // LANES)
    tall = rows + 32
    top = 16
    own = slice(LANES, LANES + cols)
    meridional = 0.1 * GRID_LAT / GRID_LON
    pieces = 6 if rows % 96 == 0 else 1
    piece = rows // pieces
    names = 6

    def body(band_ref, sector_ref, got, table, low, high, low_side, high_side,
             elev, vel, wind, depth, wet, elev_out, vel_out, load_out,
             elev_v, u_v, v_v, wx_v, wy_v, depth_v, wet_v, surf, flux, load_v,
             left_v, right_v, zonal, sine_v, merid, sems, out_sems):
        band = band_ref[0]
        fields = (
            (elev.at[0], elev_v), (depth, depth_v), (wet, wet_v), (vel.at[0, 0], u_v),
            (vel.at[0, 1], v_v), (wind.at[1], wy_v), (wind.at[0], wx_v),
        )
        copies = []
        for k in range(pieces):
            inside = pl.ds(top + k * piece, piece)
            outside = pl.ds(k * piece, piece)
            copies.append([pltpu.make_async_copy(
                source.at[outside, :], buffer.at[inside, :], sems.at[k, n])
                for n, (source, buffer) in enumerate(fields)])
            for copy in copies[k]:
                copy.start()

        row = lax.broadcasted_iota(jnp.int32, (tall, LANES), 0) - top + band * rows
        row = jnp.clip(row, 0, GRID_LAT - 1)
        sine = sine_of(colatitude(jnp.minimum(row, GRID_LAT - 1 - row)))
        sine_v[...] = sine
        zonal[...] = 0.05 / sine
        merid[...] = meridional / sine

        sign = jnp.where(band < lat // 2, 1.0, -1.0)
        mixed = (got[:, 0] + sign * got[:, 1]).reshape(2 * waves, lane_rows)
        first, second = split(mixed)
        stacked = jnp.concatenate([first, second, first], axis=0)
        line = lax.broadcasted_iota(jnp.int32, (rows + 8, lane_rows), 0)
        line = jnp.where(line < rows, line, jnp.where(line < rows + 2, line - rows - 2, line - 2))
        slot = lax.broadcasted_iota(jnp.int32, (rows + 8, lane_rows), 1)
        target = jnp.where(band < lat // 2, line + 2, rows + 1 - line)
        pick = jnp.where(slot == target, 1.0, 0.0).astype(bf16)
        factors = lax.dot_general(pick, stacked, NT, preferred_element_type=f32).astype(bf16)

        here = slice(top, top + rows)
        for n in range(names):
            left_v[n, here, :] = pltpu.roll(low_side[...], (124 - 4 * n) % LANES, 1)
            right_v[n, here, :] = pltpu.roll(high_side[...], (tail - 4 * n) % LANES, 1)

        elev_v[top - 2 : top, :] = low[0:2, :]
        elev_v[top + rows : top + rows + 2, :] = high[0:2, :]
        for n, buffer in enumerate((u_v, v_v, wy_v, depth_v, wet_v)):
            buffer[top - 1 : top, :] = low[2 + n : 3 + n, :].astype(buffer.dtype)
            buffer[top + rows : top + rows + 1, :] = high[2 + n : 3 + n, :].astype(buffer.dtype)

        group = 4
        after = slice(top + rows, top + rows + 2)
        for t in range(0, width // LANES, group):
            begin = t * LANES
            end = min((t + group) * LANES, width)
            loading = lax.dot_general(
                factors, table[:, begin:end], (((1,), (0,)), ((), ())), preferred_element_type=f32)
            surf[here, begin:end] = loading[0:rows]
            first_lane = max(begin, LANES)
            last_lane = min(end, LANES + cols)
            inner = slice(first_lane - LANES, last_lane - LANES)
            outer = slice(first_lane, last_lane)
            cut = slice(first_lane - begin, last_lane - begin)
            load_v[:, inner] = loading[0:rows, cut]
            surf[top - 2 : top, outer] = elev_v[top - 2 : top, inner] - loading[rows : rows + 2, cut]
            surf[after, outer] = elev_v[after, inner] - loading[rows + 2 : rows + 4, cut]
        load_copy = pltpu.make_async_copy(load_v, load_out.at[0], out_sems.at[0])
        load_copy.start()

        lane8 = lax.broadcasted_iota(jnp.int32, (8, LANES), 1)
        sub8 = lax.broadcasted_iota(jnp.int32, (8, LANES), 0)
        count = width // LANES

        def part(t):
            return slice(t * LANES, (t + 1) * LANES)

        def fetch(t, rows8, n, buffer):
            if t == 0:
                return left_v[n, rows8, :]
            if t <= cols // LANES:
                return buffer[rows8, part(t - 1)].astype(f32)
            if tail == LANES:
                return right_v[n, rows8, :]
            return jnp.concatenate(
                [buffer[rows8, cols - tail : cols].astype(f32), right_v[n, rows8, tail:LANES]], axis=1)

        def keep(buffer, rows8, t, value):
            if 0 < t <= cols // LANES:
                buffer[rows8, part(t - 1)] = value
            elif t and tail < LANES:
                buffer[rows8, cols - tail : cols] = value[:, 0:tail]

        def surfaces(n, carry):
            rows8 = pl.ds(pl.multiple_of(n * 8, 8), 8)
            for t in range(count):
                surf[rows8, part(t)] = fetch(t, rows8, 0, elev_v) - surf[rows8, part(t)]
            return carry

        def vertical(ref, base, at, centre):
            before = jnp.where(sub8 == 7, ref[pl.ds(base - 8, 8), at], centre)
            after = jnp.where(sub8 == 0, ref[pl.ds(base + 8, 8), at], centre)
            return pltpu.roll(after, 7, 0) - pltpu.roll(before, 1, 0)

        def across(behind, centre, ahead):
            ahead = jnp.where(lane8 == 0, ahead, centre)
            behind = jnp.where(lane8 == LANES - 1, behind, centre)
            return pltpu.roll(ahead, LANES - 1, 1) - pltpu.roll(behind, 1, 1)

        def speeds(n):
            base = pl.multiple_of(n * 8, 8)
            rows8 = pl.ds(base, 8)
            zs = zonal[rows8, :]
            sn = sine_v[rows8, :]
            level = [surf[rows8, part(0)], surf[rows8, part(0)]]
            flow = []
            wet_before = None
            for t in range(count + 1):
                if t < count:
                    at = part(t)
                    level.append(surf[rows8, part(t + 1)] if t + 1 < count else level[-1])
                    level.pop(0) if len(level) > 3 else None
                    u = fetch(t, rows8, 1, u_v)
                    v = fetch(t, rows8, 2, v_v)
                    d = fetch(t, rows8, 4, depth_v)
                    wet = fetch(t, rows8, 5, wet_v)
                    drag = wet / (d + 0.1 * jnp.sqrt(u * u + v * v))
                    new_u = drag * (u * d + fetch(t, rows8, 3, wx_v) - (zs * d) * across(*level))
                    keep(wx_v, rows8, t, new_u)
                    flow.append(d * new_u)
                    if t and not (t > cols // LANES and tail == LANES):
                        if t <= cols // LANES:
                            push = wy_v[rows8, part(t - 1)]
                        else:
                            push = jnp.concatenate(
                                [wy_v[rows8, cols - tail : cols], jnp.zeros((8, LANES - tail), f32)], axis=1)
                        new_v = drag * (v * d + push - (meridional * d) * vertical(surf, base, at, level[1]))
                        keep(wy_v, rows8, t, new_v)
                        flux[rows8, at] = sn * d * new_v
                else:
                    flow.append(flow[-1])
                if len(flow) > 3:
                    flow.pop(0)
                back = t - 1
                if len(flow) == 3 and 0 < back <= tiles:
                    change = wet_before * (zs * across(*flow))
                    if back <= cols // LANES:
                        elev_v[rows8, part(back - 1)] = elev_v[rows8, part(back - 1)] - change
                    else:
                        elev_v[rows8, cols - tail : cols] = elev_v[rows8, cols - tail : cols] - change[:, 0:tail]
                wet_before = wet

        def levels(n):
            base = pl.multiple_of(n * 8, 8)
            rows8 = pl.ds(base, 8)
            ms = merid[rows8, :]
            for t in range(1, tiles + 1):
                change = ms * vertical(flux, base, part(t), flux[rows8, part(t)])
                if t <= cols // LANES:
                    at = part(t - 1)
                else:
                    at = slice(cols - tail, cols)
                    change = change[:, 0:tail]
                elev_v[rows8, at] = elev_v[rows8, at] - wet_v[rows8, at].astype(f32) * change

        def out_copies(k):
            inside = pl.ds(top + k * piece, piece)
            outside = pl.ds(k * piece, piece)
            return (
                pltpu.make_async_copy(wx_v.at[inside, :], vel_out.at[0, 0, outside, :], out_sems.at[1 + k]),
                pltpu.make_async_copy(wy_v.at[inside, :], vel_out.at[0, 1, outside, :], out_sems.at[1 + pieces + k]),
                pltpu.make_async_copy(elev_v.at[inside, :], elev_out.at[0, outside, :], out_sems.at[1 + 2 * pieces + k]),
            )

        def both(n, carry):
            speeds(n + 1)
            levels(n)
            return carry

        def ahead_rows(n, carry):
            speeds(n)
            return carry

        per = piece // 8
        begin = top // 8
        done = begin
        for k in range(pieces):
            for copy in copies[k]:
                copy.wait()
            lax.fori_loop(begin + k * per, begin + (k + 1) * per, surfaces, 0)
            if k == 0:
                lax.fori_loop(begin - 1, begin + 1, ahead_rows, 0)
            stop = begin + (k + 1) * per - (2 if k + 1 < pieces else 0)
            lax.fori_loop(done, stop, both, 0)
            done = stop
            if k:
                for copy in out_copies(k - 1):
                    copy.start()
        for copy in out_copies(pieces - 1):
            copy.start()
        for k in range(pieces):
            for copy in out_copies(k):
                copy.wait()
        load_copy.wait()

    flat = pltpu.VMEM((tall, cols), f32)
    big = pltpu.VMEM((tall, width), f32)
    thin = pltpu.VMEM((tall, LANES), f32)
    return pl.pallas_call(
        body,
        out_shape=(
            jax.ShapeDtypeStruct((1, rows, cols), f32),
            jax.ShapeDtypeStruct((1, 2, rows, cols), f32),
            jax.ShapeDtypeStruct((1, rows, cols), f32),
        ),
        in_specs=[SMEM, SMEM, VMEM, VMEM, VMEM, VMEM, VMEM, VMEM, ANY, ANY, ANY, ANY, ANY],
        out_specs=(ANY, ANY, ANY),
        scratch_shapes=[
            flat, flat, flat, flat, flat, flat, pltpu.VMEM((tall, cols), jnp.int32), big, big,
            pltpu.VMEM((rows, cols), f32),
            pltpu.VMEM((names, tall, LANES), f32),
            pltpu.VMEM((names, tall, LANES), f32),
            thin, thin, thin,
            pltpu.SemaphoreType.DMA((pieces, 7)),
            pltpu.SemaphoreType.DMA((1 + 3 * pieces,)),
        ],
        compiler_params=pltpu.CompilerParams(vmem_limit_bytes=52 << 20),
        name="surge_step",
    )


def local(elevation, velocity, wind_forcing, ocean_depth, wet_mask, love_factor, wavenumbers):
    members, rows, cols = elevation.shape
    lat = lax.axis_size("lat")
    lon = lax.axis_size("lon")
    waves = wavenumbers.shape[0]
    assert members == 1 and waves == lat and lat % 16 == 0 and lon % 2 == 0
    bands = lat // 2
    lane_rows = round_up(rows + 4, LANES)
    width = LANES + round_up(cols + 2, LANES)
    steps = round_up((DEGREES + 1) // 2, 8)
    place = (
        lax.axis_index("lat").astype(jnp.int32)[None],
        lax.axis_index("lon").astype(jnp.int32)[None],
    )

    send, top, bottom, side, table = edge_kernel(rows, cols, width, lat, lon, waves, lane_rows)(
        *place, wavenumbers, elevation, velocity, wind_forcing, ocean_depth, wet_mask)
    got = lax.all_to_all(send, ("lat", "lon"), split_axis=0, concat_axis=0, tiled=True)
    values = legendre_kernel(bands, rows, lane_rows, steps)(*place, wavenumbers)
    values, bottom, top, side = lax.optimization_barrier((values, bottom, top, side))
    up = [(i, (i + 1) % lat) for i in range(lat)]
    down = [(i, (i - 1) % lat) for i in range(lat)]
    low = lax.ppermute(bottom, "lat", up)
    high = lax.ppermute(top, "lat", down)
    low_side = lax.ppermute(side, "lon", [(i, (i + 1) % lon) for i in range(lon)])
    high_side = low_side if lon == 2 else lax.ppermute(
        side, "lon", [(i, (i - 1) % lon) for i in range(lon)])
    send = synthesis_kernel(bands, rows, lane_rows, steps, lat, lon)(
        *place, wavenumbers, love_factor, got, pltpu.with_memory_space_constraint(values, pltpu.HBM))
    got = lax.all_to_all(send, ("lat", "lon"), split_axis=0, concat_axis=0, tiled=True)
    got = got.reshape(lat, lon, 2, lane_rows)[:, :2]
    return step_kernel(rows, cols, width, lat, waves, lane_rows)(
        *place, got, table, low, high, low_side, high_side,
        elevation, velocity, wind_forcing, ocean_depth, wet_mask)


def solution(mesh):
    return jax.shard_map(
        local,
        mesh=mesh,
        in_specs=(
            P(None, "lat", "lon"),
            P(None, None, "lat", "lon"),
            P(None, "lat", "lon"),
            P("lat", "lon"),
            P("lat", "lon"),
            P(),
            P(),
        ),
        out_specs=(P(None, "lat", "lon"), P(None, None, "lat", "lon"), P(None, "lat", "lon")),
        check_vma=False,
    )
```

```python
import math

import jax
import jax.numpy as jnp
from jax import lax
from jax.experimental import pallas as pl
from jax.experimental.pallas import tpu as pltpu
from jax.sharding import PartitionSpec as P


GRID_LAT = 3072
GRID_LON = 8640
DEGREES = 1081
LANES = 128

f32 = jnp.float32
bf16 = jnp.bfloat16
SMEM = pl.BlockSpec(memory_space=pltpu.SMEM)
VMEM = pl.BlockSpec(memory_space=pltpu.VMEM)
ANY = pl.BlockSpec(memory_space=pl.ANY)
HBM = pl.BlockSpec(memory_space=pltpu.HBM)
NT = (((1,), (1,)), ((), ()))
TN = (((0,), (0,)), ((), ()))


def round_up(value, step):
    return -(-value // step) * step


def sine_series(angle, orders=(13, 11, 9, 7, 5, 3, 1)):
    square = angle * angle
    series = None
    for order in orders:
        factor = (-1.0 if (order // 2) % 2 else 1.0) / math.factorial(order)
        series = jnp.full(angle.shape, factor, f32) if series is None else series * square + factor
    return angle * series


def cosine_of_units(units):
    turns = jnp.floor(units * (1.0 / GRID_LON) + 0.5)
    sine = sine_series((units - turns * GRID_LON) * (math.pi / GRID_LON))
    return 1.0 - 2.0 * sine * sine


def colatitude(row):
    return jnp.pi * (row.astype(f32) + 0.5) / GRID_LAT


def sine_of(angle):
    return sine_series(angle, (15, 13, 11, 9, 7, 5, 3, 1))


def split(value):
    high = value.astype(bf16)
    return high, (value - high.astype(f32)).astype(bf16)


def edge_kernel(rows, cols, width, lat, lon, waves, lane_rows):
    tail = cols % LANES or LANES

    def body(band_ref, sector_ref, waves_ref, elev, vel, wind, depth, wet,
             send, top, bottom, side, table, elev_v, wet_v, load_hi, load_lo,
             top_v, bottom_v, left_v, right_v, sems):
        band = band_ref[0]
        sector = sector_ref[0]
        first = pltpu.make_async_copy(elev.at[0], elev_v, sems.at[0])
        second = pltpu.make_async_copy(wet, wet_v, sems.at[1])
        first.start()
        second.start()
        fields = (vel.at[0, 0], vel.at[0, 1], wind.at[1], depth)
        copies = []
        for n, field in enumerate(fields):
            copies.append(pltpu.make_async_copy(field.at[pl.ds(0, 1), :], top_v.at[n], sems.at[2 + n]))
            copies.append(pltpu.make_async_copy(field.at[pl.ds(rows - 1, 1), :], bottom_v.at[n], sems.at[6 + n]))
        fields = (vel.at[0, 0], vel.at[0, 1], wind.at[0], depth)
        for n, field in enumerate(fields):
            copies.append(pltpu.make_async_copy(field.at[:, pl.ds(0, LANES)], left_v.at[n], sems.at[10 + n]))
            copies.append(pltpu.make_async_copy(
                field.at[:, pl.ds(cols - tail, tail)], right_v.at[n], sems.at[14 + n]))
        for copy in copies:
            copy.start()

        wave_row = lax.broadcasted_iota(jnp.int32, (2 * waves, LANES), 0)
        order = jnp.zeros((2 * waves, LANES), f32)
        for n in range(waves):
            order = jnp.where(wave_row // 2 == n, waves_ref[n].astype(f32), order)
        quarter = jnp.where(wave_row % 2 == 1, 0.25 * GRID_LON, 0.0)
        lane = lax.broadcasted_iota(jnp.int32, (2 * waves, LANES), 1)
        for tile in range(width // LANES):
            column = (sector * cols + (tile - 1) * LANES + lane).astype(f32)
            values = cosine_of_units(order * column - quarter)
            high, low = split(values)
            span = slice(tile * LANES, (tile + 1) * LANES)
            table[0 : 2 * waves, span] = high
            table[2 * waves : 4 * waves, span] = high
            table[4 * waves : 6 * waves, span] = low

        first.wait()
        second.wait()
        for start in range(0, rows, 8):
            here = slice(start, start + 8)
            high, low = split(elev_v[here, :] * wet_v[here, :].astype(f32))
            load_hi[here, :] = high
            load_lo[here, :] = low
        own = slice(LANES, LANES + cols)
        main_part = lax.dot_general(
            load_hi[...], table[2 * waves : 6 * waves, own], NT, preferred_element_type=f32)
        rest = lax.dot_general(load_lo[...], table[0 : 2 * waves, own], NT, preferred_element_type=f32)
        sums = (main_part[:, 0 : 2 * waves] + main_part[:, 2 * waves : 4 * waves] + rest) * (1.0 / GRID_LON)
        row = lax.broadcasted_iota(jnp.int32, (rows, lane_rows), 0)
        slot = lax.broadcasted_iota(jnp.int32, (rows, lane_rows), 1) - 2
        target = jnp.where(band < lat // 2, row, rows - 1 - row)
        pick = jnp.where(slot == target, 1.0, 0.0).astype(bf16)
        high, low = split(sums)
        lower = (sums - high.astype(f32) - low.astype(f32)).astype(bf16)
        turned = (
            lax.dot_general(high, pick, TN, preferred_element_type=f32)
            + lax.dot_general(low, pick, TN, preferred_element_type=f32)
            + lax.dot_general(lower, pick, TN, preferred_element_type=f32)
        )
        for n in range(waves):
            block = turned[2 * n : 2 * n + 2, :]
            for k in range(lon):
                send[n * lon + k, :, :] = block

        for copy in copies:
            copy.wait()
        top[0:2, :] = elev_v[0:2, :]
        bottom[0:2, :] = elev_v[rows - 2 : rows, :]
        for n in range(4):
            top[2 + n : 3 + n, :] = top_v[n]
            bottom[2 + n : 3 + n, :] = bottom_v[n]
        top[6:7, :] = wet_v[0:1, :].astype(f32)
        bottom[6:7, :] = wet_v[rows - 1 : rows, :].astype(f32)
        top[7:8, :] = jnp.zeros((1, cols), f32)
        bottom[7:8, :] = jnp.zeros((1, cols), f32)
        blank = jnp.zeros((8, LANES - tail), f32)
        for start in range(0, rows, 8):
            here = slice(start, start + 8)
            lane8 = lax.broadcasted_iota(jnp.int32, (8, LANES), 1)
            left = [elev_v[here, 0:LANES]] + [left_v[n, here, :] for n in range(4)]
            left.append(wet_v[here, 0:LANES].astype(f32))
            right = [elev_v[here, cols - tail : cols]] + [right_v[n, here, :] for n in range(4)]
            right.append(wet_v[here, cols - tail : cols].astype(f32))
            right = [jnp.concatenate([x, blank], axis=1) if tail < LANES else x for x in right]
            packed = jnp.zeros((8, LANES), f32)
            for n in range(6):
                moved = pltpu.roll(left[n], 4 * n, 1) if n else left[n]
                packed = jnp.where(lane8 // 2 == 2 * n, moved, packed)
                moved = pltpu.roll(right[n], (4 * n + 2 - (tail - 2)) % LANES, 1)
                packed = jnp.where(lane8 // 2 == 2 * n + 1, moved, packed)
            side[here, :] = packed

    return pl.pallas_call(
        body,
        out_shape=(
            jax.ShapeDtypeStruct((lat * lon, 2, lane_rows), f32),
            jax.ShapeDtypeStruct((8, cols), f32),
            jax.ShapeDtypeStruct((8, cols), f32),
            jax.ShapeDtypeStruct((rows, LANES), f32),
            jax.ShapeDtypeStruct((6 * waves, width), bf16),
        ),
        in_specs=[SMEM, SMEM, SMEM, ANY, ANY, ANY, ANY, ANY],
        out_specs=(VMEM, VMEM, VMEM, VMEM, VMEM),
        scratch_shapes=[
            pltpu.VMEM((rows, cols), f32),
            pltpu.VMEM((rows, cols), jnp.int32),
            pltpu.VMEM((rows, cols), bf16),
            pltpu.VMEM((rows, cols), bf16),
            pltpu.VMEM((4, 1, cols), f32),
            pltpu.VMEM((4, 1, cols), f32),
            pltpu.VMEM((4, rows, LANES), f32),
            pltpu.VMEM((4, rows, tail), f32),
            pltpu.SemaphoreType.DMA((18,)),
        ],
        name="edge_fourier",
    )


GROW = 2.0**40
SHRINK = 2.0**-96
SHRINK_LOG = 96.0 * math.log(2.0)


def legendre_kernel(bands, rows, lane_rows, steps):
    tile = (8, LANES)
    spots = [(r, t) for r in range(0, bands, 8) for t in range(0, lane_rows, LANES)]
    pairs = 8
    parts = 4
    share = steps // parts

    def body(band_ref, sector_ref, waves_ref, values_out, coef_a, coef_s, coef_t, values, sems):
        order = waves_ref[band_ref[0]]
        parity = sector_ref[0] % 2
        order_real = order.astype(f32)
        count = coef_a.shape[0]
        for start in range(0, count, 8):
            index = (lax.broadcasted_iota(jnp.int32, tile, 0) + start).astype(f32)
            index = jnp.maximum(index, 1.0)
            double = 2.0 * (index + order_real)
            above = index + 2.0 * order_real
            below = double - 1.0
            raising = jnp.sqrt(below * (double + 1.0) / (index * above))
            ratio = raising / below
            coef_a[start : start + 8, :] = raising
            coef_s[start : start + 8, :] = ratio * above
            coef_t[start : start + 8, :] = ratio * (index - 1.0)
        ladder_rows = round_up(DEGREES, 8 * LANES) // LANES
        ladder = (
            lax.broadcasted_iota(jnp.int32, (ladder_rows, LANES), 0) * LANES
            + lax.broadcasted_iota(jnp.int32, (ladder_rows, LANES), 1)
        ).astype(f32)
        used = (ladder >= 2.0) & (ladder <= order_real)
        safe = jnp.maximum(ladder, 1.0)
        total = jnp.sum(jnp.where(used, jnp.log((2.0 * safe + 1.0) / (2.0 * safe)), 0.0))
        total = 0.5 * (total + jnp.where(order > 0, math.log(3.0), 0.0))

        gap, level, now, slope = [], [], [], []
        for r, t in spots:
            row = (
                (lax.broadcasted_iota(jnp.int32, tile, 0) + r) * rows
                + lax.broadcasted_iota(jnp.int32, tile, 1) + (t - 2)
            )
            angle = colatitude(jnp.clip(row, 0, GRID_LAT // 2 + 1))
            half = sine_series(0.5 * angle)
            cosine = 1.0 - 2.0 * half * half
            gap.append(1.0 - cosine)
            log_start = total + order_real * jnp.log(sine_of(angle))
            rung = jnp.minimum(jnp.ceil((log_start - math.log(GROW)) / SHRINK_LOG), 0.0)
            level.append(rung)
            now.append(jnp.exp(log_start - rung * SHRINK_LOG))
            slope.append(jnp.zeros(tile, f32))

        def scale_of(level):
            return jnp.where(level == 0.0, 1.0, jnp.where(level == -1.0, SHRINK, 0.0))

        def advance(k, now, slope):
            a = jnp.broadcast_to(coef_a[pl.ds(k, 1), :], tile)
            s = jnp.broadcast_to(coef_s[pl.ds(k, 1), :], tile)
            t = jnp.broadcast_to(coef_t[pl.ds(k, 1), :], tile)
            drop = [a * h for h in gap]
            kept = [t * y for y in slope]
            slope = [y - c * x for x, y, c in zip(now, kept, drop)]
            return [(s - c) * x + y for x, y, c in zip(now, kept, drop)], slope

        odd = parity == 1
        next_now, next_slope = advance(1, now, slope)
        now = [jnp.where(odd, y, x) for x, y in zip(now, next_now)]
        slope = [jnp.where(odd, y, x) for x, y in zip(slope, next_slope)]

        def block(n, carry):
            now, slope, level = carry
            scale = [scale_of(x) for x in level]
            for q in range(pairs):
                j = n * pairs + q
                for (r, t), x, y in zip(spots, now, scale):
                    values[pl.ds(j, 1), r : r + 8, t : t + LANES] = (x * y)[None]
                k = 2 * j + parity + 1
                now, slope = advance(k, now, slope)
                now, slope = advance(k + 1, now, slope)
            large = [(jnp.maximum(jnp.abs(x), jnp.abs(y)) > GROW) & (z < 0.0)
                     for x, y, z in zip(now, slope, level)]
            factor = [jnp.where(x, SHRINK, 1.0) for x in large]
            level = [jnp.where(x, z + 1.0, z) for x, z in zip(large, level)]
            return [x * y for x, y in zip(now, factor)], [x * y for x, y in zip(slope, factor)], level

        state = (now, slope, level)
        copies = []
        for k in range(parts):
            state = lax.fori_loop(k * share // pairs, (k + 1) * share // pairs, block, state)
            here = pl.ds(k * share, share)
            copies.append(pltpu.make_async_copy(values.at[here], values_out.at[here], sems.at[k]))
            copies[k].start()
        for copy in copies:
            copy.wait()

    coefs = pltpu.VMEM((2 * steps + 8, LANES), f32)
    return pl.pallas_call(
        body,
        out_shape=pltpu.HBM((steps, bands, lane_rows), f32),
        in_specs=[SMEM, SMEM, SMEM],
        out_specs=HBM,
        scratch_shapes=[coefs, coefs, coefs, pltpu.VMEM((steps, bands, lane_rows), f32),
                        pltpu.SemaphoreType.DMA((parts,))],
        compiler_params=pltpu.CompilerParams(vmem_limit_bytes=16 << 20),
        cost_estimate=pl.CostEstimate(flops=12 * steps * bands * lane_rows, transcendentals=0,
                                      bytes_accessed=4 * steps * bands * lane_rows),
        name="legendre_values",
    )


def synthesis_kernel(bands, rows, lane_rows, steps, lat, lon):
    parts = 4
    share = steps // parts

    def body(band_ref, sector_ref, waves_ref, love, got, values_in, send, mass, totals, values, sems):
        copies = []
        for k in range(parts):
            here = pl.ds(k * share, share)
            copies.append(pltpu.make_async_copy(values_in.at[here], values.at[here], sems.at[k]))
            copies[k].start()
        order = waves_ref[band_ref[0]]
        parity = sector_ref[0] % 2
        sign = jnp.where(parity == 1, -1.0, 1.0)
        slot = lax.broadcasted_iota(jnp.int32, (1, lane_rows), 1)
        inside = (slot >= 2) & (slot < rows + 2)
        for b in range(bands):
            north = got[b * lon]
            south = got[(lat - 1 - b) * lon]
            for k in range(1, lon):
                north = north + got[b * lon + k]
                south = south + got[(lat - 1 - b) * lon + k]
            row = b * rows + slot - 2
            sine = sine_of(colatitude(jnp.clip(row, 0, GRID_LAT // 2 + 1)))
            weight = (jnp.pi / (2.0 * GRID_LAT)) * sine
            both = jnp.where(inside, (north + sign * south) * weight, 0.0)
            mass[0, b : b + 1, :] = both[0:1]
            mass[1, b : b + 1, :] = both[1:2]
        sub = lax.broadcasted_iota(jnp.int32, (8, LANES), 0)
        tiles = [(r, t) for r in range(0, bands, 8) for t in range(0, lane_rows, LANES)]

        def fold(parts, shift):
            half = len(parts) // 2
            lower = sub % (2 * shift) < shift
            out = []
            for x, y in zip(parts[:half], parts[half:]):
                out.append(jnp.where(lower, y + pltpu.roll(y, 8 - shift, 0), x + pltpu.roll(x, shift, 0)))
            return out

        def analyse(n, carry):
            for c in range(2):
                parts = []
                for q in (7, 6, 5, 4, 3, 2, 1, 0):
                    acc = None
                    for r, t in tiles:
                        term = mass[c, r : r + 8, t : t + LANES] * values[n * 8 + q, r : r + 8, t : t + LANES]
                        acc = term if acc is None else acc + term
                    parts.append(acc)
                for shift in (4, 2, 1):
                    parts = fold(parts, shift)
                totals[c, pl.ds(n * 8, 8), :] = parts[0]
            return carry

        for k in range(parts):
            copies[k].wait()
            lax.fori_loop(k * share // 8, (k + 1) * share // 8, analyse, 0)
        degree = order + parity + 2 * lax.broadcasted_iota(jnp.int32, (steps, LANES), 0)
        weight = jnp.where(degree < DEGREES, 1.0 / (2.0 * degree.astype(f32) + 1.0), 0.0)
        for c in range(2):
            totals[c] = jnp.sum(totals[c], axis=1, keepdims=True) * weight

        def synthesise(n, carry):
            carry = list(carry)
            for q in range(8):
                j = n * 8 + q
                weight = love[jnp.minimum(order + parity + 2 * j, DEGREES - 1)]
                factors = [jnp.broadcast_to(totals[c, pl.ds(j, 1), :], (8, LANES)) * weight for c in range(2)]
                for i, (r, t) in enumerate(tiles):
                    value = values[j, r : r + 8, t : t + LANES]
                    for c in range(2):
                        carry[2 * i + c] = carry[2 * i + c] + factors[c] * value
            return tuple(carry)

        zero = jnp.zeros((8, LANES), f32)
        found = lax.fori_loop(0, steps // 8, synthesise, (zero,) * (2 * len(tiles)))
        for b in range(bands):
            for t in range(0, lane_rows, LANES):
                i = tiles.index((b // 8 * 8, t))
                for c in range(2):
                    line = found[2 * i + c][b % 8 : b % 8 + 1, :]
                    for k in range(lon):
                        send[b * lon + k, c : c + 1, t : t + LANES] = line
                        send[(lat - 1 - b) * lon + k, c : c + 1, t : t + LANES] = line

    return pl.pallas_call(
        body,
        out_shape=jax.ShapeDtypeStruct((lat * lon, 2, lane_rows), f32),
        in_specs=[SMEM, SMEM, SMEM, SMEM, VMEM, HBM],
        out_specs=VMEM,
        scratch_shapes=[
            pltpu.VMEM((2, bands, lane_rows), f32),
            pltpu.VMEM((2, steps, LANES), f32),
            pltpu.VMEM((steps, bands, lane_rows), f32),
            pltpu.SemaphoreType.DMA((parts,)),
        ],
        compiler_params=pltpu.CompilerParams(vmem_limit_bytes=16 << 20),
        name="degree_sums",
    )


def step_kernel(rows, cols, width, lat, waves, lane_rows):
    tail = cols % LANES or LANES
    tiles = -(-cols // LANES)
    tall = rows + 32
    top = 16
    meridional = 0.1 * GRID_LAT / GRID_LON
    pieces = 6 if rows % 96 == 0 else 1
    piece = rows // pieces
    names = 6

    def body(band_ref, sector_ref, got, table, low, high, low_side, high_side,
             elev, vel, wind, depth, wet, elev_out, vel_out, load_out,
             elev_v, u_v, v_v, wx_v, wy_v, depth_v, wet_v, surf, flux, load_v,
             left_v, right_v, zonal, sine_v, merid, sems, out_sems):
        band = band_ref[0]
        fields = (
            (elev.at[0], elev_v), (depth, depth_v), (wet, wet_v), (vel.at[0, 0], u_v),
            (vel.at[0, 1], v_v), (wind.at[1], wy_v), (wind.at[0], wx_v),
        )
        copies = []
        for k in range(pieces):
            inside = pl.ds(top + k * piece, piece)
            outside = pl.ds(k * piece, piece)
            copies.append([pltpu.make_async_copy(
                source.at[outside, :], buffer.at[inside, :], sems.at[k, n])
                for n, (source, buffer) in enumerate(fields)])
            for copy in copies[k]:
                copy.start()

        row = lax.broadcasted_iota(jnp.int32, (tall, LANES), 0) - top + band * rows
        row = jnp.clip(row, 0, GRID_LAT - 1)
        sine = sine_of(colatitude(jnp.minimum(row, GRID_LAT - 1 - row)))
        sine_v[...] = sine
        zonal[...] = 0.05 / sine
        merid[...] = meridional / sine

        sign = jnp.where(band < lat // 2, 1.0, -1.0)
        mixed = (got[:, 0] + sign * got[:, 1]).reshape(2 * waves, lane_rows)
        first, second = split(mixed)
        stacked = jnp.concatenate([first, second, first], axis=0)
        line = lax.broadcasted_iota(jnp.int32, (rows + 8, lane_rows), 0)
        line = jnp.where(line < rows, line, jnp.where(line < rows + 2, line - rows - 2, line - 2))
        slot = lax.broadcasted_iota(jnp.int32, (rows + 8, lane_rows), 1)
        target = jnp.where(band < lat // 2, line + 2, rows + 1 - line)
        pick = jnp.where(slot == target, 1.0, 0.0).astype(bf16)
        factors = lax.dot_general(pick, stacked, NT, preferred_element_type=f32).astype(bf16)

        here = slice(top, top + rows)
        for n in range(names):
            left_v[n, here, :] = pltpu.roll(low_side[...], (124 - 4 * n) % LANES, 1)
            right_v[n, here, :] = pltpu.roll(high_side[...], (tail - 4 * n) % LANES, 1)

        elev_v[top - 2 : top, :] = low[0:2, :]
        elev_v[top + rows : top + rows + 2, :] = high[0:2, :]
        for n, buffer in enumerate((u_v, v_v, wy_v, depth_v, wet_v)):
            before, behind = low[2 + n : 3 + n, :], high[2 + n : 3 + n, :]
            if buffer is depth_v:
                before, behind = jnp.maximum(before, 0.2), jnp.maximum(behind, 0.2)
            buffer[top - 1 : top, :] = before.astype(buffer.dtype)
            buffer[top + rows : top + rows + 1, :] = behind.astype(buffer.dtype)

        group = 4
        after = slice(top + rows, top + rows + 2)
        for t in range(0, width // LANES, group):
            begin = t * LANES
            end = min((t + group) * LANES, width)
            loading = lax.dot_general(
                factors, table[:, begin:end], (((1,), (0,)), ((), ())), preferred_element_type=f32)
            surf[here, begin:end] = loading[0:rows]
            first_lane = max(begin, LANES)
            last_lane = min(end, LANES + cols)
            inner = slice(first_lane - LANES, last_lane - LANES)
            outer = slice(first_lane, last_lane)
            cut = slice(first_lane - begin, last_lane - begin)
            load_v[:, inner] = loading[0:rows, cut]
            surf[top - 2 : top, outer] = elev_v[top - 2 : top, inner] - loading[rows : rows + 2, cut]
            surf[after, outer] = elev_v[after, inner] - loading[rows + 2 : rows + 4, cut]
        load_copy = pltpu.make_async_copy(load_v, load_out.at[0], out_sems.at[0])
        load_copy.start()

        lane8 = lax.broadcasted_iota(jnp.int32, (8, LANES), 1)
        sub8 = lax.broadcasted_iota(jnp.int32, (8, LANES), 0)
        count = width // LANES

        def part(t):
            return slice(t * LANES, (t + 1) * LANES)

        def fetch(t, rows8, n, buffer):
            if t == 0:
                return left_v[n, rows8, :]
            if t <= cols // LANES:
                return buffer[rows8, part(t - 1)].astype(f32)
            if tail == LANES:
                return right_v[n, rows8, :]
            return jnp.concatenate(
                [buffer[rows8, cols - tail : cols].astype(f32), right_v[n, rows8, tail:LANES]], axis=1)

        def keep(buffer, rows8, t, value):
            if 0 < t <= cols // LANES:
                buffer[rows8, part(t - 1)] = value
            elif t and tail < LANES:
                buffer[rows8, cols - tail : cols] = value[:, 0:tail]

        def surfaces(n, carry):
            rows8 = pl.ds(pl.multiple_of(n * 8, 8), 8)
            for t in range(count):
                surf[rows8, part(t)] = fetch(t, rows8, 0, elev_v) - surf[rows8, part(t)]
            return carry

        def vertical(ref, base, at, centre):
            before = jnp.where(sub8 == 7, ref[pl.ds(base - 8, 8), at], centre)
            after = jnp.where(sub8 == 0, ref[pl.ds(base + 8, 8), at], centre)
            return pltpu.roll(after, 7, 0) - pltpu.roll(before, 1, 0)

        def across(behind, centre, ahead):
            ahead = jnp.where(lane8 == 0, ahead, centre)
            behind = jnp.where(lane8 == LANES - 1, behind, centre)
            return pltpu.roll(ahead, LANES - 1, 1) - pltpu.roll(behind, 1, 1)

        def speeds(n):
            base = pl.multiple_of(n * 8, 8)
            rows8 = pl.ds(base, 8)
            zs = zonal[rows8, :]
            sn = sine_v[rows8, :]
            level = [surf[rows8, part(0)], surf[rows8, part(0)]]
            flow = []
            wet_before = None
            for t in range(count + 1):
                if t < count:
                    at = part(t)
                    level.append(surf[rows8, part(t + 1)] if t + 1 < count else level[-1])
                    level.pop(0) if len(level) > 3 else None
                    u = fetch(t, rows8, 1, u_v)
                    v = fetch(t, rows8, 2, v_v)
                    d = fetch(t, rows8, 4, depth_v)
                    wet = fetch(t, rows8, 5, wet_v)
                    drag = wet / (d + 0.1 * jnp.sqrt(u * u + v * v))
                    new_u = drag * (u * d + fetch(t, rows8, 3, wx_v) - (zs * d) * across(*level))
                    keep(wx_v, rows8, t, new_u)
                    flow.append(d * new_u)
                    if t and not (t > cols // LANES and tail == LANES):
                        if t <= cols // LANES:
                            push = wy_v[rows8, part(t - 1)]
                        else:
                            push = jnp.concatenate(
                                [wy_v[rows8, cols - tail : cols], jnp.zeros((8, LANES - tail), f32)], axis=1)
                        new_v = drag * (v * d + push - (meridional * d) * vertical(surf, base, at, level[1]))
                        keep(wy_v, rows8, t, new_v)
                        flux[rows8, at] = sn * d * new_v
                else:
                    flow.append(flow[-1])
                if len(flow) > 3:
                    flow.pop(0)
                back = t - 1
                if len(flow) == 3 and 0 < back <= tiles:
                    change = wet_before * (zs * across(*flow))
                    if back <= cols // LANES:
                        elev_v[rows8, part(back - 1)] = elev_v[rows8, part(back - 1)] - change
                    else:
                        elev_v[rows8, cols - tail : cols] = elev_v[rows8, cols - tail : cols] - change[:, 0:tail]
                wet_before = wet

        def levels(n):
            base = pl.multiple_of(n * 8, 8)
            rows8 = pl.ds(base, 8)
            ms = merid[rows8, :]
            for t in range(1, tiles + 1):
                change = ms * vertical(flux, base, part(t), flux[rows8, part(t)])
                if t <= cols // LANES:
                    at = part(t - 1)
                else:
                    at = slice(cols - tail, cols)
                    change = change[:, 0:tail]
                elev_v[rows8, at] = elev_v[rows8, at] - wet_v[rows8, at].astype(f32) * change

        def out_copies(k):
            inside = pl.ds(top + k * piece, piece)
            outside = pl.ds(k * piece, piece)
            return (
                pltpu.make_async_copy(wx_v.at[inside, :], vel_out.at[0, 0, outside, :], out_sems.at[1 + k]),
                pltpu.make_async_copy(wy_v.at[inside, :], vel_out.at[0, 1, outside, :], out_sems.at[1 + pieces + k]),
                pltpu.make_async_copy(elev_v.at[inside, :], elev_out.at[0, outside, :], out_sems.at[1 + 2 * pieces + k]),
            )

        def both(n, carry):
            speeds(n + 1)
            levels(n)
            return carry

        def ahead_rows(n, carry):
            speeds(n)
            return carry

        per = piece // 8
        begin = top // 8
        done = begin
        for k in range(pieces):
            for copy in copies[k]:
                copy.wait()
            lax.fori_loop(begin + k * per, begin + (k + 1) * per, surfaces, 0)
            if k == 0:
                lax.fori_loop(begin - 1, begin + 1, ahead_rows, 0)
            stop = begin + (k + 1) * per - (2 if k + 1 < pieces else 0)
            lax.fori_loop(done, stop, both, 0)
            done = stop
            if k:
                for copy in out_copies(k - 1):
                    copy.start()
        for copy in out_copies(pieces - 1):
            copy.start()
        for k in range(pieces):
            for copy in out_copies(k):
                copy.wait()
        load_copy.wait()

    flat = pltpu.VMEM((tall, cols), f32)
    big = pltpu.VMEM((tall, width), f32)
    thin = pltpu.VMEM((tall, LANES), f32)
    return pl.pallas_call(
        body,
        out_shape=(
            jax.ShapeDtypeStruct((1, rows, cols), f32),
            jax.ShapeDtypeStruct((1, 2, rows, cols), f32),
            jax.ShapeDtypeStruct((1, rows, cols), f32),
        ),
        in_specs=[SMEM, SMEM, VMEM, VMEM, VMEM, VMEM, VMEM, VMEM, ANY, ANY, ANY, ANY, ANY],
        out_specs=(ANY, ANY, ANY),
        scratch_shapes=[
            flat, flat, flat, flat, flat, flat, pltpu.VMEM((tall, cols), jnp.int32), big, big,
            pltpu.VMEM((rows, cols), f32),
            pltpu.VMEM((names, tall, LANES), f32),
            pltpu.VMEM((names, tall, LANES), f32),
            thin, thin, thin,
            pltpu.SemaphoreType.DMA((pieces, 7)),
            pltpu.SemaphoreType.DMA((1 + 3 * pieces,)),
        ],
        compiler_params=pltpu.CompilerParams(vmem_limit_bytes=52 << 20),
        name="surge_step",
    )


def local(elevation, velocity, wind_forcing, ocean_depth, wet_mask, love_factor, wavenumbers):
    members, rows, cols = elevation.shape
    lat = lax.axis_size("lat")
    lon = lax.axis_size("lon")
    waves = wavenumbers.shape[0]
    assert members == 1 and waves == lat and lat % 16 == 0 and lon % 2 == 0
    bands = lat // 2
    lane_rows = round_up(rows + 4, LANES)
    width = LANES + round_up(cols + 2, LANES)
    steps = round_up((DEGREES + 1) // 2, 8)
    place = (
        lax.axis_index("lat").astype(jnp.int32)[None],
        lax.axis_index("lon").astype(jnp.int32)[None],
    )

    send, top, bottom, side, table = edge_kernel(rows, cols, width, lat, lon, waves, lane_rows)(
        *place, wavenumbers, elevation, velocity, wind_forcing, ocean_depth, wet_mask)
    got = lax.all_to_all(send, ("lat", "lon"), split_axis=0, concat_axis=0, tiled=True)
    values = legendre_kernel(bands, rows, lane_rows, steps)(*place, wavenumbers)
    send = synthesis_kernel(bands, rows, lane_rows, steps, lat, lon)(
        *place, wavenumbers, love_factor, got, pltpu.with_memory_space_constraint(values, pltpu.HBM))
    send, bottom, top, side = lax.optimization_barrier((send, bottom, top, side))
    up = [(i, i + 1) for i in range(lat - 1)]
    down = [(i + 1, i) for i in range(lat - 1)]
    got = lax.all_to_all(send, ("lat", "lon"), split_axis=0, concat_axis=0, tiled=True)
    low = lax.ppermute(bottom, "lat", up)
    high = lax.ppermute(top, "lat", down)
    low_side = lax.ppermute(side, "lon", [(i, (i + 1) % lon) for i in range(lon)])
    high_side = low_side if lon == 2 else lax.ppermute(
        side, "lon", [(i, (i - 1) % lon) for i in range(lon)])
    got = got.reshape(lat, lon, 2, lane_rows)[:, :2]
    return step_kernel(rows, cols, width, lat, waves, lane_rows)(
        *place, got, table, low, high, low_side, high_side,
        elevation, velocity, wind_forcing, ocean_depth, wet_mask)


def solution(mesh):
    return jax.shard_map(
        local,
        mesh=mesh,
        in_specs=(
            P(None, "lat", "lon"),
            P(None, None, "lat", "lon"),
            P(None, "lat", "lon"),
            P("lat", "lon"),
            P("lat", "lon"),
            P(),
            P(),
        ),
        out_specs=(P(None, "lat", "lon"), P(None, None, "lat", "lon"), P(None, "lat", "lon")),
        check_vma=False,
    )
```

```python
import math

import jax
import jax.numpy as jnp
from jax import lax
from jax.experimental import pallas as pl
from jax.experimental.pallas import tpu as pltpu
from jax.sharding import PartitionSpec as P

GRID_LAT = 3072
GRID_LON = 8640
DEGREES = 1081
LANES = 128

f32 = jnp.float32
bf16 = jnp.bfloat16
SMEM = pl.BlockSpec(memory_space=pltpu.SMEM)
VMEM = pl.BlockSpec(memory_space=pltpu.VMEM)
ANY = pl.BlockSpec(memory_space=pl.ANY)
HBM = pl.BlockSpec(memory_space=pltpu.HBM)
NT = (((1,), (1,)), ((), ()))
TN = (((0,), (0,)), ((), ()))


def round_up(value, step):
    return -(-value // step) * step


def sine_series(angle, orders=(13, 11, 9, 7, 5, 3, 1)):
    square = angle * angle
    series = None
    for order in orders:
        factor = (-1.0 if (order // 2) % 2 else 1.0) / math.factorial(order)
        series = jnp.full(angle.shape, factor, f32) if series is None else series * square + factor
    return angle * series


def cosine_of_units(units):
    turns = jnp.floor(units * (1.0 / GRID_LON) + 0.5)
    sine = sine_series((units - turns * GRID_LON) * (math.pi / GRID_LON))
    return 1.0 - 2.0 * sine * sine


def colatitude(row):
    return jnp.pi * (row.astype(f32) + 0.5) / GRID_LAT


def sine_of(angle):
    return sine_series(angle, (15, 13, 11, 9, 7, 5, 3, 1))


def split(value):
    high = value.astype(bf16)
    return high, (value - high.astype(f32)).astype(bf16)


def edge_kernel(rows, cols, width, lat, lon, waves, lane_rows):
    tail = cols % LANES or LANES

    def body(band_ref, sector_ref, waves_ref, elev, vel, wind, depth, wet,
             send, top, bottom, side, table, elev_v, wet_v, load_hi, load_lo,
             top_v, bottom_v, left_v, right_v, sems):
        band = band_ref[0]
        sector = sector_ref[0]
        first = pltpu.make_async_copy(elev.at[0], elev_v, sems.at[0])
        second = pltpu.make_async_copy(wet, wet_v, sems.at[1])
        first.start()
        second.start()
        fields = (vel.at[0, 0], vel.at[0, 1], wind.at[1], depth)
        copies = []
        for n, field in enumerate(fields):
            copies.append(pltpu.make_async_copy(field.at[pl.ds(0, 1), :], top_v.at[n], sems.at[2 + n]))
            copies.append(pltpu.make_async_copy(field.at[pl.ds(rows - 1, 1), :], bottom_v.at[n], sems.at[6 + n]))
        fields = (vel.at[0, 0], vel.at[0, 1], wind.at[0], depth)
        for n, field in enumerate(fields):
            copies.append(pltpu.make_async_copy(field.at[:, pl.ds(0, LANES)], left_v.at[n], sems.at[10 + n]))
            copies.append(pltpu.make_async_copy(
                field.at[:, pl.ds(cols - tail, tail)], right_v.at[n], sems.at[14 + n]))
        for copy in copies:
            copy.start()

        wave_row = lax.broadcasted_iota(jnp.int32, (2 * waves, LANES), 0)
        order = jnp.zeros((2 * waves, LANES), f32)
        for n in range(waves):
            order = jnp.where(wave_row // 2 == n, waves_ref[n].astype(f32), order)
        quarter = jnp.where(wave_row % 2 == 1, 0.25 * GRID_LON, 0.0)
        lane = lax.broadcasted_iota(jnp.int32, (2 * waves, LANES), 1)
        for tile in range(width // LANES):
            column = (sector * cols + (tile - 1) * LANES + lane).astype(f32)
            values = cosine_of_units(order * column - quarter)
            high, low = split(values)
            span = slice(tile * LANES, (tile + 1) * LANES)
            table[0 : 2 * waves, span] = high
            table[2 * waves : 4 * waves, span] = high
            table[4 * waves : 6 * waves, span] = low

        first.wait()
        second.wait()
        for start in range(0, rows, 8):
            here = slice(start, start + 8)
            high, low = split(elev_v[here, :] * wet_v[here, :].astype(f32))
            load_hi[here, :] = high
            load_lo[here, :] = low
        own = slice(LANES, LANES + cols)
        main_part = lax.dot_general(
            load_hi[...], table[2 * waves : 6 * waves, own], NT, preferred_element_type=f32)
        rest = lax.dot_general(load_lo[...], table[0 : 2 * waves, own], NT, preferred_element_type=f32)
        sums = (main_part[:, 0 : 2 * waves] + main_part[:, 2 * waves : 4 * waves] + rest) * (1.0 / GRID_LON)
        row = lax.broadcasted_iota(jnp.int32, (rows, lane_rows), 0)
        slot = lax.broadcasted_iota(jnp.int32, (rows, lane_rows), 1) - 2
        target = jnp.where(band < lat // 2, row, rows - 1 - row)
        pick = jnp.where(slot == target, 1.0, 0.0).astype(bf16)
        high, low = split(sums)
        lower = (sums - high.astype(f32) - low.astype(f32)).astype(bf16)
        turned = (
            lax.dot_general(high, pick, TN, preferred_element_type=f32)
            + lax.dot_general(low, pick, TN, preferred_element_type=f32)
            + lax.dot_general(lower, pick, TN, preferred_element_type=f32)
        )
        for n in range(waves):
            block = turned[2 * n : 2 * n + 2, :]
            for k in range(lon):
                send[n * lon + k, :, :] = block

        for copy in copies:
            copy.wait()
        top[0:2, :] = elev_v[0:2, :]
        bottom[0:2, :] = elev_v[rows - 2 : rows, :]
        for n in range(4):
            top[2 + n : 3 + n, :] = top_v[n]
            bottom[2 + n : 3 + n, :] = bottom_v[n]
        top[6:7, :] = wet_v[0:1, :].astype(f32)
        bottom[6:7, :] = wet_v[rows - 1 : rows, :].astype(f32)
        top[7:8, :] = jnp.zeros((1, cols), f32)
        bottom[7:8, :] = jnp.zeros((1, cols), f32)
        blank = jnp.zeros((8, LANES - tail), f32)
        for start in range(0, rows, 8):
            here = slice(start, start + 8)
            lane8 = lax.broadcasted_iota(jnp.int32, (8, LANES), 1)
            left = [elev_v[here, 0:LANES]] + [left_v[n, here, :] for n in range(4)]
            left.append(wet_v[here, 0:LANES].astype(f32))
            right = [elev_v[here, cols - tail : cols]] + [right_v[n, here, :] for n in range(4)]
            right.append(wet_v[here, cols - tail : cols].astype(f32))
            right = [jnp.concatenate([x, blank], axis=1) if tail < LANES else x for x in right]
            packed = jnp.zeros((8, LANES), f32)
            for n in range(6):
                moved = pltpu.roll(left[n], 4 * n, 1) if n else left[n]
                packed = jnp.where(lane8 // 2 == 2 * n, moved, packed)
                moved = pltpu.roll(right[n], (4 * n + 2 - (tail - 2)) % LANES, 1)
                packed = jnp.where(lane8 // 2 == 2 * n + 1, moved, packed)
            side[here, :] = packed

    return pl.pallas_call(
        body,
        out_shape=(
            jax.ShapeDtypeStruct((lat * lon, 2, lane_rows), f32),
            jax.ShapeDtypeStruct((8, cols), f32),
            jax.ShapeDtypeStruct((8, cols), f32),
            jax.ShapeDtypeStruct((rows, LANES), f32),
            jax.ShapeDtypeStruct((6 * waves, width), bf16),
        ),
        in_specs=[SMEM, SMEM, SMEM, ANY, ANY, ANY, ANY, ANY],
        out_specs=(VMEM, VMEM, VMEM, VMEM, VMEM),
        scratch_shapes=[
            pltpu.VMEM((rows, cols), f32),
            pltpu.VMEM((rows, cols), jnp.int32),
            pltpu.VMEM((rows, cols), bf16),
            pltpu.VMEM((rows, cols), bf16),
            pltpu.VMEM((4, 1, cols), f32),
            pltpu.VMEM((4, 1, cols), f32),
            pltpu.VMEM((4, rows, LANES), f32),
            pltpu.VMEM((4, rows, tail), f32),
            pltpu.SemaphoreType.DMA((18,)),
        ],
        name="edge_fourier",
    )


GROW = 2.0**40
SHRINK = 2.0**-96
SHRINK_LOG = 96.0 * math.log(2.0)


def legendre_kernel(bands, rows, lane_rows, steps):
    tile = (8, LANES)
    spots = [(r, t) for r in range(0, bands, 8) for t in range(0, lane_rows, LANES)]
    pairs = 8
    parts = 4
    share = steps // parts

    def body(band_ref, sector_ref, waves_ref, values_out, coef_a, coef_s, coef_t, values, sems):
        order = waves_ref[band_ref[0]]
        parity = sector_ref[0] % 2
        order_real = order.astype(f32)
        count = coef_a.shape[0]
        for start in range(0, count, 8):
            index = (lax.broadcasted_iota(jnp.int32, tile, 0) + start).astype(f32)
            index = jnp.maximum(index, 1.0)
            double = 2.0 * (index + order_real)
            above = index + 2.0 * order_real
            below = double - 1.0
            raising = jnp.sqrt(below * (double + 1.0) / (index * above))
            ratio = raising / below
            coef_a[start : start + 8, :] = raising
            coef_s[start : start + 8, :] = ratio * above
            coef_t[start : start + 8, :] = ratio * (index - 1.0)
        ladder_rows = round_up(DEGREES, 8 * LANES) // LANES
        ladder = (
            lax.broadcasted_iota(jnp.int32, (ladder_rows, LANES), 0) * LANES
            + lax.broadcasted_iota(jnp.int32, (ladder_rows, LANES), 1)
        ).astype(f32)
        used = (ladder >= 2.0) & (ladder <= order_real)
        safe = jnp.maximum(ladder, 1.0)
        total = jnp.sum(jnp.where(used, jnp.log((2.0 * safe + 1.0) / (2.0 * safe)), 0.0))
        total = 0.5 * (total + jnp.where(order > 0, math.log(3.0), 0.0))

        gap, level, now, slope = [], [], [], []
        for r, t in spots:
            row = (
                (lax.broadcasted_iota(jnp.int32, tile, 0) + r) * rows
                + lax.broadcasted_iota(jnp.int32, tile, 1) + (t - 2)
            )
            angle = colatitude(jnp.clip(row, 0, GRID_LAT // 2 + 1))
            half = sine_series(0.5 * angle)
            cosine = 1.0 - 2.0 * half * half
            gap.append(1.0 - cosine)
            log_start = total + order_real * jnp.log(sine_of(angle))
            rung = jnp.minimum(jnp.ceil((log_start - math.log(GROW)) / SHRINK_LOG), 0.0)
            level.append(rung)
            now.append(jnp.exp(log_start - rung * SHRINK_LOG))
            slope.append(jnp.zeros(tile, f32))

        def scale_of(level):
            return jnp.where(level == 0.0, 1.0, jnp.where(level == -1.0, SHRINK, 0.0))

        def advance(k, now, slope):
            a = jnp.broadcast_to(coef_a[pl.ds(k, 1), :], tile)
            s = jnp.broadcast_to(coef_s[pl.ds(k, 1), :], tile)
            t = jnp.broadcast_to(coef_t[pl.ds(k, 1), :], tile)
            drop = [a * h for h in gap]
            kept = [t * y for y in slope]
            slope = [y - c * x for x, y, c in zip(now, kept, drop)]
            return [(s - c) * x + y for x, y, c in zip(now, kept, drop)], slope

        odd = parity == 1
        next_now, next_slope = advance(1, now, slope)
        now = [jnp.where(odd, y, x) for x, y in zip(now, next_now)]
        slope = [jnp.where(odd, y, x) for x, y in zip(slope, next_slope)]

        def block(n, carry):
            now, slope, level = carry
            scale = [scale_of(x) for x in level]
            for q in range(pairs):
                j = n * pairs + q
                for (r, t), x, y in zip(spots, now, scale):
                    values[pl.ds(j, 1), r : r + 8, t : t + LANES] = (x * y)[None]
                k = 2 * j + parity + 1
                now, slope = advance(k, now, slope)
                now, slope = advance(k + 1, now, slope)
            large = [(jnp.maximum(jnp.abs(x), jnp.abs(y)) > GROW) & (z < 0.0)
                     for x, y, z in zip(now, slope, level)]
            factor = [jnp.where(x, SHRINK, 1.0) for x in large]
            level = [jnp.where(x, z + 1.0, z) for x, z in zip(large, level)]
            return [x * y for x, y in zip(now, factor)], [x * y for x, y in zip(slope, factor)], level

        state = (now, slope, level)
        copies = []
        for k in range(parts):
            state = lax.fori_loop(k * share // pairs, (k + 1) * share // pairs, block, state)
            here = pl.ds(k * share, share)
            copies.append(pltpu.make_async_copy(values.at[here], values_out.at[here], sems.at[k]))
            copies[k].start()
        for copy in copies:
            copy.wait()

    coefs = pltpu.VMEM((2 * steps + 8, LANES), f32)
    return pl.pallas_call(
        body,
        out_shape=pltpu.HBM((steps, bands, lane_rows), f32),
        in_specs=[SMEM, SMEM, SMEM],
        out_specs=HBM,
        scratch_shapes=[coefs, coefs, coefs, pltpu.VMEM((steps, bands, lane_rows), f32),
                        pltpu.SemaphoreType.DMA((parts,))],
        compiler_params=pltpu.CompilerParams(vmem_limit_bytes=16 << 20),
        cost_estimate=pl.CostEstimate(flops=12 * steps * bands * lane_rows, transcendentals=0,
                                      bytes_accessed=4 * steps * bands * lane_rows),
        name="legendre_values",
    )


def synthesis_kernel(bands, rows, lane_rows, steps, lat, lon):
    parts = 4
    share = steps // parts

    def body(band_ref, sector_ref, waves_ref, love, got, values_in, send, mass, totals, values, sems):
        copies = []
        for k in range(parts):
            here = pl.ds(k * share, share)
            copies.append(pltpu.make_async_copy(values_in.at[here], values.at[here], sems.at[k]))
            copies[k].start()
        order = waves_ref[band_ref[0]]
        parity = sector_ref[0] % 2
        sign = jnp.where(parity == 1, -1.0, 1.0)
        slot = lax.broadcasted_iota(jnp.int32, (1, lane_rows), 1)
        inside = (slot >= 2) & (slot < rows + 2)
        for b in range(bands):
            north = got[b * lon]
            south = got[(lat - 1 - b) * lon]
            for k in range(1, lon):
                north = north + got[b * lon + k]
                south = south + got[(lat - 1 - b) * lon + k]
            row = b * rows + slot - 2
            sine = sine_of(colatitude(jnp.clip(row, 0, GRID_LAT // 2 + 1)))
            weight = (jnp.pi / (2.0 * GRID_LAT)) * sine
            both = jnp.where(inside, (north + sign * south) * weight, 0.0)
            mass[0, b : b + 1, :] = both[0:1]
            mass[1, b : b + 1, :] = both[1:2]
        sub = lax.broadcasted_iota(jnp.int32, (8, LANES), 0)
        tiles = [(r, t) for r in range(0, bands, 8) for t in range(0, lane_rows, LANES)]

        def fold(parts, shift):
            half = len(parts) // 2
            lower = sub % (2 * shift) < shift
            out = []
            for x, y in zip(parts[:half], parts[half:]):
                out.append(jnp.where(lower, y + pltpu.roll(y, 8 - shift, 0), x + pltpu.roll(x, shift, 0)))
            return out

        def analyse(n, carry):
            for c in range(2):
                parts = []
                for q in (7, 6, 5, 4, 3, 2, 1, 0):
                    acc = None
                    for r, t in tiles:
                        term = mass[c, r : r + 8, t : t + LANES] * values[n * 8 + q, r : r + 8, t : t + LANES]
                        acc = term if acc is None else acc + term
                    parts.append(acc)
                for shift in (4, 2, 1):
                    parts = fold(parts, shift)
                totals[c, pl.ds(n * 8, 8), :] = parts[0]
            return carry

        for k in range(parts):
            copies[k].wait()
            lax.fori_loop(k * share // 8, (k + 1) * share // 8, analyse, 0)
        degree = order + parity + 2 * lax.broadcasted_iota(jnp.int32, (steps, LANES), 0)
        weight = jnp.where(degree < DEGREES, 1.0 / (2.0 * degree.astype(f32) + 1.0), 0.0)
        for c in range(2):
            totals[c] = jnp.sum(totals[c], axis=1, keepdims=True) * weight

        def synthesise(n, carry):
            carry = list(carry)
            for q in range(8):
                j = n * 8 + q
                weight = love[jnp.minimum(order + parity + 2 * j, DEGREES - 1)]
                factors = [jnp.broadcast_to(totals[c, pl.ds(j, 1), :], (8, LANES)) * weight for c in range(2)]
                for i, (r, t) in enumerate(tiles):
                    value = values[j, r : r + 8, t : t + LANES]
                    for c in range(2):
                        carry[2 * i + c] = carry[2 * i + c] + factors[c] * value
            return tuple(carry)

        zero = jnp.zeros((8, LANES), f32)
        found = lax.fori_loop(0, steps // 8, synthesise, (zero,) * (2 * len(tiles)))
        for b in range(bands):
            for t in range(0, lane_rows, LANES):
                i = tiles.index((b // 8 * 8, t))
                for c in range(2):
                    line = found[2 * i + c][b % 8 : b % 8 + 1, :]
                    for k in range(lon):
                        send[b * lon + k, c : c + 1, t : t + LANES] = line
                        send[(lat - 1 - b) * lon + k, c : c + 1, t : t + LANES] = line

    return pl.pallas_call(
        body,
        out_shape=jax.ShapeDtypeStruct((lat * lon, 2, lane_rows), f32),
        in_specs=[SMEM, SMEM, SMEM, SMEM, VMEM, HBM],
        out_specs=VMEM,
        scratch_shapes=[
            pltpu.VMEM((2, bands, lane_rows), f32),
            pltpu.VMEM((2, steps, LANES), f32),
            pltpu.VMEM((steps, bands, lane_rows), f32),
            pltpu.SemaphoreType.DMA((parts,)),
        ],
        compiler_params=pltpu.CompilerParams(vmem_limit_bytes=16 << 20),
        name="degree_sums",
    )


def step_kernel(rows, cols, width, lat, waves, lane_rows):
    tail = cols % LANES or LANES
    tiles = -(-cols // LANES)
    tall = rows + 32
    top = 16
    own = slice(LANES, LANES + cols)
    meridional = 0.1 * GRID_LAT / GRID_LON
    pieces = 6 if rows % 96 == 0 else 1
    piece = rows // pieces
    names = 6

    def body(band_ref, sector_ref, got, table, low, high, low_side, high_side,
             elev, vel, wind, depth, wet, elev_out, vel_out, load_out,
             elev_v, u_v, v_v, wx_v, wy_v, depth_v, wet_v, surf, flux, load_v,
             left_v, right_v, zonal, sine_v, merid, sems, out_sems):
        band = band_ref[0]
        fields = (
            (elev.at[0], elev_v), (depth, depth_v), (wet, wet_v), (vel.at[0, 0], u_v),
            (vel.at[0, 1], v_v), (wind.at[1], wy_v), (wind.at[0], wx_v),
        )
        copies = []
        for k in range(pieces):
            inside = pl.ds(top + k * piece, piece)
            outside = pl.ds(k * piece, piece)
            copies.append([pltpu.make_async_copy(
                source.at[outside, :], buffer.at[inside, :], sems.at[k, n])
                for n, (source, buffer) in enumerate(fields)])
            for copy in copies[k]:
                copy.start()

        row = lax.broadcasted_iota(jnp.int32, (tall, LANES), 0) - top + band * rows
        row = jnp.clip(row, 0, GRID_LAT - 1)
        sine = sine_of(colatitude(jnp.minimum(row, GRID_LAT - 1 - row)))
        sine_v[...] = sine
        zonal[...] = 0.05 / sine
        merid[...] = meridional / sine

        sign = jnp.where(band < lat // 2, 1.0, -1.0)
        mixed = (got[:, 0] + sign * got[:, 1]).reshape(2 * waves, lane_rows)
        first, second = split(mixed)
        stacked = jnp.concatenate([first, second, first], axis=0)
        line = lax.broadcasted_iota(jnp.int32, (rows + 8, lane_rows), 0)
        line = jnp.where(line < rows, line, jnp.where(line < rows + 2, line - rows - 2, line - 2))
        slot = lax.broadcasted_iota(jnp.int32, (rows + 8, lane_rows), 1)
        target = jnp.where(band < lat // 2, line + 2, rows + 1 - line)
        pick = jnp.where(slot == target, 1.0, 0.0).astype(bf16)
        factors = lax.dot_general(pick, stacked, NT, preferred_element_type=f32).astype(bf16)

        here = slice(top, top + rows)
        for n in range(names):
            left_v[n, here, :] = pltpu.roll(low_side[...], (124 - 4 * n) % LANES, 1)
            right_v[n, here, :] = pltpu.roll(high_side[...], (tail - 4 * n) % LANES, 1)

        elev_v[top - 2 : top, :] = low[0:2, :]
        elev_v[top + rows : top + rows + 2, :] = high[0:2, :]
        for n, buffer in enumerate((u_v, v_v, wy_v, depth_v, wet_v)):
            before, behind = low[2 + n : 3 + n, :], high[2 + n : 3 + n, :]
            if buffer is depth_v:
                before, behind = jnp.maximum(before, 0.2), jnp.maximum(behind, 0.2)
            buffer[top - 1 : top, :] = before.astype(buffer.dtype)
            buffer[top + rows : top + rows + 1, :] = behind.astype(buffer.dtype)

        group = 4
        after = slice(top + rows, top + rows + 2)
        for t in range(0, width // LANES, group):
            begin = t * LANES
            end = min((t + group) * LANES, width)
            loading = lax.dot_general(
                factors, table[:, begin:end], (((1,), (0,)), ((), ())), preferred_element_type=f32)
            surf[here, begin:end] = loading[0:rows]
            first_lane = max(begin, LANES)
            last_lane = min(end, LANES + cols)
            inner = slice(first_lane - LANES, last_lane - LANES)
            outer = slice(first_lane, last_lane)
            cut = slice(first_lane - begin, last_lane - begin)
            load_v[:, inner] = loading[0:rows, cut]
            surf[top - 2 : top, outer] = elev_v[top - 2 : top, inner] - loading[rows : rows + 2, cut]
            surf[after, outer] = elev_v[after, inner] - loading[rows + 2 : rows + 4, cut]
        load_copy = pltpu.make_async_copy(load_v, load_out.at[0], out_sems.at[0])
        load_copy.start()

        lane8 = lax.broadcasted_iota(jnp.int32, (8, LANES), 1)
        sub8 = lax.broadcasted_iota(jnp.int32, (8, LANES), 0)
        count = width // LANES

        def part(t):
            return slice(t * LANES, (t + 1) * LANES)

        def fetch(t, rows8, n, buffer):
            if t == 0:
                return left_v[n, rows8, :]
            if t <= cols // LANES:
                return buffer[rows8, part(t - 1)].astype(f32)
            if tail == LANES:
                return right_v[n, rows8, :]
            return jnp.concatenate(
                [buffer[rows8, cols - tail : cols].astype(f32), right_v[n, rows8, tail:LANES]], axis=1)

        def keep(buffer, rows8, t, value):
            if 0 < t <= cols // LANES:
                buffer[rows8, part(t - 1)] = value
            elif t and tail < LANES:
                buffer[rows8, cols - tail : cols] = value[:, 0:tail]

        def surfaces(n, carry):
            rows8 = pl.ds(pl.multiple_of(n * 8, 8), 8)
            for t in range(count):
                surf[rows8, part(t)] = fetch(t, rows8, 0, elev_v) - surf[rows8, part(t)]
            return carry

        def vertical(ref, base, at, centre):
            before = jnp.where(sub8 == 7, ref[pl.ds(base - 8, 8), at], centre)
            after = jnp.where(sub8 == 0, ref[pl.ds(base + 8, 8), at], centre)
            return pltpu.roll(after, 7, 0) - pltpu.roll(before, 1, 0)

        def across(behind, centre, ahead):
            ahead = jnp.where(lane8 == 0, ahead, centre)
            behind = jnp.where(lane8 == LANES - 1, behind, centre)
            return pltpu.roll(ahead, LANES - 1, 1) - pltpu.roll(behind, 1, 1)

        def speeds(n):
            base = pl.multiple_of(n * 8, 8)
            rows8 = pl.ds(base, 8)
            zs = zonal[rows8, :]
            sn = sine_v[rows8, :]
            level = [surf[rows8, part(0)], surf[rows8, part(0)]]
            flow = []
            wet_before = None
            for t in range(count + 1):
                if t < count:
                    at = part(t)
                    level.append(surf[rows8, part(t + 1)] if t + 1 < count else level[-1])
                    level.pop(0) if len(level) > 3 else None
                    u = fetch(t, rows8, 1, u_v)
                    v = fetch(t, rows8, 2, v_v)
                    d = fetch(t, rows8, 4, depth_v)
                    wet = fetch(t, rows8, 5, wet_v)
                    drag = wet / (d + 0.1 * jnp.sqrt(u * u + v * v))
                    new_u = drag * (u * d + fetch(t, rows8, 3, wx_v) - (zs * d) * across(*level))
                    keep(wx_v, rows8, t, new_u)
                    flow.append(d * new_u)
                    if t and not (t > cols // LANES and tail == LANES):
                        if t <= cols // LANES:
                            push = wy_v[rows8, part(t - 1)]
                        else:
                            push = jnp.concatenate(
                                [wy_v[rows8, cols - tail : cols], jnp.zeros((8, LANES - tail), f32)], axis=1)
                        new_v = drag * (v * d + push - (meridional * d) * vertical(surf, base, at, level[1]))
                        keep(wy_v, rows8, t, new_v)
                        flux[rows8, at] = sn * d * new_v
                else:
                    flow.append(flow[-1])
                if len(flow) > 3:
                    flow.pop(0)
                back = t - 1
                if len(flow) == 3 and 0 < back <= tiles:
                    change = wet_before * (zs * across(*flow))
                    if back <= cols // LANES:
                        elev_v[rows8, part(back - 1)] = elev_v[rows8, part(back - 1)] - change
                    else:
                        elev_v[rows8, cols - tail : cols] = elev_v[rows8, cols - tail : cols] - change[:, 0:tail]
                wet_before = wet

        def levels(n):
            base = pl.multiple_of(n * 8, 8)
            rows8 = pl.ds(base, 8)
            ms = merid[rows8, :]
            for t in range(1, tiles + 1):
                change = ms * vertical(flux, base, part(t), flux[rows8, part(t)])
                if t <= cols // LANES:
                    at = part(t - 1)
                else:
                    at = slice(cols - tail, cols)
                    change = change[:, 0:tail]
                elev_v[rows8, at] = elev_v[rows8, at] - wet_v[rows8, at].astype(f32) * change

        def out_copies(k):
            inside = pl.ds(top + k * piece, piece)
            outside = pl.ds(k * piece, piece)
            return (
                pltpu.make_async_copy(wx_v.at[inside, :], vel_out.at[0, 0, outside, :], out_sems.at[1 + k]),
                pltpu.make_async_copy(wy_v.at[inside, :], vel_out.at[0, 1, outside, :], out_sems.at[1 + pieces + k]),
                pltpu.make_async_copy(elev_v.at[inside, :], elev_out.at[0, outside, :], out_sems.at[1 + 2 * pieces + k]),
            )

        def both(n, carry):
            speeds(n + 1)
            levels(n)
            return carry

        def ahead_rows(n, carry):
            speeds(n)
            return carry

        per = piece // 8
        begin = top // 8
        done = begin
        for k in range(pieces):
            for copy in copies[k]:
                copy.wait()
            lax.fori_loop(begin + k * per, begin + (k + 1) * per, surfaces, 0)
            if k == 0:
                lax.fori_loop(begin - 1, begin + 1, ahead_rows, 0)
            stop = begin + (k + 1) * per - (2 if k + 1 < pieces else 0)
            lax.fori_loop(done, stop, both, 0)
            done = stop
            if k:
                for copy in out_copies(k - 1):
                    copy.start()
        for copy in out_copies(pieces - 1):
            copy.start()
        for k in range(pieces):
            for copy in out_copies(k):
                copy.wait()
        load_copy.wait()

    flat = pltpu.VMEM((tall, cols), f32)
    big = pltpu.VMEM((tall, width), f32)
    thin = pltpu.VMEM((tall, LANES), f32)
    return pl.pallas_call(
        body,
        out_shape=(
            jax.ShapeDtypeStruct((1, rows, cols), f32),
            jax.ShapeDtypeStruct((1, 2, rows, cols), f32),
            jax.ShapeDtypeStruct((1, rows, cols), f32),
        ),
        in_specs=[SMEM, SMEM, VMEM, VMEM, VMEM, VMEM, VMEM, VMEM, ANY, ANY, ANY, ANY, ANY],
        out_specs=(ANY, ANY, ANY),
        scratch_shapes=[
            flat, flat, flat, flat, flat, flat, pltpu.VMEM((tall, cols), jnp.int32), big, big,
            pltpu.VMEM((rows, cols), f32),
            pltpu.VMEM((names, tall, LANES), f32),
            pltpu.VMEM((names, tall, LANES), f32),
            thin, thin, thin,
            pltpu.SemaphoreType.DMA((pieces, 7)),
            pltpu.SemaphoreType.DMA((1 + 3 * pieces,)),
        ],
        compiler_params=pltpu.CompilerParams(vmem_limit_bytes=52 << 20),
        name="surge_step",
    )


def local(elevation, velocity, wind_forcing, ocean_depth, wet_mask, love_factor, wavenumbers):
    members, rows, cols = elevation.shape
    lat = lax.axis_size("lat")
    lon = lax.axis_size("lon")
    waves = wavenumbers.shape[0]
    assert members == 1 and waves == lat and lat % 16 == 0 and lon % 2 == 0
    bands = lat // 2
    lane_rows = round_up(rows + 4, LANES)
    width = LANES + round_up(cols + 2, LANES)
    steps = round_up((DEGREES + 1) // 2, 8)
    place = (
        lax.axis_index("lat").astype(jnp.int32)[None],
        lax.axis_index("lon").astype(jnp.int32)[None],
    )

    send, top, bottom, side, table = edge_kernel(rows, cols, width, lat, lon, waves, lane_rows)(
        *place, wavenumbers, elevation, velocity, wind_forcing, ocean_depth, wet_mask)
    got = lax.all_to_all(send, ("lat", "lon"), split_axis=0, concat_axis=0, tiled=True)
    values = legendre_kernel(bands, rows, lane_rows, steps)(*place, wavenumbers)
    values, bottom, top, side = lax.optimization_barrier((values, bottom, top, side))
    low = lax.ppermute(bottom, "lat", [(i, i + 1) for i in range(lat - 1)])
    high = lax.ppermute(top, "lat", [(i + 1, i) for i in range(lat - 1)])
    low_side = lax.ppermute(side, "lon", [(i, (i + 1) % lon) for i in range(lon)])
    high_side = low_side if lon == 2 else lax.ppermute(
        side, "lon", [(i, (i - 1) % lon) for i in range(lon)])
    send = synthesis_kernel(bands, rows, lane_rows, steps, lat, lon)(
        *place, wavenumbers, love_factor, got, pltpu.with_memory_space_constraint(values, pltpu.HBM))
    got = lax.all_to_all(send, ("lat", "lon"), split_axis=0, concat_axis=0, tiled=True)
    got = got.reshape(lat, lon, 2, lane_rows)[:, :2]
    return step_kernel(rows, cols, width, lat, waves, lane_rows)(
        *place, got, table, low, high, low_side, high_side,
        elevation, velocity, wind_forcing, ocean_depth, wet_mask)


def solution(mesh):
    return jax.shard_map(
        local,
        mesh=mesh,
        in_specs=(
            P(None, "lat", "lon"),
            P(None, None, "lat", "lon"),
            P(None, "lat", "lon"),
            P("lat", "lon"),
            P("lat", "lon"),
            P(),
            P(),
        ),
        out_specs=(P(None, "lat", "lon"), P(None, None, "lat", "lon"), P(None, "lat", "lon")),
        check_vma=False,
    )
```

```python
import math

import jax
import jax.numpy as jnp
from jax import lax
from jax.experimental import pallas as pl
from jax.experimental.pallas import tpu as pltpu
from jax.sharding import PartitionSpec as P

GRID_LAT = 3072
GRID_LON = 8640
DEGREES = 1081
LANES = 128

f32 = jnp.float32
bf16 = jnp.bfloat16
SMEM = pl.BlockSpec(memory_space=pltpu.SMEM)
VMEM = pl.BlockSpec(memory_space=pltpu.VMEM)
ANY = pl.BlockSpec(memory_space=pl.ANY)
HBM = pl.BlockSpec(memory_space=pltpu.HBM)
NT = (((1,), (1,)), ((), ()))
TN = (((0,), (0,)), ((), ()))


def round_up(value, step):
    return -(-value // step) * step


def sine_series(angle, orders=(13, 11, 9, 7, 5, 3, 1)):
    square = angle * angle
    series = None
    for order in orders:
        factor = (-1.0 if (order // 2) % 2 else 1.0) / math.factorial(order)
        series = jnp.full(angle.shape, factor, f32) if series is None else series * square + factor
    return angle * series


def cosine_of_units(units):
    turns = jnp.floor(units * (1.0 / GRID_LON) + 0.5)
    sine = sine_series((units - turns * GRID_LON) * (math.pi / GRID_LON))
    return 1.0 - 2.0 * sine * sine


def colatitude(row):
    return jnp.pi * (row.astype(f32) + 0.5) / GRID_LAT


def sine_of(angle):
    return sine_series(angle, (15, 13, 11, 9, 7, 5, 3, 1))


def split(value):
    high = value.astype(bf16)
    return high, (value - high.astype(f32)).astype(bf16)


def edge_kernel(rows, cols, width, lat, lon, waves, lane_rows):
    tail = cols % LANES or LANES

    def body(band_ref, sector_ref, waves_ref, elev, vel, wind, depth, wet,
             send, near, far, side, table, elev_v, wet_v, load_hi, load_lo,
             top_v, bottom_v, left_v, right_v, sems):
        band = band_ref[0]
        sector = sector_ref[0]
        first = pltpu.make_async_copy(elev.at[0], elev_v, sems.at[0])
        second = pltpu.make_async_copy(wet, wet_v, sems.at[1])
        first.start()
        second.start()
        fields = (vel.at[0, 0], vel.at[0, 1], wind.at[1], depth)
        copies = []
        for n, field in enumerate(fields):
            copies.append(pltpu.make_async_copy(field.at[pl.ds(0, 1), :], top_v.at[n], sems.at[2 + n]))
            copies.append(pltpu.make_async_copy(field.at[pl.ds(rows - 1, 1), :], bottom_v.at[n], sems.at[6 + n]))
        fields = (vel.at[0, 0], vel.at[0, 1], wind.at[0], depth)
        for n, field in enumerate(fields):
            copies.append(pltpu.make_async_copy(field.at[:, pl.ds(0, LANES)], left_v.at[n], sems.at[10 + n]))
            copies.append(pltpu.make_async_copy(
                field.at[:, pl.ds(cols - tail, tail)], right_v.at[n], sems.at[14 + n]))
        for copy in copies:
            copy.start()

        wave_row = lax.broadcasted_iota(jnp.int32, (2 * waves, LANES), 0)
        order = jnp.zeros((2 * waves, LANES), f32)
        for n in range(waves):
            order = jnp.where(wave_row // 2 == n, waves_ref[n].astype(f32), order)
        quarter = jnp.where(wave_row % 2 == 1, 0.25 * GRID_LON, 0.0)
        lane = lax.broadcasted_iota(jnp.int32, (2 * waves, LANES), 1)
        for tile in range(width // LANES):
            column = (sector * cols + (tile - 1) * LANES + lane).astype(f32)
            values = cosine_of_units(order * column - quarter)
            high, low = split(values)
            span = slice(tile * LANES, (tile + 1) * LANES)
            table[0 : 2 * waves, span] = high
            table[2 * waves : 4 * waves, span] = high
            table[4 * waves : 6 * waves, span] = low

        first.wait()
        second.wait()
        for start in range(0, rows, 8):
            here = slice(start, start + 8)
            high, low = split(elev_v[here, :] * wet_v[here, :].astype(f32))
            load_hi[here, :] = high
            load_lo[here, :] = low
        own = slice(LANES, LANES + cols)
        main_part = lax.dot_general(
            load_hi[...], table[2 * waves : 6 * waves, own], NT, preferred_element_type=f32)
        rest = lax.dot_general(load_lo[...], table[0 : 2 * waves, own], NT, preferred_element_type=f32)
        sums = (main_part[:, 0 : 2 * waves] + main_part[:, 2 * waves : 4 * waves] + rest) * (1.0 / GRID_LON)
        row = lax.broadcasted_iota(jnp.int32, (rows, lane_rows), 0)
        slot = lax.broadcasted_iota(jnp.int32, (rows, lane_rows), 1) - 2
        target = jnp.where(band < lat // 2, row, rows - 1 - row)
        pick = jnp.where(slot == target, 1.0, 0.0).astype(bf16)
        high, low = split(sums)
        lower = (sums - high.astype(f32) - low.astype(f32)).astype(bf16)
        turned = (
            lax.dot_general(high, pick, TN, preferred_element_type=f32)
            + lax.dot_general(low, pick, TN, preferred_element_type=f32)
            + lax.dot_general(lower, pick, TN, preferred_element_type=f32)
        )
        for n in range(waves):
            block = turned[2 * n : 2 * n + 2, :]
            for k in range(lon):
                send[n * lon + k, :, :] = block

        for copy in copies:
            copy.wait()
        odd = band % 2 == 1

        def pack(which, edge, start, line):
            which[0:2, :] = elev_v[start : start + 2, :]
            for n in range(4):
                which[2 + n : 3 + n, :] = edge[n]
            which[6:7, :] = wet_v[line : line + 1, :].astype(f32)
            which[7:8, :] = jnp.zeros((1, cols), f32)

        @pl.when(odd)
        def _():
            pack(near, top_v, 0, 0)
            pack(far, bottom_v, rows - 2, rows - 1)

        @pl.when(jnp.logical_not(odd))
        def _():
            pack(near, bottom_v, rows - 2, rows - 1)
            pack(far, top_v, 0, 0)

        blank = jnp.zeros((8, LANES - tail), f32)
        for start in range(0, rows, 8):
            here = slice(start, start + 8)
            lane8 = lax.broadcasted_iota(jnp.int32, (8, LANES), 1)
            left = [elev_v[here, 0:LANES]] + [left_v[n, here, :] for n in range(4)]
            left.append(wet_v[here, 0:LANES].astype(f32))
            right = [elev_v[here, cols - tail : cols]] + [right_v[n, here, :] for n in range(4)]
            right.append(wet_v[here, cols - tail : cols].astype(f32))
            right = [jnp.concatenate([x, blank], axis=1) if tail < LANES else x for x in right]
            packed = jnp.zeros((8, LANES), f32)
            for n in range(6):
                moved = pltpu.roll(left[n], 4 * n, 1) if n else left[n]
                packed = jnp.where(lane8 // 2 == 2 * n, moved, packed)
                moved = pltpu.roll(right[n], (4 * n + 2 - (tail - 2)) % LANES, 1)
                packed = jnp.where(lane8 // 2 == 2 * n + 1, moved, packed)
            side[here, :] = packed

    return pl.pallas_call(
        body,
        out_shape=(
            jax.ShapeDtypeStruct((lat * lon, 2, lane_rows), f32),
            jax.ShapeDtypeStruct((8, cols), f32),
            jax.ShapeDtypeStruct((8, cols), f32),
            jax.ShapeDtypeStruct((rows, LANES), f32),
            jax.ShapeDtypeStruct((6 * waves, width), bf16),
        ),
        in_specs=[SMEM, SMEM, SMEM, ANY, ANY, ANY, ANY, ANY],
        out_specs=(VMEM, VMEM, VMEM, VMEM, VMEM),
        scratch_shapes=[
            pltpu.VMEM((rows, cols), f32),
            pltpu.VMEM((rows, cols), jnp.int32),
            pltpu.VMEM((rows, cols), bf16),
            pltpu.VMEM((rows, cols), bf16),
            pltpu.VMEM((4, 1, cols), f32),
            pltpu.VMEM((4, 1, cols), f32),
            pltpu.VMEM((4, rows, LANES), f32),
            pltpu.VMEM((4, rows, tail), f32),
            pltpu.SemaphoreType.DMA((18,)),
        ],
        name="edge_fourier",
    )


GROW = 2.0**40
SHRINK = 2.0**-96
SHRINK_LOG = 96.0 * math.log(2.0)


def legendre_kernel(bands, rows, lane_rows, steps):
    tile = (8, LANES)
    spots = [(r, t) for r in range(0, bands, 8) for t in range(0, lane_rows, LANES)]
    pairs = 8
    parts = 4
    share = steps // parts

    def body(band_ref, sector_ref, waves_ref, values_out, coef_a, coef_s, coef_t, values, sems):
        order = waves_ref[band_ref[0]]
        parity = sector_ref[0] % 2
        order_real = order.astype(f32)
        count = coef_a.shape[0]
        for start in range(0, count, 8):
            index = (lax.broadcasted_iota(jnp.int32, tile, 0) + start).astype(f32)
            index = jnp.maximum(index, 1.0)
            double = 2.0 * (index + order_real)
            above = index + 2.0 * order_real
            below = double - 1.0
            raising = jnp.sqrt(below * (double + 1.0) / (index * above))
            ratio = raising / below
            coef_a[start : start + 8, :] = raising
            coef_s[start : start + 8, :] = ratio * above
            coef_t[start : start + 8, :] = ratio * (index - 1.0)
        ladder_rows = round_up(DEGREES, 8 * LANES) // LANES
        ladder = (
            lax.broadcasted_iota(jnp.int32, (ladder_rows, LANES), 0) * LANES
            + lax.broadcasted_iota(jnp.int32, (ladder_rows, LANES), 1)
        ).astype(f32)
        used = (ladder >= 2.0) & (ladder <= order_real)
        safe = jnp.maximum(ladder, 1.0)
        total = jnp.sum(jnp.where(used, jnp.log((2.0 * safe + 1.0) / (2.0 * safe)), 0.0))
        total = 0.5 * (total + jnp.where(order > 0, math.log(3.0), 0.0))

        gap, level, now, slope = [], [], [], []
        for r, t in spots:
            row = (
                (lax.broadcasted_iota(jnp.int32, tile, 0) + r) * rows
                + lax.broadcasted_iota(jnp.int32, tile, 1) + (t - 2)
            )
            angle = colatitude(jnp.clip(row, 0, GRID_LAT // 2 + 1))
            half = sine_series(0.5 * angle)
            cosine = 1.0 - 2.0 * half * half
            gap.append(1.0 - cosine)
            log_start = total + order_real * jnp.log(sine_of(angle))
            rung = jnp.minimum(jnp.ceil((log_start - math.log(GROW)) / SHRINK_LOG), 0.0)
            level.append(rung)
            now.append(jnp.exp(log_start - rung * SHRINK_LOG))
            slope.append(jnp.zeros(tile, f32))

        def scale_of(level):
            return jnp.where(level == 0.0, 1.0, jnp.where(level == -1.0, SHRINK, 0.0))

        def advance(k, now, slope):
            a = jnp.broadcast_to(coef_a[pl.ds(k, 1), :], tile)
            s = jnp.broadcast_to(coef_s[pl.ds(k, 1), :], tile)
            t = jnp.broadcast_to(coef_t[pl.ds(k, 1), :], tile)
            drop = [a * h for h in gap]
            kept = [t * y for y in slope]
            slope = [y - c * x for x, y, c in zip(now, kept, drop)]
            return [(s - c) * x + y for x, y, c in zip(now, kept, drop)], slope

        odd = parity == 1
        next_now, next_slope = advance(1, now, slope)
        now = [jnp.where(odd, y, x) for x, y in zip(now, next_now)]
        slope = [jnp.where(odd, y, x) for x, y in zip(slope, next_slope)]

        def block(n, carry):
            now, slope, level = carry
            scale = [scale_of(x) for x in level]
            for q in range(pairs):
                j = n * pairs + q
                for (r, t), x, y in zip(spots, now, scale):
                    values[pl.ds(j, 1), r : r + 8, t : t + LANES] = (x * y)[None]
                k = 2 * j + parity + 1
                now, slope = advance(k, now, slope)
                now, slope = advance(k + 1, now, slope)
            large = [(jnp.maximum(jnp.abs(x), jnp.abs(y)) > GROW) & (z < 0.0)
                     for x, y, z in zip(now, slope, level)]
            factor = [jnp.where(x, SHRINK, 1.0) for x in large]
            level = [jnp.where(x, z + 1.0, z) for x, z in zip(large, level)]
            return [x * y for x, y in zip(now, factor)], [x * y for x, y in zip(slope, factor)], level

        state = (now, slope, level)
        copies = []
        for k in range(parts):
            state = lax.fori_loop(k * share // pairs, (k + 1) * share // pairs, block, state)
            here = pl.ds(k * share, share)
            copies.append(pltpu.make_async_copy(values.at[here], values_out.at[here], sems.at[k]))
            copies[k].start()
        for copy in copies:
            copy.wait()

    coefs = pltpu.VMEM((2 * steps + 8, LANES), f32)
    return pl.pallas_call(
        body,
        out_shape=pltpu.HBM((steps, bands, lane_rows), f32),
        in_specs=[SMEM, SMEM, SMEM],
        out_specs=HBM,
        scratch_shapes=[coefs, coefs, coefs, pltpu.VMEM((steps, bands, lane_rows), f32),
                        pltpu.SemaphoreType.DMA((parts,))],
        compiler_params=pltpu.CompilerParams(vmem_limit_bytes=16 << 20),
        cost_estimate=pl.CostEstimate(flops=12 * steps * bands * lane_rows, transcendentals=0,
                                      bytes_accessed=4 * steps * bands * lane_rows),
        name="legendre_values",
    )


def synthesis_kernel(bands, rows, lane_rows, steps, lat, lon):
    parts = 4
    share = steps // parts

    def body(band_ref, sector_ref, waves_ref, love, got, values_in, send, mass, totals, values, sems):
        copies = []
        for k in range(parts):
            here = pl.ds(k * share, share)
            copies.append(pltpu.make_async_copy(values_in.at[here], values.at[here], sems.at[k]))
            copies[k].start()
        order = waves_ref[band_ref[0]]
        parity = sector_ref[0] % 2
        sign = jnp.where(parity == 1, -1.0, 1.0)
        slot = lax.broadcasted_iota(jnp.int32, (1, lane_rows), 1)
        inside = (slot >= 2) & (slot < rows + 2)
        for b in range(bands):
            north = got[b * lon]
            south = got[(lat - 1 - b) * lon]
            for k in range(1, lon):
                north = north + got[b * lon + k]
                south = south + got[(lat - 1 - b) * lon + k]
            row = b * rows + slot - 2
            sine = sine_of(colatitude(jnp.clip(row, 0, GRID_LAT // 2 + 1)))
            weight = (jnp.pi / (2.0 * GRID_LAT)) * sine
            both = jnp.where(inside, (north + sign * south) * weight, 0.0)
            mass[0, b : b + 1, :] = both[0:1]
            mass[1, b : b + 1, :] = both[1:2]
        sub = lax.broadcasted_iota(jnp.int32, (8, LANES), 0)
        tiles = [(r, t) for r in range(0, bands, 8) for t in range(0, lane_rows, LANES)]

        def fold(parts, shift):
            half = len(parts) // 2
            lower = sub % (2 * shift) < shift
            out = []
            for x, y in zip(parts[:half], parts[half:]):
                out.append(jnp.where(lower, y + pltpu.roll(y, 8 - shift, 0), x + pltpu.roll(x, shift, 0)))
            return out

        def analyse(n, carry):
            for c in range(2):
                parts = []
                for q in (7, 6, 5, 4, 3, 2, 1, 0):
                    acc = None
                    for r, t in tiles:
                        term = mass[c, r : r + 8, t : t + LANES] * values[n * 8 + q, r : r + 8, t : t + LANES]
                        acc = term if acc is None else acc + term
                    parts.append(acc)
                for shift in (4, 2, 1):
                    parts = fold(parts, shift)
                totals[c, pl.ds(n * 8, 8), :] = parts[0]
            return carry

        for k in range(parts):
            copies[k].wait()
            lax.fori_loop(k * share // 8, (k + 1) * share // 8, analyse, 0)
        degree = order + parity + 2 * lax.broadcasted_iota(jnp.int32, (steps, LANES), 0)
        weight = jnp.where(degree < DEGREES, 1.0 / (2.0 * degree.astype(f32) + 1.0), 0.0)
        for c in range(2):
            totals[c] = jnp.sum(totals[c], axis=1, keepdims=True) * weight

        def synthesise(n, carry):
            carry = list(carry)
            for q in range(8):
                j = n * 8 + q
                weight = love[jnp.minimum(order + parity + 2 * j, DEGREES - 1)]
                factors = [jnp.broadcast_to(totals[c, pl.ds(j, 1), :], (8, LANES)) * weight for c in range(2)]
                for i, (r, t) in enumerate(tiles):
                    value = values[j, r : r + 8, t : t + LANES]
                    for c in range(2):
                        carry[2 * i + c] = carry[2 * i + c] + factors[c] * value
            return tuple(carry)

        zero = jnp.zeros((8, LANES), f32)
        found = lax.fori_loop(0, steps // 8, synthesise, (zero,) * (2 * len(tiles)))
        for b in range(bands):
            for t in range(0, lane_rows, LANES):
                i = tiles.index((b // 8 * 8, t))
                for c in range(2):
                    line = found[2 * i + c][b % 8 : b % 8 + 1, :]
                    for k in range(lon):
                        send[b * lon + k, c : c + 1, t : t + LANES] = line
                        send[(lat - 1 - b) * lon + k, c : c + 1, t : t + LANES] = line

    return pl.pallas_call(
        body,
        out_shape=jax.ShapeDtypeStruct((lat * lon, 2, lane_rows), f32),
        in_specs=[SMEM, SMEM, SMEM, SMEM, VMEM, HBM],
        out_specs=VMEM,
        scratch_shapes=[
            pltpu.VMEM((2, bands, lane_rows), f32),
            pltpu.VMEM((2, steps, LANES), f32),
            pltpu.VMEM((steps, bands, lane_rows), f32),
            pltpu.SemaphoreType.DMA((parts,)),
        ],
        compiler_params=pltpu.CompilerParams(vmem_limit_bytes=16 << 20),
        name="degree_sums",
    )


def step_kernel(rows, cols, width, lat, waves, lane_rows):
    tail = cols % LANES or LANES
    tiles = -(-cols // LANES)
    tall = rows + 32
    top = 16
    own = slice(LANES, LANES + cols)
    meridional = 0.1 * GRID_LAT / GRID_LON
    pieces = 6 if rows % 96 == 0 else 1
    piece = rows // pieces
    names = 6

    def body(band_ref, sector_ref, got, table, near, far, low_side, high_side,
             elev, vel, wind, depth, wet, elev_out, vel_out, load_out,
             elev_v, u_v, v_v, wx_v, wy_v, depth_v, wet_v, surf, flux, load_v,
             left_v, right_v, zonal, sine_v, merid, sems, out_sems):
        band = band_ref[0]
        fields = (
            (elev.at[0], elev_v), (depth, depth_v), (wet, wet_v), (vel.at[0, 0], u_v),
            (vel.at[0, 1], v_v), (wind.at[1], wy_v), (wind.at[0], wx_v),
        )
        copies = []
        for k in range(pieces):
            inside = pl.ds(top + k * piece, piece)
            outside = pl.ds(k * piece, piece)
            copies.append([pltpu.make_async_copy(
                source.at[outside, :], buffer.at[inside, :], sems.at[k, n])
                for n, (source, buffer) in enumerate(fields)])
            for copy in copies[k]:
                copy.start()

        row = lax.broadcasted_iota(jnp.int32, (tall, LANES), 0) - top + band * rows
        row = jnp.clip(row, 0, GRID_LAT - 1)
        sine = sine_of(colatitude(jnp.minimum(row, GRID_LAT - 1 - row)))
        sine_v[...] = sine
        zonal[...] = 0.05 / sine
        merid[...] = meridional / sine

        sign = jnp.where(band < lat // 2, 1.0, -1.0)
        mixed = (got[:, 0] + sign * got[:, 1]).reshape(2 * waves, lane_rows)
        first, second = split(mixed)
        stacked = jnp.concatenate([first, second, first], axis=0)
        line = lax.broadcasted_iota(jnp.int32, (rows + 8, lane_rows), 0)
        line = jnp.where(line < rows, line, jnp.where(line < rows + 2, line - rows - 2, line - 2))
        slot = lax.broadcasted_iota(jnp.int32, (rows + 8, lane_rows), 1)
        target = jnp.where(band < lat // 2, line + 2, rows + 1 - line)
        pick = jnp.where(slot == target, 1.0, 0.0).astype(bf16)
        factors = lax.dot_general(pick, stacked, NT, preferred_element_type=f32).astype(bf16)

        here = slice(top, top + rows)
        for n in range(names):
            left_v[n, here, :] = pltpu.roll(low_side[...], (124 - 4 * n) % LANES, 1)
            right_v[n, here, :] = pltpu.roll(high_side[...], (tail - 4 * n) % LANES, 1)

        odd = band % 2 == 1
        low = jnp.where(odd, near[...], far[...])
        high = jnp.where(odd, far[...], near[...])
        elev_v[top - 2 : top, :] = low[0:2, :]
        elev_v[top + rows : top + rows + 2, :] = high[0:2, :]
        for n, buffer in enumerate((u_v, v_v, wy_v, depth_v, wet_v)):
            buffer[top - 1 : top, :] = low[2 + n : 3 + n, :].astype(buffer.dtype)
            buffer[top + rows : top + rows + 1, :] = high[2 + n : 3 + n, :].astype(buffer.dtype)

        group = 4
        after = slice(top + rows, top + rows + 2)
        for t in range(0, width // LANES, group):
            begin = t * LANES
            end = min((t + group) * LANES, width)
            loading = lax.dot_general(
                factors, table[:, begin:end], (((1,), (0,)), ((), ())), preferred_element_type=f32)
            surf[here, begin:end] = loading[0:rows]
            first_lane = max(begin, LANES)
            last_lane = min(end, LANES + cols)
            inner = slice(first_lane - LANES, last_lane - LANES)
            outer = slice(first_lane, last_lane)
            cut = slice(first_lane - begin, last_lane - begin)
            load_v[:, inner] = loading[0:rows, cut]
            surf[top - 2 : top, outer] = elev_v[top - 2 : top, inner] - loading[rows : rows + 2, cut]
            surf[after, outer] = elev_v[after, inner] - loading[rows + 2 : rows + 4, cut]
        load_copy = pltpu.make_async_copy(load_v, load_out.at[0], out_sems.at[0])
        load_copy.start()

        lane8 = lax.broadcasted_iota(jnp.int32, (8, LANES), 1)
        sub8 = lax.broadcasted_iota(jnp.int32, (8, LANES), 0)
        count = width // LANES

        def part(t):
            return slice(t * LANES, (t + 1) * LANES)

        def fetch(t, rows8, n, buffer):
            if t == 0:
                return left_v[n, rows8, :]
            if t <= cols // LANES:
                return buffer[rows8, part(t - 1)].astype(f32)
            if tail == LANES:
                return right_v[n, rows8, :]
            return jnp.concatenate(
                [buffer[rows8, cols - tail : cols].astype(f32), right_v[n, rows8, tail:LANES]], axis=1)

        def keep(buffer, rows8, t, value):
            if 0 < t <= cols // LANES:
                buffer[rows8, part(t - 1)] = value
            elif t and tail < LANES:
                buffer[rows8, cols - tail : cols] = value[:, 0:tail]

        def surfaces(n, carry):
            rows8 = pl.ds(pl.multiple_of(n * 8, 8), 8)
            for t in range(count):
                surf[rows8, part(t)] = fetch(t, rows8, 0, elev_v) - surf[rows8, part(t)]
            return carry

        def vertical(ref, base, at, centre):
            before = jnp.where(sub8 == 7, ref[pl.ds(base - 8, 8), at], centre)
            after = jnp.where(sub8 == 0, ref[pl.ds(base + 8, 8), at], centre)
            return pltpu.roll(after, 7, 0) - pltpu.roll(before, 1, 0)

        def across(behind, centre, ahead):
            ahead = jnp.where(lane8 == 0, ahead, centre)
            behind = jnp.where(lane8 == LANES - 1, behind, centre)
            return pltpu.roll(ahead, LANES - 1, 1) - pltpu.roll(behind, 1, 1)

        def speeds(n):
            base = pl.multiple_of(n * 8, 8)
            rows8 = pl.ds(base, 8)
            zs = zonal[rows8, :]
            sn = sine_v[rows8, :]
            level = [surf[rows8, part(0)], surf[rows8, part(0)]]
            flow = []
            wet_before = None
            for t in range(count + 1):
                if t < count:
                    at = part(t)
                    level.append(surf[rows8, part(t + 1)] if t + 1 < count else level[-1])
                    level.pop(0) if len(level) > 3 else None
                    u = fetch(t, rows8, 1, u_v)
                    v = fetch(t, rows8, 2, v_v)
                    d = fetch(t, rows8, 4, depth_v)
                    wet = fetch(t, rows8, 5, wet_v)
                    drag = wet / (d + 0.1 * jnp.sqrt(u * u + v * v))
                    new_u = drag * (u * d + fetch(t, rows8, 3, wx_v) - (zs * d) * across(*level))
                    keep(wx_v, rows8, t, new_u)
                    flow.append(d * new_u)
                    if t and not (t > cols // LANES and tail == LANES):
                        if t <= cols // LANES:
                            push = wy_v[rows8, part(t - 1)]
                        else:
                            push = jnp.concatenate(
                                [wy_v[rows8, cols - tail : cols], jnp.zeros((8, LANES - tail), f32)], axis=1)
                        new_v = drag * (v * d + push - (meridional * d) * vertical(surf, base, at, level[1]))
                        keep(wy_v, rows8, t, new_v)
                        flux[rows8, at] = sn * d * new_v
                else:
                    flow.append(flow[-1])
                if len(flow) > 3:
                    flow.pop(0)
                back = t - 1
                if len(flow) == 3 and 0 < back <= tiles:
                    change = wet_before * (zs * across(*flow))
                    if back <= cols // LANES:
                        elev_v[rows8, part(back - 1)] = elev_v[rows8, part(back - 1)] - change
                    else:
                        elev_v[rows8, cols - tail : cols] = elev_v[rows8, cols - tail : cols] - change[:, 0:tail]
                wet_before = wet

        def levels(n):
            base = pl.multiple_of(n * 8, 8)
            rows8 = pl.ds(base, 8)
            ms = merid[rows8, :]
            for t in range(1, tiles + 1):
                change = ms * vertical(flux, base, part(t), flux[rows8, part(t)])
                if t <= cols // LANES:
                    at = part(t - 1)
                else:
                    at = slice(cols - tail, cols)
                    change = change[:, 0:tail]
                elev_v[rows8, at] = elev_v[rows8, at] - wet_v[rows8, at].astype(f32) * change

        def out_copies(k):
            inside = pl.ds(top + k * piece, piece)
            outside = pl.ds(k * piece, piece)
            return (
                pltpu.make_async_copy(wx_v.at[inside, :], vel_out.at[0, 0, outside, :], out_sems.at[1 + k]),
                pltpu.make_async_copy(wy_v.at[inside, :], vel_out.at[0, 1, outside, :], out_sems.at[1 + pieces + k]),
                pltpu.make_async_copy(elev_v.at[inside, :], elev_out.at[0, outside, :], out_sems.at[1 + 2 * pieces + k]),
            )

        def both(n, carry):
            speeds(n + 1)
            levels(n)
            return carry

        def ahead_rows(n, carry):
            speeds(n)
            return carry

        per = piece // 8
        begin = top // 8
        done = begin
        for k in range(pieces):
            for copy in copies[k]:
                copy.wait()
            lax.fori_loop(begin + k * per, begin + (k + 1) * per, surfaces, 0)
            if k == 0:
                lax.fori_loop(begin - 1, begin + 1, ahead_rows, 0)
            stop = begin + (k + 1) * per - (2 if k + 1 < pieces else 0)
            lax.fori_loop(done, stop, both, 0)
            done = stop
            if k:
                for copy in out_copies(k - 1):
                    copy.start()
        for copy in out_copies(pieces - 1):
            copy.start()
        for k in range(pieces):
            for copy in out_copies(k):
                copy.wait()
        load_copy.wait()

    flat = pltpu.VMEM((tall, cols), f32)
    big = pltpu.VMEM((tall, width), f32)
    thin = pltpu.VMEM((tall, LANES), f32)
    return pl.pallas_call(
        body,
        out_shape=(
            jax.ShapeDtypeStruct((1, rows, cols), f32),
            jax.ShapeDtypeStruct((1, 2, rows, cols), f32),
            jax.ShapeDtypeStruct((1, rows, cols), f32),
        ),
        in_specs=[SMEM, SMEM, VMEM, VMEM, VMEM, VMEM, VMEM, VMEM, ANY, ANY, ANY, ANY, ANY],
        out_specs=(ANY, ANY, ANY),
        scratch_shapes=[
            flat, flat, flat, flat, flat, flat, pltpu.VMEM((tall, cols), jnp.int32), big, big,
            pltpu.VMEM((rows, cols), f32),
            pltpu.VMEM((names, tall, LANES), f32),
            pltpu.VMEM((names, tall, LANES), f32),
            thin, thin, thin,
            pltpu.SemaphoreType.DMA((pieces, 7)),
            pltpu.SemaphoreType.DMA((1 + 3 * pieces,)),
        ],
        compiler_params=pltpu.CompilerParams(vmem_limit_bytes=52 << 20),
        name="surge_step",
    )


def local(elevation, velocity, wind_forcing, ocean_depth, wet_mask, love_factor, wavenumbers):
    members, rows, cols = elevation.shape
    lat = lax.axis_size("lat")
    lon = lax.axis_size("lon")
    waves = wavenumbers.shape[0]
    assert members == 1 and waves == lat and lat % 16 == 0 and lon % 2 == 0
    bands = lat // 2
    lane_rows = round_up(rows + 4, LANES)
    width = LANES + round_up(cols + 2, LANES)
    steps = round_up((DEGREES + 1) // 2, 8)
    place = (
        lax.axis_index("lat").astype(jnp.int32)[None],
        lax.axis_index("lon").astype(jnp.int32)[None],
    )

    send, first, second, side, table = edge_kernel(rows, cols, width, lat, lon, waves, lane_rows)(
        *place, wavenumbers, elevation, velocity, wind_forcing, ocean_depth, wet_mask)
    got = lax.all_to_all(send, ("lat", "lon"), split_axis=0, concat_axis=0, tiled=True)
    values = legendre_kernel(bands, rows, lane_rows, steps)(*place, wavenumbers)
    values, first, second, side = lax.optimization_barrier((values, first, second, side))
    pairs = [(i, i ^ 1) for i in range(lat)]
    others = [(i, min(max(i - 1 + 2 * (i % 2), 0), lat - 1)) for i in range(lat)]
    near = lax.ppermute(first, "lat", pairs)
    far = lax.ppermute(second, "lat", others)
    low_side = lax.ppermute(side, "lon", [(i, (i + 1) % lon) for i in range(lon)])
    high_side = low_side if lon == 2 else lax.ppermute(
        side, "lon", [(i, (i - 1) % lon) for i in range(lon)])
    send = synthesis_kernel(bands, rows, lane_rows, steps, lat, lon)(
        *place, wavenumbers, love_factor, got, pltpu.with_memory_space_constraint(values, pltpu.HBM))
    got = lax.all_to_all(send, ("lat", "lon"), split_axis=0, concat_axis=0, tiled=True)
    got = got.reshape(lat, lon, 2, lane_rows)[:, :2]
    return step_kernel(rows, cols, width, lat, waves, lane_rows)(
        *place, got, table, near, far, low_side, high_side,
        elevation, velocity, wind_forcing, ocean_depth, wet_mask)


def solution(mesh):
    return jax.shard_map(
        local,
        mesh=mesh,
        in_specs=(
            P(None, "lat", "lon"),
            P(None, None, "lat", "lon"),
            P(None, "lat", "lon"),
            P("lat", "lon"),
            P("lat", "lon"),
            P(),
            P(),
        ),
        out_specs=(P(None, "lat", "lon"), P(None, None, "lat", "lon"), P(None, "lat", "lon")),
        check_vma=False,
    )
```

```python
import math

import jax
import jax.numpy as jnp
from jax import lax
from jax.experimental import pallas as pl
from jax.experimental.pallas import tpu as pltpu
from jax.sharding import PartitionSpec as P

GRID_LAT = 3072
GRID_LON = 8640
DEGREES = 1081
LANES = 128

f32 = jnp.float32
bf16 = jnp.bfloat16
SMEM = pl.BlockSpec(memory_space=pltpu.SMEM)
VMEM = pl.BlockSpec(memory_space=pltpu.VMEM)
ANY = pl.BlockSpec(memory_space=pl.ANY)
HBM = pl.BlockSpec(memory_space=pltpu.HBM)
NT = (((1,), (1,)), ((), ()))
TN = (((0,), (0,)), ((), ()))


def round_up(value, step):
    return -(-value // step) * step


def sine_series(angle, orders=(13, 11, 9, 7, 5, 3, 1)):
    square = angle * angle
    series = None
    for order in orders:
        factor = (-1.0 if (order // 2) % 2 else 1.0) / math.factorial(order)
        series = jnp.full(angle.shape, factor, f32) if series is None else series * square + factor
    return angle * series


def cosine_of_units(units):
    turns = jnp.floor(units * (1.0 / GRID_LON) + 0.5)
    sine = sine_series((units - turns * GRID_LON) * (math.pi / GRID_LON))
    return 1.0 - 2.0 * sine * sine


def colatitude(row):
    return jnp.pi * (row.astype(f32) + 0.5) / GRID_LAT


def sine_of(angle):
    return sine_series(angle, (15, 13, 11, 9, 7, 5, 3, 1))


def split(value):
    high = value.astype(bf16)
    return high, (value - high.astype(f32)).astype(bf16)


def edge_kernel(rows, cols, width, lat, lon, waves, lane_rows):
    tail = cols % LANES or LANES
    pieces = 4 if rows % 32 == 0 else 1
    piece = rows // pieces

    def body(band_ref, sector_ref, waves_ref, elev, vel, wind, depth, wet,
             send, top, bottom, side, table_out, table, elev_v, wet_v, load_hi, load_lo,
             top_v, bottom_v, left_v, right_v, sems):
        band = band_ref[0]
        sector = sector_ref[0]
        main = []
        for k in range(pieces):
            here = pl.ds(k * piece, piece)
            main.append((
                pltpu.make_async_copy(elev.at[0, here, :], elev_v.at[here, :], sems.at[18 + k]),
                pltpu.make_async_copy(wet.at[here, :], wet_v.at[here, :], sems.at[18 + pieces + k]),
            ))
            for copy in main[k]:
                copy.start()
        fields = (vel.at[0, 0], vel.at[0, 1], wind.at[1], depth)
        copies = []
        for n, field in enumerate(fields):
            copies.append(pltpu.make_async_copy(field.at[pl.ds(0, 1), :], top_v.at[n], sems.at[2 + n]))
            copies.append(pltpu.make_async_copy(field.at[pl.ds(rows - 1, 1), :], bottom_v.at[n], sems.at[6 + n]))
        fields = (vel.at[0, 0], vel.at[0, 1], wind.at[0], depth)
        for n, field in enumerate(fields):
            copies.append(pltpu.make_async_copy(field.at[:, pl.ds(0, LANES)], left_v.at[n], sems.at[10 + n]))
            copies.append(pltpu.make_async_copy(
                field.at[:, pl.ds(cols - tail, tail)], right_v.at[n], sems.at[14 + n]))
        for copy in copies:
            copy.start()

        wave_row = lax.broadcasted_iota(jnp.int32, (2 * waves, LANES), 0)
        order = jnp.zeros((2 * waves, LANES), f32)
        for n in range(waves):
            order = jnp.where(wave_row // 2 == n, waves_ref[n].astype(f32), order)
        quarter = jnp.where(wave_row % 2 == 1, 0.25 * GRID_LON, 0.0)
        lane = lax.broadcasted_iota(jnp.int32, (2 * waves, LANES), 1)
        for tile in range(width // LANES):
            column = (sector * cols + (tile - 1) * LANES + lane).astype(f32)
            values = cosine_of_units(order * column - quarter)
            high, low = split(values)
            span = slice(tile * LANES, (tile + 1) * LANES)
            table[0 : 2 * waves, span] = high
            table[2 * waves : 4 * waves, span] = high
            table[4 * waves : 6 * waves, span] = low

        table_copy = pltpu.make_async_copy(table, table_out, sems.at[0])
        table_copy.start()
        for start in range(0, rows, 8):
            if start % piece == 0:
                for copy in main[start // piece]:
                    copy.wait()
            here = slice(start, start + 8)
            high, low = split(elev_v[here, :] * wet_v[here, :].astype(f32))
            load_hi[here, :] = high
            load_lo[here, :] = low
        own = slice(LANES, LANES + cols)
        main_part = lax.dot_general(
            load_hi[...], table[2 * waves : 6 * waves, own], NT, preferred_element_type=f32)
        rest = lax.dot_general(load_lo[...], table[0 : 2 * waves, own], NT, preferred_element_type=f32)
        sums = (main_part[:, 0 : 2 * waves] + main_part[:, 2 * waves : 4 * waves] + rest) * (1.0 / GRID_LON)
        row = lax.broadcasted_iota(jnp.int32, (rows, lane_rows), 0)
        slot = lax.broadcasted_iota(jnp.int32, (rows, lane_rows), 1) - 2
        target = jnp.where(band < lat // 2, row, rows - 1 - row)
        pick = jnp.where(slot == target, 1.0, 0.0).astype(bf16)
        high, low = split(sums)
        lower = (sums - high.astype(f32) - low.astype(f32)).astype(bf16)
        turned = (
            lax.dot_general(high, pick, TN, preferred_element_type=f32)
            + lax.dot_general(low, pick, TN, preferred_element_type=f32)
            + lax.dot_general(lower, pick, TN, preferred_element_type=f32)
        )
        for n in range(waves):
            block = turned[2 * n : 2 * n + 2, :]
            for k in range(lon):
                send[n * lon + k, :, :] = block

        for copy in copies:
            copy.wait()
        top[0:2, :] = elev_v[0:2, :]
        bottom[0:2, :] = elev_v[rows - 2 : rows, :]
        for n in range(4):
            top[2 + n : 3 + n, :] = top_v[n]
            bottom[2 + n : 3 + n, :] = bottom_v[n]
        top[6:7, :] = wet_v[0:1, :].astype(f32)
        bottom[6:7, :] = wet_v[rows - 1 : rows, :].astype(f32)
        top[7:8, :] = jnp.zeros((1, cols), f32)
        bottom[7:8, :] = jnp.zeros((1, cols), f32)
        blank = jnp.zeros((8, LANES - tail), f32)
        for start in range(0, rows, 8):
            here = slice(start, start + 8)
            lane8 = lax.broadcasted_iota(jnp.int32, (8, LANES), 1)
            left = [elev_v[here, 0:LANES]] + [left_v[n, here, :] for n in range(4)]
            left.append(wet_v[here, 0:LANES].astype(f32))
            right = [elev_v[here, cols - tail : cols]] + [right_v[n, here, :] for n in range(4)]
            right.append(wet_v[here, cols - tail : cols].astype(f32))
            right = [jnp.concatenate([x, blank], axis=1) if tail < LANES else x for x in right]
            packed = jnp.zeros((8, LANES), f32)
            for n in range(6):
                moved = pltpu.roll(left[n], 4 * n, 1) if n else left[n]
                packed = jnp.where(lane8 // 2 == 2 * n, moved, packed)
                moved = pltpu.roll(right[n], (4 * n + 2 - (tail - 2)) % LANES, 1)
                packed = jnp.where(lane8 // 2 == 2 * n + 1, moved, packed)
            side[here, :] = packed
        table_copy.wait()

    return pl.pallas_call(
        body,
        out_shape=(
            jax.ShapeDtypeStruct((lat * lon, 2, lane_rows), f32),
            jax.ShapeDtypeStruct((8, cols), f32),
            jax.ShapeDtypeStruct((8, cols), f32),
            jax.ShapeDtypeStruct((rows, LANES), f32),
            jax.ShapeDtypeStruct((6 * waves, width), bf16),
        ),
        in_specs=[SMEM, SMEM, SMEM, ANY, ANY, ANY, ANY, ANY],
        out_specs=(VMEM, VMEM, VMEM, VMEM, ANY),
        scratch_shapes=[
            pltpu.VMEM((6 * waves, width), bf16),
            pltpu.VMEM((rows, cols), f32),
            pltpu.VMEM((rows, cols), jnp.int32),
            pltpu.VMEM((rows, cols), bf16),
            pltpu.VMEM((rows, cols), bf16),
            pltpu.VMEM((4, 1, cols), f32),
            pltpu.VMEM((4, 1, cols), f32),
            pltpu.VMEM((4, rows, LANES), f32),
            pltpu.VMEM((4, rows, tail), f32),
            pltpu.SemaphoreType.DMA((18 + 2 * pieces,)),
        ],
        name="edge_fourier",
    )


GROW = 2.0**40
SHRINK = 2.0**-96
SHRINK_LOG = 96.0 * math.log(2.0)


def legendre_kernel(bands, rows, lane_rows, steps):
    tile = (8, LANES)
    spots = [(r, t) for r in range(0, bands, 8) for t in range(0, lane_rows, LANES)]
    pairs = 8
    parts = 4
    share = steps // parts

    def body(band_ref, sector_ref, waves_ref, values_out, coef_a, coef_s, coef_t, values, sems):
        order = waves_ref[band_ref[0]]
        parity = sector_ref[0] % 2
        order_real = order.astype(f32)
        count = coef_a.shape[0]
        for start in range(0, count, 8):
            index = (lax.broadcasted_iota(jnp.int32, tile, 0) + start).astype(f32)
            index = jnp.maximum(index, 1.0)
            double = 2.0 * (index + order_real)
            above = index + 2.0 * order_real
            below = double - 1.0
            raising = jnp.sqrt(below * (double + 1.0) / (index * above))
            ratio = raising / below
            coef_a[start : start + 8, :] = raising
            coef_s[start : start + 8, :] = ratio * above
            coef_t[start : start + 8, :] = ratio * (index - 1.0)
        ladder_rows = round_up(DEGREES, 8 * LANES) // LANES
        ladder = (
            lax.broadcasted_iota(jnp.int32, (ladder_rows, LANES), 0) * LANES
            + lax.broadcasted_iota(jnp.int32, (ladder_rows, LANES), 1)
        ).astype(f32)
        used = (ladder >= 2.0) & (ladder <= order_real)
        safe = jnp.maximum(ladder, 1.0)
        total = jnp.sum(jnp.where(used, jnp.log((2.0 * safe + 1.0) / (2.0 * safe)), 0.0))
        total = 0.5 * (total + jnp.where(order > 0, math.log(3.0), 0.0))

        gap, level, now, slope = [], [], [], []
        for r, t in spots:
            row = (
                (lax.broadcasted_iota(jnp.int32, tile, 0) + r) * rows
                + lax.broadcasted_iota(jnp.int32, tile, 1) + (t - 2)
            )
            angle = colatitude(jnp.clip(row, 0, GRID_LAT // 2 + 1))
            half = sine_series(0.5 * angle)
            cosine = 1.0 - 2.0 * half * half
            gap.append(1.0 - cosine)
            log_start = total + order_real * jnp.log(sine_of(angle))
            rung = jnp.minimum(jnp.ceil((log_start - math.log(GROW)) / SHRINK_LOG), 0.0)
            level.append(rung)
            now.append(jnp.exp(log_start - rung * SHRINK_LOG))
            slope.append(jnp.zeros(tile, f32))

        def scale_of(level):
            return jnp.where(level == 0.0, 1.0, jnp.where(level == -1.0, SHRINK, 0.0))

        def advance(k, now, slope):
            a = jnp.broadcast_to(coef_a[pl.ds(k, 1), :], tile)
            s = jnp.broadcast_to(coef_s[pl.ds(k, 1), :], tile)
            t = jnp.broadcast_to(coef_t[pl.ds(k, 1), :], tile)
            drop = [a * h for h in gap]
            kept = [t * y for y in slope]
            slope = [y - c * x for x, y, c in zip(now, kept, drop)]
            return [(s - c) * x + y for x, y, c in zip(now, kept, drop)], slope

        odd = parity == 1
        next_now, next_slope = advance(1, now, slope)
        now = [jnp.where(odd, y, x) for x, y in zip(now, next_now)]
        slope = [jnp.where(odd, y, x) for x, y in zip(slope, next_slope)]

        def block(n, carry):
            now, slope, level = carry
            scale = [scale_of(x) for x in level]
            for q in range(pairs):
                j = n * pairs + q
                for (r, t), x, y in zip(spots, now, scale):
                    values[pl.ds(j, 1), r : r + 8, t : t + LANES] = (x * y)[None]
                k = 2 * j + parity + 1
                now, slope = advance(k, now, slope)
                now, slope = advance(k + 1, now, slope)
            large = [(jnp.maximum(jnp.abs(x), jnp.abs(y)) > GROW) & (z < 0.0)
                     for x, y, z in zip(now, slope, level)]
            factor = [jnp.where(x, SHRINK, 1.0) for x in large]
            level = [jnp.where(x, z + 1.0, z) for x, z in zip(large, level)]
            return [x * y for x, y in zip(now, factor)], [x * y for x, y in zip(slope, factor)], level

        state = (now, slope, level)
        copies = []
        for k in range(parts):
            state = lax.fori_loop(k * share // pairs, (k + 1) * share // pairs, block, state)
            here = pl.ds(k * share, share)
            copies.append(pltpu.make_async_copy(values.at[here], values_out.at[here], sems.at[k]))
            copies[k].start()
        for copy in copies:
            copy.wait()

    coefs = pltpu.VMEM((2 * steps + 8, LANES), f32)
    return pl.pallas_call(
        body,
        out_shape=pltpu.HBM((steps, bands, lane_rows), f32),
        in_specs=[SMEM, SMEM, SMEM],
        out_specs=HBM,
        scratch_shapes=[coefs, coefs, coefs, pltpu.VMEM((steps, bands, lane_rows), f32),
                        pltpu.SemaphoreType.DMA((parts,))],
        compiler_params=pltpu.CompilerParams(vmem_limit_bytes=16 << 20),
        cost_estimate=pl.CostEstimate(flops=12 * steps * bands * lane_rows, transcendentals=0,
                                      bytes_accessed=4 * steps * bands * lane_rows),
        name="legendre_values",
    )


def synthesis_kernel(bands, rows, lane_rows, steps, lat, lon):
    parts = 2
    share = steps // parts
    assert share % 16 == 0

    def body(band_ref, sector_ref, waves_ref, love, got, values_in, send, mass, totals, values, sems):
        copies = []
        for k in range(parts):
            here = pl.ds(k * share, share)
            copies.append(pltpu.make_async_copy(values_in.at[here], values.at[here], sems.at[k]))
            copies[k].start()
        order = waves_ref[band_ref[0]]
        parity = sector_ref[0] % 2
        sign = jnp.where(parity == 1, -1.0, 1.0)
        slot = lax.broadcasted_iota(jnp.int32, (1, lane_rows), 1)
        inside = (slot >= 2) & (slot < rows + 2)
        for b in range(bands):
            north = got[b * lon]
            south = got[(lat - 1 - b) * lon]
            for k in range(1, lon):
                north = north + got[b * lon + k]
                south = south + got[(lat - 1 - b) * lon + k]
            row = b * rows + slot - 2
            sine = sine_of(colatitude(jnp.clip(row, 0, GRID_LAT // 2 + 1)))
            weight = (jnp.pi / (2.0 * GRID_LAT)) * sine
            both = jnp.where(inside, (north + sign * south) * weight, 0.0)
            mass[0, b : b + 1, :] = both[0:1]
            mass[1, b : b + 1, :] = both[1:2]
        sub = lax.broadcasted_iota(jnp.int32, (8, LANES), 0)
        tiles = [(r, t) for r in range(0, bands, 8) for t in range(0, lane_rows, LANES)]

        def fold(parts, shift):
            half = len(parts) // 2
            lower = sub % (2 * shift) < shift
            out = []
            for x, y in zip(parts[:half], parts[half:]):
                out.append(jnp.where(lower, y + pltpu.roll(y, 8 - shift, 0), x + pltpu.roll(x, shift, 0)))
            return out

        held = [[mass[c, r : r + 8, t : t + LANES] for r, t in tiles] for c in range(2)] if len(tiles) <= 4 else None

        def weights(c, i):
            r, t = tiles[i]
            return held[c][i] if held else mass[c, r : r + 8, t : t + LANES]

        def analyse(n, carry):
            for group in range(2):
                first = n * 16 + group * 8
                sums = [[], []]
                for q in (7, 6, 5, 4, 3, 2, 1, 0):
                    value = [values[first + q, r : r + 8, t : t + LANES] for r, t in tiles]
                    for c in range(2):
                        acc = None
                        for i, x in enumerate(value):
                            term = weights(c, i) * x
                            acc = term if acc is None else acc + term
                        sums[c].append(acc)
                for c in range(2):
                    found = sums[c]
                    for shift in (4, 2, 1):
                        found = fold(found, shift)
                    totals[c, pl.ds(pl.multiple_of(first, 8), 8), :] = found[0]
            return carry

        for k in range(parts):
            copies[k].wait()
            lax.fori_loop(k * share // 16, (k + 1) * share // 16, analyse, 0)
        degree = order + parity + 2 * lax.broadcasted_iota(jnp.int32, (steps, LANES), 0)
        weight = jnp.where(degree < DEGREES, 1.0 / (2.0 * degree.astype(f32) + 1.0), 0.0)
        for c in range(2):
            totals[c] = jnp.sum(totals[c], axis=1, keepdims=True) * weight

        def synthesise(n, carry):
            carry = list(carry)
            for q in range(8):
                j = n * 8 + q
                weight = love[jnp.minimum(order + parity + 2 * j, DEGREES - 1)]
                factors = [jnp.broadcast_to(totals[c, pl.ds(j, 1), :], (8, LANES)) * weight for c in range(2)]
                for i, (r, t) in enumerate(tiles):
                    value = values[j, r : r + 8, t : t + LANES]
                    for c in range(2):
                        carry[2 * i + c] = carry[2 * i + c] + factors[c] * value
            return tuple(carry)

        zero = jnp.zeros((8, LANES), f32)
        found = lax.fori_loop(0, steps // 8, synthesise, (zero,) * (2 * len(tiles)))
        for b in range(bands):
            for t in range(0, lane_rows, LANES):
                i = tiles.index((b // 8 * 8, t))
                for c in range(2):
                    line = found[2 * i + c][b % 8 : b % 8 + 1, :]
                    for k in range(lon):
                        send[b * lon + k, c : c + 1, t : t + LANES] = line
                        send[(lat - 1 - b) * lon + k, c : c + 1, t : t + LANES] = line

    return pl.pallas_call(
        body,
        out_shape=jax.ShapeDtypeStruct((lat * lon, 2, lane_rows), f32),
        in_specs=[SMEM, SMEM, SMEM, SMEM, VMEM, HBM],
        out_specs=VMEM,
        scratch_shapes=[
            pltpu.VMEM((2, bands, lane_rows), f32),
            pltpu.VMEM((2, steps, LANES), f32),
            pltpu.VMEM((steps, bands, lane_rows), f32),
            pltpu.SemaphoreType.DMA((parts,)),
        ],
        compiler_params=pltpu.CompilerParams(vmem_limit_bytes=16 << 20),
        name="degree_sums",
    )


def step_kernel(rows, cols, width, lat, waves, lane_rows):
    tail = cols % LANES or LANES
    tiles = -(-cols // LANES)
    tall = rows + 32
    top = 16
    own = slice(LANES, LANES + cols)
    meridional = 0.1 * GRID_LAT / GRID_LON
    pieces = 6 if rows % 96 == 0 else 1
    piece = rows // pieces
    names = 6

    def body(band_ref, sector_ref, got, table, low, high, low_side, high_side,
             elev, vel, wind, depth, wet, elev_out, vel_out, load_out,
             elev_v, u_v, v_v, wx_v, wy_v, depth_v, wet_v, surf, flux, load_v,
             left_v, right_v, zonal, sine_v, merid, sems, out_sems):
        band = band_ref[0]
        fields = (
            (elev.at[0], elev_v), (depth, depth_v), (wet, wet_v), (vel.at[0, 0], u_v),
            (vel.at[0, 1], v_v), (wind.at[1], wy_v), (wind.at[0], wx_v),
        )
        copies = []
        for k in range(pieces):
            inside = pl.ds(top + k * piece, piece)
            outside = pl.ds(k * piece, piece)
            copies.append([pltpu.make_async_copy(
                source.at[outside, :], buffer.at[inside, :], sems.at[k, n])
                for n, (source, buffer) in enumerate(fields)])
            for copy in copies[k]:
                copy.start()

        row = lax.broadcasted_iota(jnp.int32, (tall, LANES), 0) - top + band * rows
        row = jnp.clip(row, 0, GRID_LAT - 1)
        sine = sine_of(colatitude(jnp.minimum(row, GRID_LAT - 1 - row)))
        sine_v[...] = sine
        zonal[...] = 0.05 / sine
        merid[...] = meridional / sine

        sign = jnp.where(band < lat // 2, 1.0, -1.0)
        mixed = (got[:, 0] + sign * got[:, 1]).reshape(2 * waves, lane_rows)
        first, second = split(mixed)
        stacked = jnp.concatenate([first, second, first], axis=0)
        line = lax.broadcasted_iota(jnp.int32, (rows + 8, lane_rows), 0)
        line = jnp.where(line < rows, line, jnp.where(line < rows + 2, line - rows - 2, line - 2))
        slot = lax.broadcasted_iota(jnp.int32, (rows + 8, lane_rows), 1)
        target = jnp.where(band < lat // 2, line + 2, rows + 1 - line)
        pick = jnp.where(slot == target, 1.0, 0.0).astype(bf16)
        factors = lax.dot_general(pick, stacked, NT, preferred_element_type=f32).astype(bf16)

        here = slice(top, top + rows)
        for n in range(names):
            left_v[n, here, :] = pltpu.roll(low_side[...], (124 - 4 * n) % LANES, 1)
            right_v[n, here, :] = pltpu.roll(high_side[...], (tail - 4 * n) % LANES, 1)

        elev_v[top - 2 : top, :] = low[0:2, :]
        elev_v[top + rows : top + rows + 2, :] = high[0:2, :]
        for n, buffer in enumerate((u_v, v_v, wy_v, depth_v, wet_v)):
            buffer[top - 1 : top, :] = low[2 + n : 3 + n, :].astype(buffer.dtype)
            buffer[top + rows : top + rows + 1, :] = high[2 + n : 3 + n, :].astype(buffer.dtype)

        group = 4
        after = slice(top + rows, top + rows + 2)
        for t in range(0, width // LANES, group):
            begin = t * LANES
            end = min((t + group) * LANES, width)
            loading = lax.dot_general(
                factors, table[:, begin:end], (((1,), (0,)), ((), ())), preferred_element_type=f32)
            surf[here, begin:end] = loading[0:rows]
            first_lane = max(begin, LANES)
            last_lane = min(end, LANES + cols)
            inner = slice(first_lane - LANES, last_lane - LANES)
            outer = slice(first_lane, last_lane)
            cut = slice(first_lane - begin, last_lane - begin)
            load_v[:, inner] = loading[0:rows, cut]
            surf[top - 2 : top, outer] = elev_v[top - 2 : top, inner] - loading[rows : rows + 2, cut]
            surf[after, outer] = elev_v[after, inner] - loading[rows + 2 : rows + 4, cut]
        load_copy = pltpu.make_async_copy(load_v, load_out.at[0], out_sems.at[0])
        load_copy.start()

        lane8 = lax.broadcasted_iota(jnp.int32, (8, LANES), 1)
        sub8 = lax.broadcasted_iota(jnp.int32, (8, LANES), 0)
        count = width // LANES

        def part(t):
            return slice(t * LANES, (t + 1) * LANES)

        def fetch(t, rows8, n, buffer):
            if t == 0:
                return left_v[n, rows8, :]
            if t <= cols // LANES:
                return buffer[rows8, part(t - 1)].astype(f32)
            if tail == LANES:
                return right_v[n, rows8, :]
            return jnp.concatenate(
                [buffer[rows8, cols - tail : cols].astype(f32), right_v[n, rows8, tail:LANES]], axis=1)

        def keep(buffer, rows8, t, value):
            if 0 < t <= cols // LANES:
                buffer[rows8, part(t - 1)] = value
            elif t and tail < LANES:
                buffer[rows8, cols - tail : cols] = value[:, 0:tail]

        def surfaces(n, carry):
            rows8 = pl.ds(pl.multiple_of(n * 8, 8), 8)
            for t in range(count):
                surf[rows8, part(t)] = fetch(t, rows8, 0, elev_v) - surf[rows8, part(t)]
            return carry

        def vertical(ref, base, at, centre):
            before = jnp.where(sub8 == 7, ref[pl.ds(base - 8, 8), at], centre)
            after = jnp.where(sub8 == 0, ref[pl.ds(base + 8, 8), at], centre)
            return pltpu.roll(after, 7, 0) - pltpu.roll(before, 1, 0)

        def across(behind, centre, ahead):
            ahead = jnp.where(lane8 == 0, ahead, centre)
            behind = jnp.where(lane8 == LANES - 1, behind, centre)
            return pltpu.roll(ahead, LANES - 1, 1) - pltpu.roll(behind, 1, 1)

        def speeds(n):
            base = pl.multiple_of(n * 8, 8)
            rows8 = pl.ds(base, 8)
            zs = zonal[rows8, :]
            sn = sine_v[rows8, :]
            level = [surf[rows8, part(0)], surf[rows8, part(0)]]
            flow = []
            wet_before = None
            for t in range(count + 1):
                if t < count:
                    at = part(t)
                    level.append(surf[rows8, part(t + 1)] if t + 1 < count else level[-1])
                    level.pop(0) if len(level) > 3 else None
                    u = fetch(t, rows8, 1, u_v)
                    v = fetch(t, rows8, 2, v_v)
                    d = fetch(t, rows8, 4, depth_v)
                    wet = fetch(t, rows8, 5, wet_v)
                    drag = wet / (d + 0.1 * jnp.sqrt(u * u + v * v))
                    new_u = drag * (fetch(t, rows8, 3, wx_v) + d * (u - zs * across(*level)))
                    keep(wx_v, rows8, t, new_u)
                    flow.append(d * new_u)
                    if t and not (t > cols // LANES and tail == LANES):
                        if t <= cols // LANES:
                            push = wy_v[rows8, part(t - 1)]
                        else:
                            push = jnp.concatenate(
                                [wy_v[rows8, cols - tail : cols], jnp.zeros((8, LANES - tail), f32)], axis=1)
                        new_v = drag * (push + d * (v - meridional * vertical(surf, base, at, level[1])))
                        keep(wy_v, rows8, t, new_v)
                        flux[rows8, at] = sn * d * new_v
                else:
                    flow.append(flow[-1])
                if len(flow) > 3:
                    flow.pop(0)
                back = t - 1
                if len(flow) == 3 and 0 < back <= tiles:
                    change = wet_before * (zs * across(*flow))
                    if back <= cols // LANES:
                        elev_v[rows8, part(back - 1)] = elev_v[rows8, part(back - 1)] - change
                    else:
                        elev_v[rows8, cols - tail : cols] = elev_v[rows8, cols - tail : cols] - change[:, 0:tail]
                wet_before = wet

        def levels(n):
            base = pl.multiple_of(n * 8, 8)
            rows8 = pl.ds(base, 8)
            ms = merid[rows8, :]
            for t in range(1, tiles + 1):
                change = ms * vertical(flux, base, part(t), flux[rows8, part(t)])
                if t <= cols // LANES:
                    at = part(t - 1)
                else:
                    at = slice(cols - tail, cols)
                    change = change[:, 0:tail]
                elev_v[rows8, at] = elev_v[rows8, at] - wet_v[rows8, at].astype(f32) * change

        def out_copies(k):
            inside = pl.ds(top + k * piece, piece)
            outside = pl.ds(k * piece, piece)
            return (
                pltpu.make_async_copy(wx_v.at[inside, :], vel_out.at[0, 0, outside, :], out_sems.at[1 + k]),
                pltpu.make_async_copy(wy_v.at[inside, :], vel_out.at[0, 1, outside, :], out_sems.at[1 + pieces + k]),
                pltpu.make_async_copy(elev_v.at[inside, :], elev_out.at[0, outside, :], out_sems.at[1 + 2 * pieces + k]),
            )

        def both(n, carry):
            speeds(n + 1)
            levels(n)
            return carry

        def ahead_rows(n, carry):
            speeds(n)
            return carry

        per = piece // 8
        begin = top // 8
        done = begin
        for k in range(pieces):
            for copy in copies[k]:
                copy.wait()
            lax.fori_loop(begin + k * per, begin + (k + 1) * per, surfaces, 0)
            if k == 0:
                lax.fori_loop(begin - 1, begin + 1, ahead_rows, 0)
            stop = begin + (k + 1) * per - (2 if k + 1 < pieces else 0)
            lax.fori_loop(done, stop, both, 0)
            done = stop
            if k:
                for copy in out_copies(k - 1):
                    copy.start()
        for copy in out_copies(pieces - 1):
            copy.start()
        for k in range(pieces):
            for copy in out_copies(k):
                copy.wait()
        load_copy.wait()

    flat = pltpu.VMEM((tall, cols), f32)
    big = pltpu.VMEM((tall, width), f32)
    thin = pltpu.VMEM((tall, LANES), f32)
    return pl.pallas_call(
        body,
        out_shape=(
            jax.ShapeDtypeStruct((1, rows, cols), f32),
            jax.ShapeDtypeStruct((1, 2, rows, cols), f32),
            jax.ShapeDtypeStruct((1, rows, cols), f32),
        ),
        in_specs=[SMEM, SMEM, VMEM, VMEM, VMEM, VMEM, VMEM, VMEM, ANY, ANY, ANY, ANY, ANY],
        out_specs=(ANY, ANY, ANY),
        scratch_shapes=[
            flat, flat, flat, flat, flat, flat, pltpu.VMEM((tall, cols), jnp.int32), big, big,
            pltpu.VMEM((rows, cols), f32),
            pltpu.VMEM((names, tall, LANES), f32),
            pltpu.VMEM((names, tall, LANES), f32),
            thin, thin, thin,
            pltpu.SemaphoreType.DMA((pieces, 7)),
            pltpu.SemaphoreType.DMA((1 + 3 * pieces,)),
        ],
        compiler_params=pltpu.CompilerParams(vmem_limit_bytes=52 << 20),
        name="surge_step",
    )


def local(elevation, velocity, wind_forcing, ocean_depth, wet_mask, love_factor, wavenumbers):
    members, rows, cols = elevation.shape
    lat = lax.axis_size("lat")
    lon = lax.axis_size("lon")
    waves = wavenumbers.shape[0]
    assert members == 1 and waves == lat and lat % 16 == 0 and lon % 2 == 0
    bands = lat // 2
    lane_rows = round_up(rows + 4, LANES)
    width = LANES + round_up(cols + 2, LANES)
    steps = round_up((DEGREES + 1) // 2, 8)
    place = (
        lax.axis_index("lat").astype(jnp.int32)[None],
        lax.axis_index("lon").astype(jnp.int32)[None],
    )

    send, top, bottom, side, table = edge_kernel(rows, cols, width, lat, lon, waves, lane_rows)(
        *place, wavenumbers, elevation, velocity, wind_forcing, ocean_depth, wet_mask)
    got = lax.all_to_all(send, ("lat", "lon"), split_axis=0, concat_axis=0, tiled=True)
    values = legendre_kernel(bands, rows, lane_rows, steps)(*place, wavenumbers)
    values, bottom, top, side = lax.optimization_barrier((values, bottom, top, side))
    up = [(i, (i + 1) % lat) for i in range(lat)]
    down = [(i, (i - 1) % lat) for i in range(lat)]
    low = lax.ppermute(bottom, "lat", up)
    high = lax.ppermute(top, "lat", down)
    low_side = lax.ppermute(side, "lon", [(i, (i + 1) % lon) for i in range(lon)])
    high_side = low_side if lon == 2 else lax.ppermute(
        side, "lon", [(i, (i - 1) % lon) for i in range(lon)])
    send = synthesis_kernel(bands, rows, lane_rows, steps, lat, lon)(
        *place, wavenumbers, love_factor, got, pltpu.with_memory_space_constraint(values, pltpu.HBM))
    got = lax.all_to_all(send, ("lat", "lon"), split_axis=0, concat_axis=0, tiled=True)
    got = got.reshape(lat, lon, 2, lane_rows)[:, :2]
    return step_kernel(rows, cols, width, lat, waves, lane_rows)(
        *place, got, table, low, high, low_side, high_side,
        elevation, velocity, wind_forcing, ocean_depth, wet_mask)


def solution(mesh):
    return jax.shard_map(
        local,
        mesh=mesh,
        in_specs=(
            P(None, "lat", "lon"),
            P(None, None, "lat", "lon"),
            P(None, "lat", "lon"),
            P("lat", "lon"),
            P("lat", "lon"),
            P(),
            P(),
        ),
        out_specs=(P(None, "lat", "lon"), P(None, None, "lat", "lon"), P(None, "lat", "lon")),
        check_vma=False,
    )
```

```python
import math

import jax
import jax.numpy as jnp
from jax import lax
from jax.experimental import pallas as pl
from jax.experimental.pallas import tpu as pltpu
from jax.sharding import PartitionSpec as P


GRID_LAT = 3072
GRID_LON = 8640
DEGREES = 1081
LANES = 128

f32 = jnp.float32
bf16 = jnp.bfloat16
SMEM = pl.BlockSpec(memory_space=pltpu.SMEM)
VMEM = pl.BlockSpec(memory_space=pltpu.VMEM)
ANY = pl.BlockSpec(memory_space=pl.ANY)
HBM = pl.BlockSpec(memory_space=pltpu.HBM)
NT = (((1,), (1,)), ((), ()))
TN = (((0,), (0,)), ((), ()))


def round_up(value, step):
    return -(-value // step) * step


def sine_series(angle, orders=(13, 11, 9, 7, 5, 3, 1)):
    square = angle * angle
    series = None
    for order in orders:
        factor = (-1.0 if (order // 2) % 2 else 1.0) / math.factorial(order)
        series = jnp.full(angle.shape, factor, f32) if series is None else series * square + factor
    return angle * series


def cosine_of_units(units):
    turns = jnp.floor(units * (1.0 / GRID_LON) + 0.5)
    sine = sine_series((units - turns * GRID_LON) * (math.pi / GRID_LON))
    return 1.0 - 2.0 * sine * sine


def colatitude(row):
    return jnp.pi * (row.astype(f32) + 0.5) / GRID_LAT


def sine_of(angle):
    return sine_series(angle, (15, 13, 11, 9, 7, 5, 3, 1))


def split(value):
    high = value.astype(bf16)
    return high, (value - high.astype(f32)).astype(bf16)


def edge_kernel(rows, cols, width, lat, lon, waves, lane_rows):
    tail = cols % LANES or LANES

    def body(band_ref, sector_ref, waves_ref, elev, vel, wind, depth, wet,
             send, top, bottom, side, table, elev_v, wet_v, load_hi, load_lo,
             top_v, bottom_v, left_v, right_v, sems):
        band = band_ref[0]
        sector = sector_ref[0]
        first = pltpu.make_async_copy(elev.at[0], elev_v, sems.at[0])
        second = pltpu.make_async_copy(wet, wet_v, sems.at[1])
        first.start()
        second.start()
        fields = (vel.at[0, 0], vel.at[0, 1], wind.at[1], depth)
        copies = []
        for n, field in enumerate(fields):
            copies.append(pltpu.make_async_copy(field.at[pl.ds(0, 1), :], top_v.at[n], sems.at[2 + n]))
            copies.append(pltpu.make_async_copy(field.at[pl.ds(rows - 1, 1), :], bottom_v.at[n], sems.at[6 + n]))
        fields = (vel.at[0, 0], vel.at[0, 1], wind.at[0], depth)
        for n, field in enumerate(fields):
            copies.append(pltpu.make_async_copy(field.at[:, pl.ds(0, LANES)], left_v.at[n], sems.at[10 + n]))
            copies.append(pltpu.make_async_copy(
                field.at[:, pl.ds(cols - tail, tail)], right_v.at[n], sems.at[14 + n]))
        for copy in copies:
            copy.start()

        wave_row = lax.broadcasted_iota(jnp.int32, (2 * waves, LANES), 0)
        order = jnp.zeros((2 * waves, LANES), f32)
        for n in range(waves):
            order = jnp.where(wave_row // 2 == n, waves_ref[n].astype(f32), order)
        quarter = jnp.where(wave_row % 2 == 1, 0.25 * GRID_LON, 0.0)
        lane = lax.broadcasted_iota(jnp.int32, (2 * waves, LANES), 1)
        for tile in range(width // LANES):
            column = (sector * cols + (tile - 1) * LANES + lane).astype(f32)
            values = cosine_of_units(order * column - quarter)
            high, low = split(values)
            span = slice(tile * LANES, (tile + 1) * LANES)
            table[0 : 2 * waves, span] = high
            table[2 * waves : 4 * waves, span] = high
            table[4 * waves : 6 * waves, span] = low

        first.wait()
        second.wait()
        for start in range(0, rows, 8):
            here = slice(start, start + 8)
            high, low = split(elev_v[here, :] * wet_v[here, :].astype(f32))
            load_hi[here, :] = high
            load_lo[here, :] = low
        own = slice(LANES, LANES + cols)
        main_part = lax.dot_general(
            load_hi[...], table[2 * waves : 6 * waves, own], NT, preferred_element_type=f32)
        rest = lax.dot_general(load_lo[...], table[0 : 2 * waves, own], NT, preferred_element_type=f32)
        sums = (main_part[:, 0 : 2 * waves] + main_part[:, 2 * waves : 4 * waves] + rest) * (1.0 / GRID_LON)
        row = lax.broadcasted_iota(jnp.int32, (rows, lane_rows), 0)
        slot = lax.broadcasted_iota(jnp.int32, (rows, lane_rows), 1) - 2
        target = jnp.where(band < lat // 2, row, rows - 1 - row)
        pick = jnp.where(slot == target, 1.0, 0.0).astype(bf16)
        high, low = split(sums)
        lower = (sums - high.astype(f32) - low.astype(f32)).astype(bf16)
        turned = (
            lax.dot_general(high, pick, TN, preferred_element_type=f32)
            + lax.dot_general(low, pick, TN, preferred_element_type=f32)
            + lax.dot_general(lower, pick, TN, preferred_element_type=f32)
        )
        for n in range(waves):
            block = turned[2 * n : 2 * n + 2, :]
            for k in range(lon):
                send[n * lon + k, :, :] = block

        for copy in copies:
            copy.wait()
        top[0:2, :] = elev_v[0:2, :]
        bottom[0:2, :] = elev_v[rows - 2 : rows, :]
        for n in range(4):
            top[2 + n : 3 + n, :] = top_v[n]
            bottom[2 + n : 3 + n, :] = bottom_v[n]
        top[6:7, :] = wet_v[0:1, :].astype(f32)
        bottom[6:7, :] = wet_v[rows - 1 : rows, :].astype(f32)
        top[7:8, :] = jnp.zeros((1, cols), f32)
        bottom[7:8, :] = jnp.zeros((1, cols), f32)
        blank = jnp.zeros((8, LANES - tail), f32)
        for start in range(0, rows, 8):
            here = slice(start, start + 8)
            lane8 = lax.broadcasted_iota(jnp.int32, (8, LANES), 1)
            left = [elev_v[here, 0:LANES]] + [left_v[n, here, :] for n in range(4)]
            left.append(wet_v[here, 0:LANES].astype(f32))
            right = [elev_v[here, cols - tail : cols]] + [right_v[n, here, :] for n in range(4)]
            right.append(wet_v[here, cols - tail : cols].astype(f32))
            right = [jnp.concatenate([x, blank], axis=1) if tail < LANES else x for x in right]
            packed = jnp.zeros((8, LANES), f32)
            for n in range(6):
                moved = pltpu.roll(left[n], 4 * n, 1) if n else left[n]
                packed = jnp.where(lane8 // 2 == 2 * n, moved, packed)
                moved = pltpu.roll(right[n], (4 * n + 2 - (tail - 2)) % LANES, 1)
                packed = jnp.where(lane8 // 2 == 2 * n + 1, moved, packed)
            side[here, :] = packed

    return pl.pallas_call(
        body,
        out_shape=(
            jax.ShapeDtypeStruct((lat * lon, 2, lane_rows), f32),
            jax.ShapeDtypeStruct((8, cols), f32),
            jax.ShapeDtypeStruct((8, cols), f32),
            jax.ShapeDtypeStruct((rows, LANES), f32),
            jax.ShapeDtypeStruct((6 * waves, width), bf16),
        ),
        in_specs=[SMEM, SMEM, SMEM, ANY, ANY, ANY, ANY, ANY],
        out_specs=(VMEM, VMEM, VMEM, VMEM, VMEM),
        scratch_shapes=[
            pltpu.VMEM((rows, cols), f32),
            pltpu.VMEM((rows, cols), jnp.int32),
            pltpu.VMEM((rows, cols), bf16),
            pltpu.VMEM((rows, cols), bf16),
            pltpu.VMEM((4, 1, cols), f32),
            pltpu.VMEM((4, 1, cols), f32),
            pltpu.VMEM((4, rows, LANES), f32),
            pltpu.VMEM((4, rows, tail), f32),
            pltpu.SemaphoreType.DMA((18,)),
        ],
        name="edge_fourier",
    )


GROW = 2.0**40
SHRINK = 2.0**-96
SHRINK_LOG = 96.0 * math.log(2.0)


def legendre_kernel(bands, rows, lane_rows, steps):
    tile = (8, LANES)
    spots = [(r, t) for r in range(0, bands, 8) for t in range(0, lane_rows, LANES)]
    pairs = 8
    parts = 4
    share = steps // parts

    def body(band_ref, sector_ref, waves_ref, values_out, coef_a, coef_s, coef_t, values, sems):
        order = waves_ref[band_ref[0]]
        parity = sector_ref[0] % 2
        order_real = order.astype(f32)
        count = coef_a.shape[0]
        for start in range(0, count, 8):
            index = (lax.broadcasted_iota(jnp.int32, tile, 0) + start).astype(f32)
            index = jnp.maximum(index, 1.0)
            double = 2.0 * (index + order_real)
            above = index + 2.0 * order_real
            below = double - 1.0
            raising = jnp.sqrt(below * (double + 1.0) / (index * above))
            ratio = raising / below
            coef_a[start : start + 8, :] = raising
            coef_s[start : start + 8, :] = ratio * above
            coef_t[start : start + 8, :] = ratio * (index - 1.0)
        ladder_rows = round_up(DEGREES, 8 * LANES) // LANES
        ladder = (
            lax.broadcasted_iota(jnp.int32, (ladder_rows, LANES), 0) * LANES
            + lax.broadcasted_iota(jnp.int32, (ladder_rows, LANES), 1)
        ).astype(f32)
        used = (ladder >= 2.0) & (ladder <= order_real)
        safe = jnp.maximum(ladder, 1.0)
        total = jnp.sum(jnp.where(used, jnp.log((2.0 * safe + 1.0) / (2.0 * safe)), 0.0))
        total = 0.5 * (total + jnp.where(order > 0, math.log(3.0), 0.0))

        gap, level, now, slope = [], [], [], []
        for r, t in spots:
            row = (
                (lax.broadcasted_iota(jnp.int32, tile, 0) + r) * rows
                + lax.broadcasted_iota(jnp.int32, tile, 1) + (t - 2)
            )
            angle = colatitude(jnp.clip(row, 0, GRID_LAT // 2 + 1))
            half = sine_series(0.5 * angle)
            cosine = 1.0 - 2.0 * half * half
            gap.append(1.0 - cosine)
            log_start = total + order_real * jnp.log(sine_of(angle))
            rung = jnp.minimum(jnp.ceil((log_start - math.log(GROW)) / SHRINK_LOG), 0.0)
            level.append(rung)
            now.append(jnp.exp(log_start - rung * SHRINK_LOG))
            slope.append(jnp.zeros(tile, f32))

        def scale_of(level):
            return jnp.where(level == 0.0, 1.0, jnp.where(level == -1.0, SHRINK, 0.0))

        def advance(k, now, slope):
            a = jnp.broadcast_to(coef_a[pl.ds(k, 1), :], tile)
            s = jnp.broadcast_to(coef_s[pl.ds(k, 1), :], tile)
            t = jnp.broadcast_to(coef_t[pl.ds(k, 1), :], tile)
            drop = [a * h for h in gap]
            kept = [t * y for y in slope]
            slope = [y - c * x for x, y, c in zip(now, kept, drop)]
            return [(s - c) * x + y for x, y, c in zip(now, kept, drop)], slope

        odd = parity == 1
        next_now, next_slope = advance(1, now, slope)
        now = [jnp.where(odd, y, x) for x, y in zip(now, next_now)]
        slope = [jnp.where(odd, y, x) for x, y in zip(slope, next_slope)]

        def block(n, carry):
            now, slope, level = carry
            scale = [scale_of(x) for x in level]
            for q in range(pairs):
                j = n * pairs + q
                for (r, t), x, y in zip(spots, now, scale):
                    values[pl.ds(j, 1), r : r + 8, t : t + LANES] = (x * y)[None]
                k = 2 * j + parity + 1
                now, slope = advance(k, now, slope)
                now, slope = advance(k + 1, now, slope)
            large = [(jnp.maximum(jnp.abs(x), jnp.abs(y)) > GROW) & (z < 0.0)
                     for x, y, z in zip(now, slope, level)]
            factor = [jnp.where(x, SHRINK, 1.0) for x in large]
            level = [jnp.where(x, z + 1.0, z) for x, z in zip(large, level)]
            return [x * y for x, y in zip(now, factor)], [x * y for x, y in zip(slope, factor)], level

        state = (now, slope, level)
        copies = []
        for k in range(parts):
            state = lax.fori_loop(k * share // pairs, (k + 1) * share // pairs, block, state)
            here = pl.ds(k * share, share)
            copies.append(pltpu.make_async_copy(values.at[here], values_out.at[here], sems.at[k]))
            copies[k].start()
        for copy in copies:
            copy.wait()

    coefs = pltpu.VMEM((2 * steps + 8, LANES), f32)
    return pl.pallas_call(
        body,
        out_shape=pltpu.HBM((steps, bands, lane_rows), f32),
        in_specs=[SMEM, SMEM, SMEM],
        out_specs=HBM,
        scratch_shapes=[coefs, coefs, coefs, pltpu.VMEM((steps, bands, lane_rows), f32),
                        pltpu.SemaphoreType.DMA((parts,))],
        compiler_params=pltpu.CompilerParams(vmem_limit_bytes=16 << 20),
        cost_estimate=pl.CostEstimate(flops=12 * steps * bands * lane_rows, transcendentals=0,
                                      bytes_accessed=4 * steps * bands * lane_rows),
        name="legendre_values",
    )


def synthesis_kernel(bands, rows, lane_rows, steps, lat, lon):
    parts = 4
    share = steps // parts

    def body(band_ref, sector_ref, waves_ref, love, got, values_in, send, mass, totals, values, sems):
        copies = []
        for k in range(parts):
            here = pl.ds(k * share, share)
            copies.append(pltpu.make_async_copy(values_in.at[here], values.at[here], sems.at[k]))
            copies[k].start()
        order = waves_ref[band_ref[0]]
        parity = sector_ref[0] % 2
        sign = jnp.where(parity == 1, -1.0, 1.0)
        slot = lax.broadcasted_iota(jnp.int32, (1, lane_rows), 1)
        inside = (slot >= 2) & (slot < rows + 2)
        for b in range(bands):
            north = got[b * lon]
            south = got[(lat - 1 - b) * lon]
            for k in range(1, lon):
                north = north + got[b * lon + k]
                south = south + got[(lat - 1 - b) * lon + k]
            row = b * rows + slot - 2
            sine = sine_of(colatitude(jnp.clip(row, 0, GRID_LAT // 2 + 1)))
            weight = (jnp.pi / (2.0 * GRID_LAT)) * sine
            both = jnp.where(inside, (north + sign * south) * weight, 0.0)
            mass[0, b : b + 1, :] = both[0:1]
            mass[1, b : b + 1, :] = both[1:2]
        sub = lax.broadcasted_iota(jnp.int32, (8, LANES), 0)
        tiles = [(r, t) for r in range(0, bands, 8) for t in range(0, lane_rows, LANES)]

        def fold(parts, shift):
            half = len(parts) // 2
            lower = sub % (2 * shift) < shift
            out = []
            for x, y in zip(parts[:half], parts[half:]):
                out.append(jnp.where(lower, y + pltpu.roll(y, 8 - shift, 0), x + pltpu.roll(x, shift, 0)))
            return out

        def analyse(n, carry):
            for c in range(2):
                parts = []
                for q in (7, 6, 5, 4, 3, 2, 1, 0):
                    acc = None
                    for r, t in tiles:
                        term = mass[c, r : r + 8, t : t + LANES] * values[n * 8 + q, r : r + 8, t : t + LANES]
                        acc = term if acc is None else acc + term
                    parts.append(acc)
                for shift in (4, 2, 1):
                    parts = fold(parts, shift)
                totals[c, pl.ds(n * 8, 8), :] = parts[0]
            return carry

        for k in range(parts):
            copies[k].wait()
            lax.fori_loop(k * share // 8, (k + 1) * share // 8, analyse, 0)
        degree = order + parity + 2 * lax.broadcasted_iota(jnp.int32, (steps, LANES), 0)
        weight = jnp.where(degree < DEGREES, 1.0 / (2.0 * degree.astype(f32) + 1.0), 0.0)
        for c in range(2):
            totals[c] = jnp.sum(totals[c], axis=1, keepdims=True) * weight

        def synthesise(n, carry):
            carry = list(carry)
            for q in range(8):
                j = n * 8 + q
                weight = love[jnp.minimum(order + parity + 2 * j, DEGREES - 1)]
                factors = [jnp.broadcast_to(totals[c, pl.ds(j, 1), :], (8, LANES)) * weight for c in range(2)]
                for i, (r, t) in enumerate(tiles):
                    value = values[j, r : r + 8, t : t + LANES]
                    for c in range(2):
                        carry[2 * i + c] = carry[2 * i + c] + factors[c] * value
            return tuple(carry)

        zero = jnp.zeros((8, LANES), f32)
        found = lax.fori_loop(0, steps // 8, synthesise, (zero,) * (2 * len(tiles)))
        for b in range(bands):
            for t in range(0, lane_rows, LANES):
                i = tiles.index((b // 8 * 8, t))
                for c in range(2):
                    line = found[2 * i + c][b % 8 : b % 8 + 1, :]
                    for k in range(lon):
                        send[b * lon + k, c : c + 1, t : t + LANES] = line
                        send[(lat - 1 - b) * lon + k, c : c + 1, t : t + LANES] = line

    return pl.pallas_call(
        body,
        out_shape=jax.ShapeDtypeStruct((lat * lon, 2, lane_rows), f32),
        in_specs=[SMEM, SMEM, SMEM, SMEM, VMEM, HBM],
        out_specs=VMEM,
        scratch_shapes=[
            pltpu.VMEM((2, bands, lane_rows), f32),
            pltpu.VMEM((2, steps, LANES), f32),
            pltpu.VMEM((steps, bands, lane_rows), f32),
            pltpu.SemaphoreType.DMA((parts,)),
        ],
        compiler_params=pltpu.CompilerParams(vmem_limit_bytes=16 << 20),
        name="degree_sums",
    )


def step_kernel(rows, cols, width, lat, waves, lane_rows):
    tail = cols % LANES or LANES
    tiles = -(-cols // LANES)
    tall = rows + 32
    top = 16
    meridional = 0.1 * GRID_LAT / GRID_LON
    pieces = 6 if rows % 96 == 0 else 1
    piece = rows // pieces
    names = 6

    def body(band_ref, sector_ref, got, table, low, high, low_side, high_side,
             elev, vel, wind, depth, wet, elev_out, vel_out, load_out,
             elev_v, u_v, v_v, wx_v, wy_v, depth_v, wet_v, surf, flux, load_v,
             left_v, right_v, zonal, sine_v, merid, sems, out_sems):
        band = band_ref[0]
        fields = (
            (elev.at[0], elev_v), (depth, depth_v), (wet, wet_v), (vel.at[0, 0], u_v),
            (vel.at[0, 1], v_v), (wind.at[1], wy_v), (wind.at[0], wx_v),
        )
        copies = []
        for k in range(pieces):
            inside = pl.ds(top + k * piece, piece)
            outside = pl.ds(k * piece, piece)
            copies.append([pltpu.make_async_copy(
                source.at[outside, :], buffer.at[inside, :], sems.at[k, n])
                for n, (source, buffer) in enumerate(fields)])
            for copy in copies[k]:
                copy.start()

        row = lax.broadcasted_iota(jnp.int32, (tall, LANES), 0) - top + band * rows
        row = jnp.clip(row, 0, GRID_LAT - 1)
        sine = sine_of(colatitude(jnp.minimum(row, GRID_LAT - 1 - row)))
        sine_v[...] = sine
        zonal[...] = 0.05 / sine
        merid[...] = meridional / sine

        sign = jnp.where(band < lat // 2, 1.0, -1.0)
        mixed = (got[:, 0] + sign * got[:, 1]).reshape(2 * waves, lane_rows)
        first, second = split(mixed)
        stacked = jnp.concatenate([first, second, first], axis=0)
        line = lax.broadcasted_iota(jnp.int32, (rows + 8, lane_rows), 0)
        line = jnp.where(line < rows, line, jnp.where(line < rows + 2, line - rows - 2, line - 2))
        slot = lax.broadcasted_iota(jnp.int32, (rows + 8, lane_rows), 1)
        target = jnp.where(band < lat // 2, line + 2, rows + 1 - line)
        pick = jnp.where(slot == target, 1.0, 0.0).astype(bf16)
        factors = lax.dot_general(pick, stacked, NT, preferred_element_type=f32).astype(bf16)

        here = slice(top, top + rows)
        for n in range(names):
            left_v[n, here, :] = pltpu.roll(low_side[...], (124 - 4 * n) % LANES, 1)
            right_v[n, here, :] = pltpu.roll(high_side[...], (tail - 4 * n) % LANES, 1)

        elev_v[top - 2 : top, :] = low[0:2, :]
        elev_v[top + rows : top + rows + 2, :] = high[0:2, :]
        for n, buffer in enumerate((u_v, v_v, wy_v, depth_v, wet_v)):
            buffer[top - 1 : top, :] = low[2 + n : 3 + n, :].astype(buffer.dtype)
            buffer[top + rows : top + rows + 1, :] = high[2 + n : 3 + n, :].astype(buffer.dtype)

        group = 4
        after = slice(top + rows, top + rows + 2)
        for t in range(0, width // LANES, group):
            begin = t * LANES
            end = min((t + group) * LANES, width)
            loading = lax.dot_general(
                factors, table[:, begin:end], (((1,), (0,)), ((), ())), preferred_element_type=f32)
            surf[here, begin:end] = loading[0:rows]
            first_lane = max(begin, LANES)
            last_lane = min(end, LANES + cols)
            inner = slice(first_lane - LANES, last_lane - LANES)
            outer = slice(first_lane, last_lane)
            cut = slice(first_lane - begin, last_lane - begin)
            load_v[:, inner] = loading[0:rows, cut]
            surf[top - 2 : top, outer] = elev_v[top - 2 : top, inner] - loading[rows : rows + 2, cut]
            surf[after, outer] = elev_v[after, inner] - loading[rows + 2 : rows + 4, cut]
        load_copy = pltpu.make_async_copy(load_v, load_out.at[0], out_sems.at[0])
        load_copy.start()

        lane8 = lax.broadcasted_iota(jnp.int32, (8, LANES), 1)
        sub8 = lax.broadcasted_iota(jnp.int32, (8, LANES), 0)
        count = width // LANES

        def part(t):
            return slice(t * LANES, (t + 1) * LANES)

        def fetch(t, rows8, n, buffer):
            if t == 0:
                return left_v[n, rows8, :]
            if t <= cols // LANES:
                return buffer[rows8, part(t - 1)].astype(f32)
            if tail == LANES:
                return right_v[n, rows8, :]
            return jnp.concatenate(
                [buffer[rows8, cols - tail : cols].astype(f32), right_v[n, rows8, tail:LANES]], axis=1)

        def keep(buffer, rows8, t, value):
            if 0 < t <= cols // LANES:
                buffer[rows8, part(t - 1)] = value
            elif t and tail < LANES:
                buffer[rows8, cols - tail : cols] = value[:, 0:tail]

        def surfaces(n, carry):
            rows8 = pl.ds(pl.multiple_of(n * 8, 8), 8)
            for t in range(count):
                surf[rows8, part(t)] = fetch(t, rows8, 0, elev_v) - surf[rows8, part(t)]
            return carry

        def vertical(ref, base, at, centre):
            before = jnp.where(sub8 == 7, ref[pl.ds(base - 8, 8), at], centre)
            after = jnp.where(sub8 == 0, ref[pl.ds(base + 8, 8), at], centre)
            return pltpu.roll(after, 7, 0) - pltpu.roll(before, 1, 0)

        def across(behind, centre, ahead):
            ahead = jnp.where(lane8 == 0, ahead, centre)
            behind = jnp.where(lane8 == LANES - 1, behind, centre)
            return pltpu.roll(ahead, LANES - 1, 1) - pltpu.roll(behind, 1, 1)

        def speeds(n):
            base = pl.multiple_of(n * 8, 8)
            rows8 = pl.ds(base, 8)
            zs = zonal[rows8, :]
            sn = sine_v[rows8, :]
            level = [surf[rows8, part(0)], surf[rows8, part(0)]]
            flow = []
            wet_before = None
            for t in range(count + 1):
                if t < count:
                    at = part(t)
                    level.append(surf[rows8, part(t + 1)] if t + 1 < count else level[-1])
                    level.pop(0) if len(level) > 3 else None
                    u = fetch(t, rows8, 1, u_v)
                    v = fetch(t, rows8, 2, v_v)
                    d = fetch(t, rows8, 4, depth_v)
                    wet = fetch(t, rows8, 5, wet_v)
                    drag = wet / (d + 0.1 * jnp.sqrt(u * u + v * v))
                    new_u = drag * (u * d + fetch(t, rows8, 3, wx_v) - (zs * d) * across(*level))
                    keep(wx_v, rows8, t, new_u)
                    flow.append(d * new_u)
                    if t and not (t > cols // LANES and tail == LANES):
                        if t <= cols // LANES:
                            push = wy_v[rows8, part(t - 1)]
                        else:
                            push = jnp.concatenate(
                                [wy_v[rows8, cols - tail : cols], jnp.zeros((8, LANES - tail), f32)], axis=1)
                        new_v = drag * (v * d + push - (meridional * d) * vertical(surf, base, at, level[1]))
                        keep(wy_v, rows8, t, new_v)
                        flux[rows8, at] = sn * d * new_v
                else:
                    flow.append(flow[-1])
                if len(flow) > 3:
                    flow.pop(0)
                back = t - 1
                if len(flow) == 3 and 0 < back <= tiles:
                    change = wet_before * (zs * across(*flow))
                    if back <= cols // LANES:
                        elev_v[rows8, part(back - 1)] = elev_v[rows8, part(back - 1)] - change
                    else:
                        elev_v[rows8, cols - tail : cols] = elev_v[rows8, cols - tail : cols] - change[:, 0:tail]
                wet_before = wet

        def levels(n):
            base = pl.multiple_of(n * 8, 8)
            rows8 = pl.ds(base, 8)
            ms = merid[rows8, :]
            for t in range(1, tiles + 1):
                change = ms * vertical(flux, base, part(t), flux[rows8, part(t)])
                if t <= cols // LANES:
                    at = part(t - 1)
                else:
                    at = slice(cols - tail, cols)
                    change = change[:, 0:tail]
                elev_v[rows8, at] = elev_v[rows8, at] - wet_v[rows8, at].astype(f32) * change

        def out_copies(k):
            inside = pl.ds(top + k * piece, piece)
            outside = pl.ds(k * piece, piece)
            return (
                pltpu.make_async_copy(wx_v.at[inside, :], vel_out.at[0, 0, outside, :], out_sems.at[1 + k]),
                pltpu.make_async_copy(wy_v.at[inside, :], vel_out.at[0, 1, outside, :], out_sems.at[1 + pieces + k]),
                pltpu.make_async_copy(elev_v.at[inside, :], elev_out.at[0, outside, :], out_sems.at[1 + 2 * pieces + k]),
            )

        def both(n, carry):
            speeds(n + 1)
            levels(n)
            return carry

        def ahead_rows(n, carry):
            speeds(n)
            return carry

        per = piece // 8
        begin = top // 8
        done = begin
        for k in range(pieces):
            for copy in copies[k]:
                copy.wait()
            lax.fori_loop(begin + k * per, begin + (k + 1) * per, surfaces, 0)
            if k == 0:
                lax.fori_loop(begin - 1, begin + 1, ahead_rows, 0)
            stop = begin + (k + 1) * per - (2 if k + 1 < pieces else 0)
            lax.fori_loop(done, stop, both, 0)
            done = stop
            if k:
                for copy in out_copies(k - 1):
                    copy.start()
        for copy in out_copies(pieces - 1):
            copy.start()
        for k in range(pieces):
            for copy in out_copies(k):
                copy.wait()
        load_copy.wait()

    flat = pltpu.VMEM((tall, cols), f32)
    big = pltpu.VMEM((tall, width), f32)
    thin = pltpu.VMEM((tall, LANES), f32)
    return pl.pallas_call(
        body,
        out_shape=(
            jax.ShapeDtypeStruct((1, rows, cols), f32),
            jax.ShapeDtypeStruct((1, 2, rows, cols), f32),
            jax.ShapeDtypeStruct((1, rows, cols), f32),
        ),
        in_specs=[SMEM, SMEM, VMEM, VMEM, VMEM, VMEM, VMEM, VMEM, ANY, ANY, ANY, ANY, ANY],
        out_specs=(ANY, ANY, ANY),
        scratch_shapes=[
            flat, flat, flat, flat, flat, flat, pltpu.VMEM((tall, cols), jnp.int32), big, big,
            pltpu.VMEM((rows, cols), f32),
            pltpu.VMEM((names, tall, LANES), f32),
            pltpu.VMEM((names, tall, LANES), f32),
            thin, thin, thin,
            pltpu.SemaphoreType.DMA((pieces, 7)),
            pltpu.SemaphoreType.DMA((1 + 3 * pieces,)),
        ],
        compiler_params=pltpu.CompilerParams(vmem_limit_bytes=52 << 20),
        name="surge_step",
    )


def local(elevation, velocity, wind_forcing, ocean_depth, wet_mask, love_factor, wavenumbers):
    members, rows, cols = elevation.shape
    lat = lax.axis_size("lat")
    lon = lax.axis_size("lon")
    waves = wavenumbers.shape[0]
    assert members == 1 and waves == lat and lat % 16 == 0 and lon % 2 == 0
    bands = lat // 2
    lane_rows = round_up(rows + 4, LANES)
    width = LANES + round_up(cols + 2, LANES)
    steps = round_up((DEGREES + 1) // 2, 8)
    place = (
        lax.axis_index("lat").astype(jnp.int32)[None],
        lax.axis_index("lon").astype(jnp.int32)[None],
    )

    send, top, bottom, side, table = edge_kernel(rows, cols, width, lat, lon, waves, lane_rows)(
        *place, wavenumbers, elevation, velocity, wind_forcing, ocean_depth, wet_mask)
    got = lax.all_to_all(send, ("lat", "lon"), split_axis=0, concat_axis=0, tiled=True)
    values = legendre_kernel(bands, rows, lane_rows, steps)(*place, wavenumbers)
    values, bottom = lax.optimization_barrier((values, bottom))
    low = lax.ppermute(bottom, "lat", [(i, (i + 1) % lat) for i in range(lat)])
    send = synthesis_kernel(bands, rows, lane_rows, steps, lat, lon)(
        *place, wavenumbers, love_factor, got, pltpu.with_memory_space_constraint(values, pltpu.HBM))
    send, top, side = lax.optimization_barrier((send, top, side))
    got = lax.all_to_all(send, ("lat", "lon"), split_axis=0, concat_axis=0, tiled=True)
    high = lax.ppermute(top, "lat", [(i, (i - 1) % lat) for i in range(lat)])
    low_side = lax.ppermute(side, "lon", [(i, (i + 1) % lon) for i in range(lon)])
    high_side = low_side if lon == 2 else lax.ppermute(
        side, "lon", [(i, (i - 1) % lon) for i in range(lon)])
    got = got.reshape(lat, lon, 2, lane_rows)[:, :2]
    return step_kernel(rows, cols, width, lat, waves, lane_rows)(
        *place, got, table, low, high, low_side, high_side,
        elevation, velocity, wind_forcing, ocean_depth, wet_mask)


def solution(mesh):
    return jax.shard_map(
        local,
        mesh=mesh,
        in_specs=(
            P(None, "lat", "lon"),
            P(None, None, "lat", "lon"),
            P(None, "lat", "lon"),
            P("lat", "lon"),
            P("lat", "lon"),
            P(),
            P(),
        ),
        out_specs=(P(None, "lat", "lon"), P(None, None, "lat", "lon"), P(None, "lat", "lon")),
        check_vma=False,
    )
```

```python
import math

import jax
import jax.numpy as jnp
from jax import lax
from jax.experimental import pallas as pl
from jax.experimental.pallas import tpu as pltpu
from jax.sharding import PartitionSpec as P


GRID_LAT = 3072
GRID_LON = 8640
DEGREES = 1081
LANES = 128

f32 = jnp.float32
bf16 = jnp.bfloat16
SMEM = pl.BlockSpec(memory_space=pltpu.SMEM)
VMEM = pl.BlockSpec(memory_space=pltpu.VMEM)
ANY = pl.BlockSpec(memory_space=pl.ANY)
HBM = pl.BlockSpec(memory_space=pltpu.HBM)
NT = (((1,), (1,)), ((), ()))
TN = (((0,), (0,)), ((), ()))


def round_up(value, step):
    return -(-value // step) * step


def sine_series(angle, orders=(13, 11, 9, 7, 5, 3, 1)):
    square = angle * angle
    series = None
    for order in orders:
        factor = (-1.0 if (order // 2) % 2 else 1.0) / math.factorial(order)
        series = jnp.full(angle.shape, factor, f32) if series is None else series * square + factor
    return angle * series


def cosine_of_units(units):
    turns = jnp.floor(units * (1.0 / GRID_LON) + 0.5)
    sine = sine_series((units - turns * GRID_LON) * (math.pi / GRID_LON))
    return 1.0 - 2.0 * sine * sine


def colatitude(row):
    return jnp.pi * (row.astype(f32) + 0.5) / GRID_LAT


def sine_of(angle):
    return sine_series(angle, (15, 13, 11, 9, 7, 5, 3, 1))


def split(value):
    high = value.astype(bf16)
    return high, (value - high.astype(f32)).astype(bf16)


def edge_kernel(rows, cols, width, lat, lon, waves, lane_rows):
    tail = cols % LANES or LANES

    def body(band_ref, sector_ref, waves_ref, elev, vel, wind, depth, wet,
             send, top, bottom, side, table, elev_v, wet_v, load_hi, load_lo,
             top_v, bottom_v, left_v, right_v, sems):
        band = band_ref[0]
        sector = sector_ref[0]
        first = pltpu.make_async_copy(elev.at[0], elev_v, sems.at[0])
        second = pltpu.make_async_copy(wet, wet_v, sems.at[1])
        first.start()
        second.start()
        fields = (vel.at[0, 0], vel.at[0, 1], wind.at[1], depth)
        copies = []
        for n, field in enumerate(fields):
            copies.append(pltpu.make_async_copy(field.at[pl.ds(0, 1), :], top_v.at[n], sems.at[2 + n]))
            copies.append(pltpu.make_async_copy(field.at[pl.ds(rows - 1, 1), :], bottom_v.at[n], sems.at[6 + n]))
        fields = (vel.at[0, 0], vel.at[0, 1], wind.at[0], depth)
        for n, field in enumerate(fields):
            copies.append(pltpu.make_async_copy(field.at[:, pl.ds(0, LANES)], left_v.at[n], sems.at[10 + n]))
            copies.append(pltpu.make_async_copy(
                field.at[:, pl.ds(cols - tail, tail)], right_v.at[n], sems.at[14 + n]))
        for copy in copies:
            copy.start()

        wave_row = lax.broadcasted_iota(jnp.int32, (2 * waves, LANES), 0)
        order = jnp.zeros((2 * waves, LANES), f32)
        for n in range(waves):
            order = jnp.where(wave_row // 2 == n, waves_ref[n].astype(f32), order)
        quarter = jnp.where(wave_row % 2 == 1, 0.25 * GRID_LON, 0.0)
        lane = lax.broadcasted_iota(jnp.int32, (2 * waves, LANES), 1)
        for tile in range(width // LANES):
            column = (sector * cols + (tile - 1) * LANES + lane).astype(f32)
            values = cosine_of_units(order * column - quarter)
            high, low = split(values)
            span = slice(tile * LANES, (tile + 1) * LANES)
            table[0 : 2 * waves, span] = high
            table[2 * waves : 4 * waves, span] = high
            table[4 * waves : 6 * waves, span] = low

        first.wait()
        second.wait()
        for start in range(0, rows, 8):
            here = slice(start, start + 8)
            high, low = split(elev_v[here, :] * wet_v[here, :].astype(f32))
            load_hi[here, :] = high
            load_lo[here, :] = low
        own = slice(LANES, LANES + cols)
        main_part = lax.dot_general(
            load_hi[...], table[2 * waves : 6 * waves, own], NT, preferred_element_type=f32)
        rest = lax.dot_general(load_lo[...], table[0 : 2 * waves, own], NT, preferred_element_type=f32)
        sums = (main_part[:, 0 : 2 * waves] + main_part[:, 2 * waves : 4 * waves] + rest) * (1.0 / GRID_LON)
        row = lax.broadcasted_iota(jnp.int32, (rows, lane_rows), 0)
        slot = lax.broadcasted_iota(jnp.int32, (rows, lane_rows), 1) - 2
        target = jnp.where(band < lat // 2, row, rows - 1 - row)
        pick = jnp.where(slot == target, 1.0, 0.0).astype(bf16)
        high, low = split(sums)
        lower = (sums - high.astype(f32) - low.astype(f32)).astype(bf16)
        turned = (
            lax.dot_general(high, pick, TN, preferred_element_type=f32)
            + lax.dot_general(low, pick, TN, preferred_element_type=f32)
            + lax.dot_general(lower, pick, TN, preferred_element_type=f32)
        )
        for n in range(waves):
            block = turned[2 * n : 2 * n + 2, :]
            for k in range(lon):
                send[n * lon + k, :, :] = block

        for copy in copies:
            copy.wait()
        top[0:2, :] = elev_v[0:2, :]
        bottom[0:2, :] = elev_v[rows - 2 : rows, :]
        for n in range(4):
            top[2 + n : 3 + n, :] = top_v[n]
            bottom[2 + n : 3 + n, :] = bottom_v[n]
        top[6:7, :] = wet_v[0:1, :].astype(f32)
        bottom[6:7, :] = wet_v[rows - 1 : rows, :].astype(f32)
        top[7:8, :] = jnp.zeros((1, cols), f32)
        bottom[7:8, :] = jnp.zeros((1, cols), f32)
        blank = jnp.zeros((8, LANES - tail), f32)
        for start in range(0, rows, 8):
            here = slice(start, start + 8)
            lane8 = lax.broadcasted_iota(jnp.int32, (8, LANES), 1)
            left = [elev_v[here, 0:LANES]] + [left_v[n, here, :] for n in range(4)]
            left.append(wet_v[here, 0:LANES].astype(f32))
            right = [elev_v[here, cols - tail : cols]] + [right_v[n, here, :] for n in range(4)]
            right.append(wet_v[here, cols - tail : cols].astype(f32))
            right = [jnp.concatenate([x, blank], axis=1) if tail < LANES else x for x in right]
            packed = jnp.zeros((8, LANES), f32)
            for n in range(6):
                moved = pltpu.roll(left[n], 4 * n, 1) if n else left[n]
                packed = jnp.where(lane8 // 2 == 2 * n, moved, packed)
                moved = pltpu.roll(right[n], (4 * n + 2 - (tail - 2)) % LANES, 1)
                packed = jnp.where(lane8 // 2 == 2 * n + 1, moved, packed)
            side[here, :] = packed

    return pl.pallas_call(
        body,
        out_shape=(
            jax.ShapeDtypeStruct((lat * lon, 2, lane_rows), f32),
            jax.ShapeDtypeStruct((8, cols), f32),
            jax.ShapeDtypeStruct((8, cols), f32),
            jax.ShapeDtypeStruct((rows, LANES), f32),
            jax.ShapeDtypeStruct((6 * waves, width), bf16),
        ),
        in_specs=[SMEM, SMEM, SMEM, ANY, ANY, ANY, ANY, ANY],
        out_specs=(VMEM, VMEM, VMEM, VMEM, VMEM),
        scratch_shapes=[
            pltpu.VMEM((rows, cols), f32),
            pltpu.VMEM((rows, cols), jnp.int32),
            pltpu.VMEM((rows, cols), bf16),
            pltpu.VMEM((rows, cols), bf16),
            pltpu.VMEM((4, 1, cols), f32),
            pltpu.VMEM((4, 1, cols), f32),
            pltpu.VMEM((4, rows, LANES), f32),
            pltpu.VMEM((4, rows, tail), f32),
            pltpu.SemaphoreType.DMA((18,)),
        ],
        name="edge_fourier",
    )


GROW = 2.0**40
SHRINK = 2.0**-96
SHRINK_LOG = 96.0 * math.log(2.0)


def legendre_kernel(bands, rows, lane_rows, steps):
    tile = (8, LANES)
    spots = [(r, t) for r in range(0, bands, 8) for t in range(0, lane_rows, LANES)]
    pairs = 8
    parts = 4
    share = steps // parts

    def body(band_ref, sector_ref, waves_ref, values_out, coef_a, coef_s, coef_t, values, sems):
        order = waves_ref[band_ref[0]]
        parity = sector_ref[0] % 2
        order_real = order.astype(f32)
        count = coef_a.shape[0]
        for start in range(0, count, 8):
            index = (lax.broadcasted_iota(jnp.int32, tile, 0) + start).astype(f32)
            index = jnp.maximum(index, 1.0)
            double = 2.0 * (index + order_real)
            above = index + 2.0 * order_real
            below = double - 1.0
            raising = jnp.sqrt(below * (double + 1.0) / (index * above))
            ratio = raising / below
            coef_a[start : start + 8, :] = raising
            coef_s[start : start + 8, :] = ratio * above
            coef_t[start : start + 8, :] = ratio * (index - 1.0)
        ladder_rows = round_up(DEGREES, 8 * LANES) // LANES
        ladder = (
            lax.broadcasted_iota(jnp.int32, (ladder_rows, LANES), 0) * LANES
            + lax.broadcasted_iota(jnp.int32, (ladder_rows, LANES), 1)
        ).astype(f32)
        used = (ladder >= 2.0) & (ladder <= order_real)
        safe = jnp.maximum(ladder, 1.0)
        total = jnp.sum(jnp.where(used, jnp.log((2.0 * safe + 1.0) / (2.0 * safe)), 0.0))
        total = 0.5 * (total + jnp.where(order > 0, math.log(3.0), 0.0))

        gap, level, now, slope = [], [], [], []
        for r, t in spots:
            row = (
                (lax.broadcasted_iota(jnp.int32, tile, 0) + r) * rows
                + lax.broadcasted_iota(jnp.int32, tile, 1) + (t - 2)
            )
            angle = colatitude(jnp.clip(row, 0, GRID_LAT // 2 + 1))
            half = sine_series(0.5 * angle)
            cosine = 1.0 - 2.0 * half * half
            gap.append(1.0 - cosine)
            log_start = total + order_real * jnp.log(sine_of(angle))
            rung = jnp.minimum(jnp.ceil((log_start - math.log(GROW)) / SHRINK_LOG), 0.0)
            level.append(rung)
            now.append(jnp.exp(log_start - rung * SHRINK_LOG))
            slope.append(jnp.zeros(tile, f32))

        def scale_of(level):
            return jnp.where(level == 0.0, 1.0, jnp.where(level == -1.0, SHRINK, 0.0))

        def advance(k, now, slope):
            a = jnp.broadcast_to(coef_a[pl.ds(k, 1), :], tile)
            s = jnp.broadcast_to(coef_s[pl.ds(k, 1), :], tile)
            t = jnp.broadcast_to(coef_t[pl.ds(k, 1), :], tile)
            drop = [a * h for h in gap]
            kept = [t * y for y in slope]
            slope = [y - c * x for x, y, c in zip(now, kept, drop)]
            return [(s - c) * x + y for x, y, c in zip(now, kept, drop)], slope

        odd = parity == 1
        next_now, next_slope = advance(1, now, slope)
        now = [jnp.where(odd, y, x) for x, y in zip(now, next_now)]
        slope = [jnp.where(odd, y, x) for x, y in zip(slope, next_slope)]

        def block(n, carry):
            now, slope, level = carry
            scale = [scale_of(x) for x in level]
            for q in range(pairs):
                j = n * pairs + q
                for (r, t), x, y in zip(spots, now, scale):
                    values[pl.ds(j, 1), r : r + 8, t : t + LANES] = (x * y)[None]
                k = 2 * j + parity + 1
                now, slope = advance(k, now, slope)
                now, slope = advance(k + 1, now, slope)
            large = [(jnp.maximum(jnp.abs(x), jnp.abs(y)) > GROW) & (z < 0.0)
                     for x, y, z in zip(now, slope, level)]
            factor = [jnp.where(x, SHRINK, 1.0) for x in large]
            level = [jnp.where(x, z + 1.0, z) for x, z in zip(large, level)]
            return [x * y for x, y in zip(now, factor)], [x * y for x, y in zip(slope, factor)], level

        state = (now, slope, level)
        copies = []
        for k in range(parts):
            state = lax.fori_loop(k * share // pairs, (k + 1) * share // pairs, block, state)
            here = pl.ds(k * share, share)
            copies.append(pltpu.make_async_copy(values.at[here], values_out.at[here], sems.at[k]))
            copies[k].start()
        for copy in copies:
            copy.wait()

    coefs = pltpu.VMEM((2 * steps + 8, LANES), f32)
    return pl.pallas_call(
        body,
        out_shape=pltpu.HBM((steps, bands, lane_rows), f32),
        in_specs=[SMEM, SMEM, SMEM],
        out_specs=HBM,
        scratch_shapes=[coefs, coefs, coefs, pltpu.VMEM((steps, bands, lane_rows), f32),
                        pltpu.SemaphoreType.DMA((parts,))],
        compiler_params=pltpu.CompilerParams(vmem_limit_bytes=16 << 20),
        cost_estimate=pl.CostEstimate(flops=12 * steps * bands * lane_rows, transcendentals=0,
                                      bytes_accessed=4 * steps * bands * lane_rows),
        name="legendre_values",
    )


def synthesis_kernel(bands, rows, lane_rows, steps, lat, lon):
    parts = 4
    share = steps // parts

    def body(band_ref, sector_ref, waves_ref, love, got, values_in, send, mass, totals, values, sems):
        copies = []
        for k in range(parts):
            here = pl.ds(k * share, share)
            copies.append(pltpu.make_async_copy(values_in.at[here], values.at[here], sems.at[k]))
            copies[k].start()
        order = waves_ref[band_ref[0]]
        parity = sector_ref[0] % 2
        sign = jnp.where(parity == 1, -1.0, 1.0)
        slot = lax.broadcasted_iota(jnp.int32, (1, lane_rows), 1)
        inside = (slot >= 2) & (slot < rows + 2)
        for b in range(bands):
            north = got[b * lon]
            south = got[(lat - 1 - b) * lon]
            for k in range(1, lon):
                north = north + got[b * lon + k]
                south = south + got[(lat - 1 - b) * lon + k]
            row = b * rows + slot - 2
            sine = sine_of(colatitude(jnp.clip(row, 0, GRID_LAT // 2 + 1)))
            weight = (jnp.pi / (2.0 * GRID_LAT)) * sine
            both = jnp.where(inside, (north + sign * south) * weight, 0.0)
            mass[0, b : b + 1, :] = both[0:1]
            mass[1, b : b + 1, :] = both[1:2]
        sub = lax.broadcasted_iota(jnp.int32, (8, LANES), 0)
        tiles = [(r, t) for r in range(0, bands, 8) for t in range(0, lane_rows, LANES)]

        def fold(parts, shift):
            half = len(parts) // 2
            lower = sub % (2 * shift) < shift
            out = []
            for x, y in zip(parts[:half], parts[half:]):
                out.append(jnp.where(lower, y + pltpu.roll(y, 8 - shift, 0), x + pltpu.roll(x, shift, 0)))
            return out

        def analyse(n, carry):
            for c in range(2):
                parts = []
                for q in (7, 6, 5, 4, 3, 2, 1, 0):
                    acc = None
                    for r, t in tiles:
                        term = mass[c, r : r + 8, t : t + LANES] * values[n * 8 + q, r : r + 8, t : t + LANES]
                        acc = term if acc is None else acc + term
                    parts.append(acc)
                for shift in (4, 2, 1):
                    parts = fold(parts, shift)
                totals[c, pl.ds(n * 8, 8), :] = parts[0]
            return carry

        for k in range(parts):
            copies[k].wait()
            lax.fori_loop(k * share // 8, (k + 1) * share // 8, analyse, 0)
        degree = order + parity + 2 * lax.broadcasted_iota(jnp.int32, (steps, LANES), 0)
        weight = jnp.where(degree < DEGREES, 1.0 / (2.0 * degree.astype(f32) + 1.0), 0.0)
        for c in range(2):
            totals[c] = jnp.sum(totals[c], axis=1, keepdims=True) * weight

        def synthesise(n, carry):
            carry = list(carry)
            for q in range(8):
                j = n * 8 + q
                weight = love[jnp.minimum(order + parity + 2 * j, DEGREES - 1)]
                factors = [jnp.broadcast_to(totals[c, pl.ds(j, 1), :], (8, LANES)) * weight for c in range(2)]
                for i, (r, t) in enumerate(tiles):
                    value = values[j, r : r + 8, t : t + LANES]
                    for c in range(2):
                        carry[2 * i + c] = carry[2 * i + c] + factors[c] * value
            return tuple(carry)

        zero = jnp.zeros((8, LANES), f32)
        found = lax.fori_loop(0, steps // 8, synthesise, (zero,) * (2 * len(tiles)))
        for b in range(bands):
            for t in range(0, lane_rows, LANES):
                i = tiles.index((b // 8 * 8, t))
                for c in range(2):
                    line = found[2 * i + c][b % 8 : b % 8 + 1, :]
                    for k in range(lon):
                        send[b * lon + k, c : c + 1, t : t + LANES] = line
                        send[(lat - 1 - b) * lon + k, c : c + 1, t : t + LANES] = line

    return pl.pallas_call(
        body,
        out_shape=jax.ShapeDtypeStruct((lat * lon, 2, lane_rows), f32),
        in_specs=[SMEM, SMEM, SMEM, SMEM, VMEM, HBM],
        out_specs=VMEM,
        scratch_shapes=[
            pltpu.VMEM((2, bands, lane_rows), f32),
            pltpu.VMEM((2, steps, LANES), f32),
            pltpu.VMEM((steps, bands, lane_rows), f32),
            pltpu.SemaphoreType.DMA((parts,)),
        ],
        compiler_params=pltpu.CompilerParams(vmem_limit_bytes=16 << 20),
        name="degree_sums",
    )


def step_kernel(rows, cols, width, lat, waves, lane_rows):
    tail = cols % LANES or LANES
    tiles = -(-cols // LANES)
    tall = rows + 32
    top = 16
    meridional = 0.1 * GRID_LAT / GRID_LON
    pieces = 6 if rows % 96 == 0 else 1
    piece = rows // pieces
    names = 6

    def body(band_ref, sector_ref, got, table, low, high, low_side, high_side,
             elev, vel, wind, depth, wet, elev_out, vel_out, load_out,
             elev_v, u_v, v_v, wx_v, wy_v, depth_v, wet_v, surf, flux, load_v,
             left_v, right_v, zonal, sine_v, merid, sems, out_sems):
        band = band_ref[0]
        fields = (
            (elev.at[0], elev_v), (depth, depth_v), (wet, wet_v), (vel.at[0, 0], u_v),
            (vel.at[0, 1], v_v), (wind.at[1], wy_v), (wind.at[0], wx_v),
        )
        copies = []
        for k in range(pieces):
            inside = pl.ds(top + k * piece, piece)
            outside = pl.ds(k * piece, piece)
            copies.append([pltpu.make_async_copy(
                source.at[outside, :], buffer.at[inside, :], sems.at[k, n])
                for n, (source, buffer) in enumerate(fields)])
            for copy in copies[k]:
                copy.start()

        row = lax.broadcasted_iota(jnp.int32, (tall, LANES), 0) - top + band * rows
        row = jnp.clip(row, 0, GRID_LAT - 1)
        sine = sine_of(colatitude(jnp.minimum(row, GRID_LAT - 1 - row)))
        sine_v[...] = sine
        zonal[...] = 0.05 / sine
        merid[...] = meridional / sine

        sign = jnp.where(band < lat // 2, 1.0, -1.0)
        mixed = (got[:, 0] + sign * got[:, 1]).reshape(2 * waves, lane_rows)
        first, second = split(mixed)
        stacked = jnp.concatenate([first, second, first], axis=0)
        line = lax.broadcasted_iota(jnp.int32, (rows + 8, lane_rows), 0)
        line = jnp.where(line < rows, line, jnp.where(line < rows + 2, line - rows - 2, line - 2))
        slot = lax.broadcasted_iota(jnp.int32, (rows + 8, lane_rows), 1)
        target = jnp.where(band < lat // 2, line + 2, rows + 1 - line)
        pick = jnp.where(slot == target, 1.0, 0.0).astype(bf16)
        factors = lax.dot_general(pick, stacked, NT, preferred_element_type=f32).astype(bf16)

        here = slice(top, top + rows)
        for n in range(names):
            left_v[n, here, :] = pltpu.roll(low_side[...], (124 - 4 * n) % LANES, 1)
            right_v[n, here, :] = pltpu.roll(high_side[...], (tail - 4 * n) % LANES, 1)

        elev_v[top - 2 : top, :] = low[0:2, :]
        elev_v[top + rows : top + rows + 2, :] = high[0:2, :]
        for n, buffer in enumerate((u_v, v_v, wy_v, depth_v, wet_v)):
            buffer[top - 1 : top, :] = low[2 + n : 3 + n, :].astype(buffer.dtype)
            behind = high[2 + n : 3 + n, :]
            behind = jnp.maximum(behind, 0.2) if buffer is depth_v else behind
            buffer[top + rows : top + rows + 1, :] = behind.astype(buffer.dtype)

        group = 4
        after = slice(top + rows, top + rows + 2)
        for t in range(0, width // LANES, group):
            begin = t * LANES
            end = min((t + group) * LANES, width)
            loading = lax.dot_general(
                factors, table[:, begin:end], (((1,), (0,)), ((), ())), preferred_element_type=f32)
            surf[here, begin:end] = loading[0:rows]
            first_lane = max(begin, LANES)
            last_lane = min(end, LANES + cols)
            inner = slice(first_lane - LANES, last_lane - LANES)
            outer = slice(first_lane, last_lane)
            cut = slice(first_lane - begin, last_lane - begin)
            load_v[:, inner] = loading[0:rows, cut]
            surf[top - 2 : top, outer] = elev_v[top - 2 : top, inner] - loading[rows : rows + 2, cut]
            surf[after, outer] = elev_v[after, inner] - loading[rows + 2 : rows + 4, cut]
        load_copy = pltpu.make_async_copy(load_v, load_out.at[0], out_sems.at[0])
        load_copy.start()

        lane8 = lax.broadcasted_iota(jnp.int32, (8, LANES), 1)
        sub8 = lax.broadcasted_iota(jnp.int32, (8, LANES), 0)
        count = width // LANES

        def part(t):
            return slice(t * LANES, (t + 1) * LANES)

        def fetch(t, rows8, n, buffer):
            if t == 0:
                return left_v[n, rows8, :]
            if t <= cols // LANES:
                return buffer[rows8, part(t - 1)].astype(f32)
            if tail == LANES:
                return right_v[n, rows8, :]
            return jnp.concatenate(
                [buffer[rows8, cols - tail : cols].astype(f32), right_v[n, rows8, tail:LANES]], axis=1)

        def keep(buffer, rows8, t, value):
            if 0 < t <= cols // LANES:
                buffer[rows8, part(t - 1)] = value
            elif t and tail < LANES:
                buffer[rows8, cols - tail : cols] = value[:, 0:tail]

        def surfaces(n, carry):
            rows8 = pl.ds(pl.multiple_of(n * 8, 8), 8)
            for t in range(count):
                surf[rows8, part(t)] = fetch(t, rows8, 0, elev_v) - surf[rows8, part(t)]
            return carry

        def vertical(ref, base, at, centre):
            before = jnp.where(sub8 == 7, ref[pl.ds(base - 8, 8), at], centre)
            after = jnp.where(sub8 == 0, ref[pl.ds(base + 8, 8), at], centre)
            return pltpu.roll(after, 7, 0) - pltpu.roll(before, 1, 0)

        def across(behind, centre, ahead):
            ahead = jnp.where(lane8 == 0, ahead, centre)
            behind = jnp.where(lane8 == LANES - 1, behind, centre)
            return pltpu.roll(ahead, LANES - 1, 1) - pltpu.roll(behind, 1, 1)

        def speeds(n):
            base = pl.multiple_of(n * 8, 8)
            rows8 = pl.ds(base, 8)
            zs = zonal[rows8, :]
            sn = sine_v[rows8, :]
            level = [surf[rows8, part(0)], surf[rows8, part(0)]]
            flow = []
            wet_before = None
            for t in range(count + 1):
                if t < count:
                    at = part(t)
                    level.append(surf[rows8, part(t + 1)] if t + 1 < count else level[-1])
                    level.pop(0) if len(level) > 3 else None
                    u = fetch(t, rows8, 1, u_v)
                    v = fetch(t, rows8, 2, v_v)
                    d = fetch(t, rows8, 4, depth_v)
                    wet = fetch(t, rows8, 5, wet_v)
                    drag = wet / (d + 0.1 * jnp.sqrt(u * u + v * v))
                    new_u = drag * (u * d + fetch(t, rows8, 3, wx_v) - (zs * d) * across(*level))
                    keep(wx_v, rows8, t, new_u)
                    flow.append(d * new_u)
                    if t and not (t > cols // LANES and tail == LANES):
                        if t <= cols // LANES:
                            push = wy_v[rows8, part(t - 1)]
                        else:
                            push = jnp.concatenate(
                                [wy_v[rows8, cols - tail : cols], jnp.zeros((8, LANES - tail), f32)], axis=1)
                        new_v = drag * (v * d + push - (meridional * d) * vertical(surf, base, at, level[1]))
                        keep(wy_v, rows8, t, new_v)
                        flux[rows8, at] = sn * d * new_v
                else:
                    flow.append(flow[-1])
                if len(flow) > 3:
                    flow.pop(0)
                back = t - 1
                if len(flow) == 3 and 0 < back <= tiles:
                    change = wet_before * (zs * across(*flow))
                    if back <= cols // LANES:
                        elev_v[rows8, part(back - 1)] = elev_v[rows8, part(back - 1)] - change
                    else:
                        elev_v[rows8, cols - tail : cols] = elev_v[rows8, cols - tail : cols] - change[:, 0:tail]
                wet_before = wet

        def levels(n):
            base = pl.multiple_of(n * 8, 8)
            rows8 = pl.ds(base, 8)
            ms = merid[rows8, :]
            for t in range(1, tiles + 1):
                change = ms * vertical(flux, base, part(t), flux[rows8, part(t)])
                if t <= cols // LANES:
                    at = part(t - 1)
                else:
                    at = slice(cols - tail, cols)
                    change = change[:, 0:tail]
                elev_v[rows8, at] = elev_v[rows8, at] - wet_v[rows8, at].astype(f32) * change

        def out_copies(k):
            inside = pl.ds(top + k * piece, piece)
            outside = pl.ds(k * piece, piece)
            return (
                pltpu.make_async_copy(wx_v.at[inside, :], vel_out.at[0, 0, outside, :], out_sems.at[1 + k]),
                pltpu.make_async_copy(wy_v.at[inside, :], vel_out.at[0, 1, outside, :], out_sems.at[1 + pieces + k]),
                pltpu.make_async_copy(elev_v.at[inside, :], elev_out.at[0, outside, :], out_sems.at[1 + 2 * pieces + k]),
            )

        def both(n, carry):
            speeds(n + 1)
            levels(n)
            return carry

        def ahead_rows(n, carry):
            speeds(n)
            return carry

        per = piece // 8
        begin = top // 8
        done = begin
        for k in range(pieces):
            for copy in copies[k]:
                copy.wait()
            lax.fori_loop(begin + k * per, begin + (k + 1) * per, surfaces, 0)
            if k == 0:
                lax.fori_loop(begin - 1, begin + 1, ahead_rows, 0)
            stop = begin + (k + 1) * per - (2 if k + 1 < pieces else 0)
            lax.fori_loop(done, stop, both, 0)
            done = stop
            if k:
                for copy in out_copies(k - 1):
                    copy.start()
        for copy in out_copies(pieces - 1):
            copy.start()
        for k in range(pieces):
            for copy in out_copies(k):
                copy.wait()
        load_copy.wait()

    flat = pltpu.VMEM((tall, cols), f32)
    big = pltpu.VMEM((tall, width), f32)
    thin = pltpu.VMEM((tall, LANES), f32)
    return pl.pallas_call(
        body,
        out_shape=(
            jax.ShapeDtypeStruct((1, rows, cols), f32),
            jax.ShapeDtypeStruct((1, 2, rows, cols), f32),
            jax.ShapeDtypeStruct((1, rows, cols), f32),
        ),
        in_specs=[SMEM, SMEM, VMEM, VMEM, VMEM, VMEM, VMEM, VMEM, ANY, ANY, ANY, ANY, ANY],
        out_specs=(ANY, ANY, ANY),
        scratch_shapes=[
            flat, flat, flat, flat, flat, flat, pltpu.VMEM((tall, cols), jnp.int32), big, big,
            pltpu.VMEM((rows, cols), f32),
            pltpu.VMEM((names, tall, LANES), f32),
            pltpu.VMEM((names, tall, LANES), f32),
            thin, thin, thin,
            pltpu.SemaphoreType.DMA((pieces, 7)),
            pltpu.SemaphoreType.DMA((1 + 3 * pieces,)),
        ],
        compiler_params=pltpu.CompilerParams(vmem_limit_bytes=52 << 20),
        name="surge_step",
    )


def local(elevation, velocity, wind_forcing, ocean_depth, wet_mask, love_factor, wavenumbers):
    members, rows, cols = elevation.shape
    lat = lax.axis_size("lat")
    lon = lax.axis_size("lon")
    waves = wavenumbers.shape[0]
    assert members == 1 and waves == lat and lat % 16 == 0 and lon % 2 == 0
    bands = lat // 2
    lane_rows = round_up(rows + 4, LANES)
    width = LANES + round_up(cols + 2, LANES)
    steps = round_up((DEGREES + 1) // 2, 8)
    place = (
        lax.axis_index("lat").astype(jnp.int32)[None],
        lax.axis_index("lon").astype(jnp.int32)[None],
    )

    send, top, bottom, side, table = edge_kernel(rows, cols, width, lat, lon, waves, lane_rows)(
        *place, wavenumbers, elevation, velocity, wind_forcing, ocean_depth, wet_mask)
    got = lax.all_to_all(send, ("lat", "lon"), split_axis=0, concat_axis=0, tiled=True)
    values = legendre_kernel(bands, rows, lane_rows, steps)(*place, wavenumbers)
    values, bottom = lax.optimization_barrier((values, bottom))
    low = lax.ppermute(bottom, "lat", [(i, (i + 1) % lat) for i in range(lat)])
    send = synthesis_kernel(bands, rows, lane_rows, steps, lat, lon)(
        *place, wavenumbers, love_factor, got, pltpu.with_memory_space_constraint(values, pltpu.HBM))
    send, top, side = lax.optimization_barrier((send, top, side))
    got = lax.all_to_all(send, ("lat", "lon"), split_axis=0, concat_axis=0, tiled=True)
    high = lax.ppermute(top, "lat", [(i + 1, i) for i in range(lat - 1)])
    low_side = lax.ppermute(side, "lon", [(i, (i + 1) % lon) for i in range(lon)])
    high_side = low_side if lon == 2 else lax.ppermute(
        side, "lon", [(i, (i - 1) % lon) for i in range(lon)])
    got = got.reshape(lat, lon, 2, lane_rows)[:, :2]
    return step_kernel(rows, cols, width, lat, waves, lane_rows)(
        *place, got, table, low, high, low_side, high_side,
        elevation, velocity, wind_forcing, ocean_depth, wet_mask)


def solution(mesh):
    return jax.shard_map(
        local,
        mesh=mesh,
        in_specs=(
            P(None, "lat", "lon"),
            P(None, None, "lat", "lon"),
            P(None, "lat", "lon"),
            P("lat", "lon"),
            P("lat", "lon"),
            P(),
            P(),
        ),
        out_specs=(P(None, "lat", "lon"), P(None, None, "lat", "lon"), P(None, "lat", "lon")),
        check_vma=False,
    )
```

```python
import math

import jax
import jax.numpy as jnp
from jax import lax
from jax.experimental import pallas as pl
from jax.experimental.pallas import tpu as pltpu
from jax.sharding import PartitionSpec as P


GRID_LAT = 3072
GRID_LON = 8640
DEGREES = 1081
LANES = 128

f32 = jnp.float32
bf16 = jnp.bfloat16
SMEM = pl.BlockSpec(memory_space=pltpu.SMEM)
VMEM = pl.BlockSpec(memory_space=pltpu.VMEM)
ANY = pl.BlockSpec(memory_space=pl.ANY)
HBM = pl.BlockSpec(memory_space=pltpu.HBM)
NT = (((1,), (1,)), ((), ()))
TN = (((0,), (0,)), ((), ()))


def round_up(value, step):
    return -(-value // step) * step


def sine_series(angle, orders=(13, 11, 9, 7, 5, 3, 1)):
    square = angle * angle
    series = None
    for order in orders:
        factor = (-1.0 if (order // 2) % 2 else 1.0) / math.factorial(order)
        series = jnp.full(angle.shape, factor, f32) if series is None else series * square + factor
    return angle * series


def cosine_of_units(units):
    turns = jnp.floor(units * (1.0 / GRID_LON) + 0.5)
    sine = sine_series((units - turns * GRID_LON) * (math.pi / GRID_LON))
    return 1.0 - 2.0 * sine * sine


def colatitude(row):
    return jnp.pi * (row.astype(f32) + 0.5) / GRID_LAT


def sine_of(angle):
    return sine_series(angle, (15, 13, 11, 9, 7, 5, 3, 1))


def split(value):
    high = value.astype(bf16)
    return high, (value - high.astype(f32)).astype(bf16)


def edge_kernel(rows, cols, width, lat, lon, waves, lane_rows):
    tail = cols % LANES or LANES

    def body(band_ref, sector_ref, waves_ref, elev, vel, wind, depth, wet,
             send, top, bottom, side, table, elev_v, wet_v, load_hi, load_lo,
             top_v, bottom_v, left_v, right_v, sems):
        band = band_ref[0]
        sector = sector_ref[0]
        first = pltpu.make_async_copy(elev.at[0], elev_v, sems.at[0])
        second = pltpu.make_async_copy(wet, wet_v, sems.at[1])
        first.start()
        second.start()
        fields = (vel.at[0, 0], vel.at[0, 1], wind.at[1], depth)
        copies = []
        for n, field in enumerate(fields):
            copies.append(pltpu.make_async_copy(field.at[pl.ds(0, 1), :], top_v.at[n], sems.at[2 + n]))
            copies.append(pltpu.make_async_copy(field.at[pl.ds(rows - 1, 1), :], bottom_v.at[n], sems.at[6 + n]))
        fields = (vel.at[0, 0], vel.at[0, 1], wind.at[0], depth)
        for n, field in enumerate(fields):
            copies.append(pltpu.make_async_copy(field.at[:, pl.ds(0, LANES)], left_v.at[n], sems.at[10 + n]))
            copies.append(pltpu.make_async_copy(
                field.at[:, pl.ds(cols - tail, tail)], right_v.at[n], sems.at[14 + n]))
        for copy in copies:
            copy.start()

        wave_row = lax.broadcasted_iota(jnp.int32, (2 * waves, LANES), 0)
        order = jnp.zeros((2 * waves, LANES), f32)
        for n in range(waves):
            order = jnp.where(wave_row // 2 == n, waves_ref[n].astype(f32), order)
        quarter = jnp.where(wave_row % 2 == 1, 0.25 * GRID_LON, 0.0)
        lane = lax.broadcasted_iota(jnp.int32, (2 * waves, LANES), 1)
        for tile in range(width // LANES):
            column = (sector * cols + (tile - 1) * LANES + lane).astype(f32)
            values = cosine_of_units(order * column - quarter)
            high, low = split(values)
            span = slice(tile * LANES, (tile + 1) * LANES)
            table[0 : 2 * waves, span] = high
            table[2 * waves : 4 * waves, span] = high
            table[4 * waves : 6 * waves, span] = low

        first.wait()
        second.wait()
        for start in range(0, rows, 8):
            here = slice(start, start + 8)
            high, low = split(elev_v[here, :] * wet_v[here, :].astype(f32))
            load_hi[here, :] = high
            load_lo[here, :] = low
        own = slice(LANES, LANES + cols)
        main_part = lax.dot_general(
            load_hi[...], table[2 * waves : 6 * waves, own], NT, preferred_element_type=f32)
        rest = lax.dot_general(load_lo[...], table[0 : 2 * waves, own], NT, preferred_element_type=f32)
        sums = (main_part[:, 0 : 2 * waves] + main_part[:, 2 * waves : 4 * waves] + rest) * (1.0 / GRID_LON)
        row = lax.broadcasted_iota(jnp.int32, (rows, lane_rows), 0)
        slot = lax.broadcasted_iota(jnp.int32, (rows, lane_rows), 1) - 2
        target = jnp.where(band < lat // 2, row, rows - 1 - row)
        pick = jnp.where(slot == target, 1.0, 0.0).astype(bf16)
        high, low = split(sums)
        lower = (sums - high.astype(f32) - low.astype(f32)).astype(bf16)
        turned = (
            lax.dot_general(high, pick, TN, preferred_element_type=f32)
            + lax.dot_general(low, pick, TN, preferred_element_type=f32)
            + lax.dot_general(lower, pick, TN, preferred_element_type=f32)
        )
        for n in range(waves):
            block = turned[2 * n : 2 * n + 2, :]
            for k in range(lon):
                send[n * lon + k, :, :] = block

        for copy in copies:
            copy.wait()
        for which, edge, start, line in ((top, top_v, 0, 0), (bottom, bottom_v, rows - 2, rows - 1)):
            u, v, wind_y, d = (edge[n] for n in range(4))
            drag = wet_v[line : line + 1, :].astype(f32) / (d + 0.1 * jnp.sqrt(u * u + v * v))
            which[0:2, :] = elev_v[start : start + 2, :]
            which[2:3, :] = d * drag * (wind_y + d * v)
            which[3:4, :] = d * d * drag
        blank = jnp.zeros((8, LANES - tail), f32)
        for start in range(0, rows, 8):
            here = slice(start, start + 8)
            lane8 = lax.broadcasted_iota(jnp.int32, (8, LANES), 1)
            left = [elev_v[here, 0:LANES]] + [left_v[n, here, :] for n in range(4)]
            left.append(wet_v[here, 0:LANES].astype(f32))
            right = [elev_v[here, cols - tail : cols]] + [right_v[n, here, :] for n in range(4)]
            right.append(wet_v[here, cols - tail : cols].astype(f32))
            right = [jnp.concatenate([x, blank], axis=1) if tail < LANES else x for x in right]
            packed = jnp.zeros((8, LANES), f32)
            for n in range(6):
                moved = pltpu.roll(left[n], 4 * n, 1) if n else left[n]
                packed = jnp.where(lane8 // 2 == 2 * n, moved, packed)
                moved = pltpu.roll(right[n], (4 * n + 2 - (tail - 2)) % LANES, 1)
                packed = jnp.where(lane8 // 2 == 2 * n + 1, moved, packed)
            side[here, :] = packed

    return pl.pallas_call(
        body,
        out_shape=(
            jax.ShapeDtypeStruct((lat * lon, 2, lane_rows), f32),
            jax.ShapeDtypeStruct((4, cols), f32),
            jax.ShapeDtypeStruct((4, cols), f32),
            jax.ShapeDtypeStruct((rows, LANES), f32),
            jax.ShapeDtypeStruct((6 * waves, width), bf16),
        ),
        in_specs=[SMEM, SMEM, SMEM, ANY, ANY, ANY, ANY, ANY],
        out_specs=(VMEM, VMEM, VMEM, VMEM, VMEM),
        scratch_shapes=[
            pltpu.VMEM((rows, cols), f32),
            pltpu.VMEM((rows, cols), jnp.int32),
            pltpu.VMEM((rows, cols), bf16),
            pltpu.VMEM((rows, cols), bf16),
            pltpu.VMEM((4, 1, cols), f32),
            pltpu.VMEM((4, 1, cols), f32),
            pltpu.VMEM((4, rows, LANES), f32),
            pltpu.VMEM((4, rows, tail), f32),
            pltpu.SemaphoreType.DMA((18,)),
        ],
        name="edge_fourier",
    )


GROW = 2.0**40
SHRINK = 2.0**-96
SHRINK_LOG = 96.0 * math.log(2.0)


def legendre_kernel(bands, rows, lane_rows, steps):
    tile = (8, LANES)
    spots = [(r, t) for r in range(0, bands, 8) for t in range(0, lane_rows, LANES)]
    pairs = 8
    parts = 4
    share = steps // parts

    def body(band_ref, sector_ref, waves_ref, values_out, coef_a, coef_s, coef_t, values, sems):
        order = waves_ref[band_ref[0]]
        parity = sector_ref[0] % 2
        order_real = order.astype(f32)
        count = coef_a.shape[0]
        for start in range(0, count, 8):
            index = (lax.broadcasted_iota(jnp.int32, tile, 0) + start).astype(f32)
            index = jnp.maximum(index, 1.0)
            double = 2.0 * (index + order_real)
            above = index + 2.0 * order_real
            below = double - 1.0
            raising = jnp.sqrt(below * (double + 1.0) / (index * above))
            ratio = raising / below
            coef_a[start : start + 8, :] = raising
            coef_s[start : start + 8, :] = ratio * above
            coef_t[start : start + 8, :] = ratio * (index - 1.0)
        ladder_rows = round_up(DEGREES, 8 * LANES) // LANES
        ladder = (
            lax.broadcasted_iota(jnp.int32, (ladder_rows, LANES), 0) * LANES
            + lax.broadcasted_iota(jnp.int32, (ladder_rows, LANES), 1)
        ).astype(f32)
        used = (ladder >= 2.0) & (ladder <= order_real)
        safe = jnp.maximum(ladder, 1.0)
        total = jnp.sum(jnp.where(used, jnp.log((2.0 * safe + 1.0) / (2.0 * safe)), 0.0))
        total = 0.5 * (total + jnp.where(order > 0, math.log(3.0), 0.0))

        gap, level, now, slope = [], [], [], []
        for r, t in spots:
            row = (
                (lax.broadcasted_iota(jnp.int32, tile, 0) + r) * rows
                + lax.broadcasted_iota(jnp.int32, tile, 1) + (t - 2)
            )
            angle = colatitude(jnp.clip(row, 0, GRID_LAT // 2 + 1))
            half = sine_series(0.5 * angle)
            cosine = 1.0 - 2.0 * half * half
            gap.append(1.0 - cosine)
            log_start = total + order_real * jnp.log(sine_of(angle))
            rung = jnp.minimum(jnp.ceil((log_start - math.log(GROW)) / SHRINK_LOG), 0.0)
            level.append(rung)
            now.append(jnp.exp(log_start - rung * SHRINK_LOG))
            slope.append(jnp.zeros(tile, f32))

        def scale_of(level):
            return jnp.where(level == 0.0, 1.0, jnp.where(level == -1.0, SHRINK, 0.0))

        def advance(k, now, slope):
            a = jnp.broadcast_to(coef_a[pl.ds(k, 1), :], tile)
            s = jnp.broadcast_to(coef_s[pl.ds(k, 1), :], tile)
            t = jnp.broadcast_to(coef_t[pl.ds(k, 1), :], tile)
            drop = [a * h for h in gap]
            kept = [t * y for y in slope]
            slope = [y - c * x for x, y, c in zip(now, kept, drop)]
            return [(s - c) * x + y for x, y, c in zip(now, kept, drop)], slope

        odd = parity == 1
        next_now, next_slope = advance(1, now, slope)
        now = [jnp.where(odd, y, x) for x, y in zip(now, next_now)]
        slope = [jnp.where(odd, y, x) for x, y in zip(slope, next_slope)]

        def block(n, carry):
            now, slope, level = carry
            scale = [scale_of(x) for x in level]
            for q in range(pairs):
                j = n * pairs + q
                for (r, t), x, y in zip(spots, now, scale):
                    values[pl.ds(j, 1), r : r + 8, t : t + LANES] = (x * y)[None]
                k = 2 * j + parity + 1
                now, slope = advance(k, now, slope)
                now, slope = advance(k + 1, now, slope)
            large = [(jnp.maximum(jnp.abs(x), jnp.abs(y)) > GROW) & (z < 0.0)
                     for x, y, z in zip(now, slope, level)]
            factor = [jnp.where(x, SHRINK, 1.0) for x in large]
            level = [jnp.where(x, z + 1.0, z) for x, z in zip(large, level)]
            return [x * y for x, y in zip(now, factor)], [x * y for x, y in zip(slope, factor)], level

        state = (now, slope, level)
        copies = []
        for k in range(parts):
            state = lax.fori_loop(k * share // pairs, (k + 1) * share // pairs, block, state)
            here = pl.ds(k * share, share)
            copies.append(pltpu.make_async_copy(values.at[here], values_out.at[here], sems.at[k]))
            copies[k].start()
        for copy in copies:
            copy.wait()

    coefs = pltpu.VMEM((2 * steps + 8, LANES), f32)
    return pl.pallas_call(
        body,
        out_shape=pltpu.HBM((steps, bands, lane_rows), f32),
        in_specs=[SMEM, SMEM, SMEM],
        out_specs=HBM,
        scratch_shapes=[coefs, coefs, coefs, pltpu.VMEM((steps, bands, lane_rows), f32),
                        pltpu.SemaphoreType.DMA((parts,))],
        compiler_params=pltpu.CompilerParams(vmem_limit_bytes=16 << 20),
        cost_estimate=pl.CostEstimate(flops=12 * steps * bands * lane_rows, transcendentals=0,
                                      bytes_accessed=4 * steps * bands * lane_rows),
        name="legendre_values",
    )


def synthesis_kernel(bands, rows, lane_rows, steps, lat, lon):
    parts = 4
    share = steps // parts

    def body(band_ref, sector_ref, waves_ref, love, got, values_in, send, mass, totals, values, sems):
        copies = []
        for k in range(parts):
            here = pl.ds(k * share, share)
            copies.append(pltpu.make_async_copy(values_in.at[here], values.at[here], sems.at[k]))
            copies[k].start()
        order = waves_ref[band_ref[0]]
        parity = sector_ref[0] % 2
        sign = jnp.where(parity == 1, -1.0, 1.0)
        slot = lax.broadcasted_iota(jnp.int32, (1, lane_rows), 1)
        inside = (slot >= 2) & (slot < rows + 2)
        for b in range(bands):
            north = got[b * lon]
            south = got[(lat - 1 - b) * lon]
            for k in range(1, lon):
                north = north + got[b * lon + k]
                south = south + got[(lat - 1 - b) * lon + k]
            row = b * rows + slot - 2
            sine = sine_of(colatitude(jnp.clip(row, 0, GRID_LAT // 2 + 1)))
            weight = (jnp.pi / (2.0 * GRID_LAT)) * sine
            both = jnp.where(inside, (north + sign * south) * weight, 0.0)
            mass[0, b : b + 1, :] = both[0:1]
            mass[1, b : b + 1, :] = both[1:2]
        sub = lax.broadcasted_iota(jnp.int32, (8, LANES), 0)
        tiles = [(r, t) for r in range(0, bands, 8) for t in range(0, lane_rows, LANES)]

        def fold(parts, shift):
            half = len(parts) // 2
            lower = sub % (2 * shift) < shift
            out = []
            for x, y in zip(parts[:half], parts[half:]):
                out.append(jnp.where(lower, y + pltpu.roll(y, 8 - shift, 0), x + pltpu.roll(x, shift, 0)))
            return out

        def analyse(n, carry):
            for c in range(2):
                parts = []
                for q in (7, 6, 5, 4, 3, 2, 1, 0):
                    acc = None
                    for r, t in tiles:
                        term = mass[c, r : r + 8, t : t + LANES] * values[n * 8 + q, r : r + 8, t : t + LANES]
                        acc = term if acc is None else acc + term
                    parts.append(acc)
                for shift in (4, 2, 1):
                    parts = fold(parts, shift)
                totals[c, pl.ds(n * 8, 8), :] = parts[0]
            return carry

        for k in range(parts):
            copies[k].wait()
            lax.fori_loop(k * share // 8, (k + 1) * share // 8, analyse, 0)
        degree = order + parity + 2 * lax.broadcasted_iota(jnp.int32, (steps, LANES), 0)
        weight = jnp.where(degree < DEGREES, 1.0 / (2.0 * degree.astype(f32) + 1.0), 0.0)
        for c in range(2):
            totals[c] = jnp.sum(totals[c], axis=1, keepdims=True) * weight

        def synthesise(n, carry):
            carry = list(carry)
            for q in range(8):
                j = n * 8 + q
                weight = love[jnp.minimum(order + parity + 2 * j, DEGREES - 1)]
                factors = [jnp.broadcast_to(totals[c, pl.ds(j, 1), :], (8, LANES)) * weight for c in range(2)]
                for i, (r, t) in enumerate(tiles):
                    value = values[j, r : r + 8, t : t + LANES]
                    for c in range(2):
                        carry[2 * i + c] = carry[2 * i + c] + factors[c] * value
            return tuple(carry)

        zero = jnp.zeros((8, LANES), f32)
        found = lax.fori_loop(0, steps // 8, synthesise, (zero,) * (2 * len(tiles)))
        for b in range(bands):
            for t in range(0, lane_rows, LANES):
                i = tiles.index((b // 8 * 8, t))
                for c in range(2):
                    line = found[2 * i + c][b % 8 : b % 8 + 1, :]
                    for k in range(lon):
                        send[b * lon + k, c : c + 1, t : t + LANES] = line
                        send[(lat - 1 - b) * lon + k, c : c + 1, t : t + LANES] = line

    return pl.pallas_call(
        body,
        out_shape=jax.ShapeDtypeStruct((lat * lon, 2, lane_rows), f32),
        in_specs=[SMEM, SMEM, SMEM, SMEM, VMEM, HBM],
        out_specs=VMEM,
        scratch_shapes=[
            pltpu.VMEM((2, bands, lane_rows), f32),
            pltpu.VMEM((2, steps, LANES), f32),
            pltpu.VMEM((steps, bands, lane_rows), f32),
            pltpu.SemaphoreType.DMA((parts,)),
        ],
        compiler_params=pltpu.CompilerParams(vmem_limit_bytes=16 << 20),
        name="degree_sums",
    )


def step_kernel(rows, cols, width, lat, waves, lane_rows):
    tail = cols % LANES or LANES
    tiles = -(-cols // LANES)
    tall = rows + 32
    top = 16
    meridional = 0.1 * GRID_LAT / GRID_LON
    pieces = 6 if rows % 96 == 0 else 1
    piece = rows // pieces
    names = 6

    def body(band_ref, sector_ref, got, table, low, high, low_side, high_side,
             elev, vel, wind, depth, wet, elev_out, vel_out, load_out,
             elev_v, u_v, v_v, wx_v, wy_v, depth_v, wet_v, surf, flux, load_v,
             left_v, right_v, zonal, sine_v, merid, sems, out_sems):
        band = band_ref[0]
        fields = (
            (elev.at[0], elev_v), (depth, depth_v), (wet, wet_v), (vel.at[0, 0], u_v),
            (vel.at[0, 1], v_v), (wind.at[1], wy_v), (wind.at[0], wx_v),
        )
        copies = []
        for k in range(pieces):
            inside = pl.ds(top + k * piece, piece)
            outside = pl.ds(k * piece, piece)
            copies.append([pltpu.make_async_copy(
                source.at[outside, :], buffer.at[inside, :], sems.at[k, n])
                for n, (source, buffer) in enumerate(fields)])
            for copy in copies[k]:
                copy.start()

        row = lax.broadcasted_iota(jnp.int32, (tall, LANES), 0) - top + band * rows
        row = jnp.clip(row, 0, GRID_LAT - 1)
        sine = sine_of(colatitude(jnp.minimum(row, GRID_LAT - 1 - row)))
        sine_v[...] = sine
        zonal[...] = 0.05 / sine
        merid[...] = meridional / sine

        sign = jnp.where(band < lat // 2, 1.0, -1.0)
        mixed = (got[:, 0] + sign * got[:, 1]).reshape(2 * waves, lane_rows)
        first, second = split(mixed)
        stacked = jnp.concatenate([first, second, first], axis=0)
        line = lax.broadcasted_iota(jnp.int32, (rows + 8, lane_rows), 0)
        line = jnp.where(line < rows, line, jnp.where(line < rows + 2, line - rows - 2, line - 2))
        slot = lax.broadcasted_iota(jnp.int32, (rows + 8, lane_rows), 1)
        target = jnp.where(band < lat // 2, line + 2, rows + 1 - line)
        pick = jnp.where(slot == target, 1.0, 0.0).astype(bf16)
        factors = lax.dot_general(pick, stacked, NT, preferred_element_type=f32).astype(bf16)

        here = slice(top, top + rows)
        for n in range(names):
            left_v[n, here, :] = pltpu.roll(low_side[...], (124 - 4 * n) % LANES, 1)
            right_v[n, here, :] = pltpu.roll(high_side[...], (tail - 4 * n) % LANES, 1)

        elev_v[top - 2 : top, :] = low[0:2, :]
        elev_v[top + rows : top + rows + 2, :] = high[0:2, :]
        for line, block in ((top - 1, low), (top + rows, high)):
            push, give = block[2:3, :], block[3:4, :]
            spot = slice(line, line + 1)
            u_v[spot, :] = jnp.zeros((1, cols), f32)
            v_v[spot, :] = jnp.zeros((1, cols), f32)
            wy_v[spot, :] = push
            depth_v[spot, :] = jnp.where(give > 0.0, give, 1.0)
            wet_v[spot, :] = jnp.where(give > 0.0, 1, 0)

        group = 4
        after = slice(top + rows, top + rows + 2)
        for t in range(0, width // LANES, group):
            begin = t * LANES
            end = min((t + group) * LANES, width)
            loading = lax.dot_general(
                factors, table[:, begin:end], (((1,), (0,)), ((), ())), preferred_element_type=f32)
            surf[here, begin:end] = loading[0:rows]
            first_lane = max(begin, LANES)
            last_lane = min(end, LANES + cols)
            inner = slice(first_lane - LANES, last_lane - LANES)
            outer = slice(first_lane, last_lane)
            cut = slice(first_lane - begin, last_lane - begin)
            load_v[:, inner] = loading[0:rows, cut]
            surf[top - 2 : top, outer] = elev_v[top - 2 : top, inner] - loading[rows : rows + 2, cut]
            surf[after, outer] = elev_v[after, inner] - loading[rows + 2 : rows + 4, cut]
        load_copy = pltpu.make_async_copy(load_v, load_out.at[0], out_sems.at[0])
        load_copy.start()

        lane8 = lax.broadcasted_iota(jnp.int32, (8, LANES), 1)
        sub8 = lax.broadcasted_iota(jnp.int32, (8, LANES), 0)
        count = width // LANES

        def part(t):
            return slice(t * LANES, (t + 1) * LANES)

        def fetch(t, rows8, n, buffer):
            if t == 0:
                return left_v[n, rows8, :]
            if t <= cols // LANES:
                return buffer[rows8, part(t - 1)].astype(f32)
            if tail == LANES:
                return right_v[n, rows8, :]
            return jnp.concatenate(
                [buffer[rows8, cols - tail : cols].astype(f32), right_v[n, rows8, tail:LANES]], axis=1)

        def keep(buffer, rows8, t, value):
            if 0 < t <= cols // LANES:
                buffer[rows8, part(t - 1)] = value
            elif t and tail < LANES:
                buffer[rows8, cols - tail : cols] = value[:, 0:tail]

        def surfaces(n, carry):
            rows8 = pl.ds(pl.multiple_of(n * 8, 8), 8)
            for t in range(count):
                surf[rows8, part(t)] = fetch(t, rows8, 0, elev_v) - surf[rows8, part(t)]
            return carry

        def vertical(ref, base, at, centre):
            before = jnp.where(sub8 == 7, ref[pl.ds(base - 8, 8), at], centre)
            after = jnp.where(sub8 == 0, ref[pl.ds(base + 8, 8), at], centre)
            return pltpu.roll(after, 7, 0) - pltpu.roll(before, 1, 0)

        def across(behind, centre, ahead):
            ahead = jnp.where(lane8 == 0, ahead, centre)
            behind = jnp.where(lane8 == LANES - 1, behind, centre)
            return pltpu.roll(ahead, LANES - 1, 1) - pltpu.roll(behind, 1, 1)

        def speeds(n):
            base = pl.multiple_of(n * 8, 8)
            rows8 = pl.ds(base, 8)
            zs = zonal[rows8, :]
            sn = sine_v[rows8, :]
            level = [surf[rows8, part(0)], surf[rows8, part(0)]]
            flow = []
            wet_before = None
            for t in range(count + 1):
                if t < count:
                    at = part(t)
                    level.append(surf[rows8, part(t + 1)] if t + 1 < count else level[-1])
                    level.pop(0) if len(level) > 3 else None
                    u = fetch(t, rows8, 1, u_v)
                    v = fetch(t, rows8, 2, v_v)
                    d = fetch(t, rows8, 4, depth_v)
                    wet = fetch(t, rows8, 5, wet_v)
                    drag = wet / (d + 0.1 * jnp.sqrt(u * u + v * v))
                    new_u = drag * (u * d + fetch(t, rows8, 3, wx_v) - (zs * d) * across(*level))
                    keep(wx_v, rows8, t, new_u)
                    flow.append(d * new_u)
                    if t and not (t > cols // LANES and tail == LANES):
                        if t <= cols // LANES:
                            push = wy_v[rows8, part(t - 1)]
                        else:
                            push = jnp.concatenate(
                                [wy_v[rows8, cols - tail : cols], jnp.zeros((8, LANES - tail), f32)], axis=1)
                        new_v = drag * (v * d + push - (meridional * d) * vertical(surf, base, at, level[1]))
                        keep(wy_v, rows8, t, new_v)
                        flux[rows8, at] = sn * d * new_v
                else:
                    flow.append(flow[-1])
                if len(flow) > 3:
                    flow.pop(0)
                back = t - 1
                if len(flow) == 3 and 0 < back <= tiles:
                    change = wet_before * (zs * across(*flow))
                    if back <= cols // LANES:
                        elev_v[rows8, part(back - 1)] = elev_v[rows8, part(back - 1)] - change
                    else:
                        elev_v[rows8, cols - tail : cols] = elev_v[rows8, cols - tail : cols] - change[:, 0:tail]
                wet_before = wet

        def levels(n):
            base = pl.multiple_of(n * 8, 8)
            rows8 = pl.ds(base, 8)
            ms = merid[rows8, :]
            for t in range(1, tiles + 1):
                change = ms * vertical(flux, base, part(t), flux[rows8, part(t)])
                if t <= cols // LANES:
                    at = part(t - 1)
                else:
                    at = slice(cols - tail, cols)
                    change = change[:, 0:tail]
                elev_v[rows8, at] = elev_v[rows8, at] - wet_v[rows8, at].astype(f32) * change

        def out_copies(k):
            inside = pl.ds(top + k * piece, piece)
            outside = pl.ds(k * piece, piece)
            return (
                pltpu.make_async_copy(wx_v.at[inside, :], vel_out.at[0, 0, outside, :], out_sems.at[1 + k]),
                pltpu.make_async_copy(wy_v.at[inside, :], vel_out.at[0, 1, outside, :], out_sems.at[1 + pieces + k]),
                pltpu.make_async_copy(elev_v.at[inside, :], elev_out.at[0, outside, :], out_sems.at[1 + 2 * pieces + k]),
            )

        def both(n, carry):
            speeds(n + 1)
            levels(n)
            return carry

        def ahead_rows(n, carry):
            speeds(n)
            return carry

        per = piece // 8
        begin = top // 8
        done = begin
        for k in range(pieces):
            for copy in copies[k]:
                copy.wait()
            lax.fori_loop(begin + k * per, begin + (k + 1) * per, surfaces, 0)
            if k == 0:
                lax.fori_loop(begin - 1, begin + 1, ahead_rows, 0)
            stop = begin + (k + 1) * per - (2 if k + 1 < pieces else 0)
            lax.fori_loop(done, stop, both, 0)
            done = stop
            if k:
                for copy in out_copies(k - 1):
                    copy.start()
        for copy in out_copies(pieces - 1):
            copy.start()
        for k in range(pieces):
            for copy in out_copies(k):
                copy.wait()
        load_copy.wait()

    flat = pltpu.VMEM((tall, cols), f32)
    big = pltpu.VMEM((tall, width), f32)
    thin = pltpu.VMEM((tall, LANES), f32)
    return pl.pallas_call(
        body,
        out_shape=(
            jax.ShapeDtypeStruct((1, rows, cols), f32),
            jax.ShapeDtypeStruct((1, 2, rows, cols), f32),
            jax.ShapeDtypeStruct((1, rows, cols), f32),
        ),
        in_specs=[SMEM, SMEM, VMEM, VMEM, VMEM, VMEM, VMEM, VMEM, ANY, ANY, ANY, ANY, ANY],
        out_specs=(ANY, ANY, ANY),
        scratch_shapes=[
            flat, flat, flat, flat, flat, flat, pltpu.VMEM((tall, cols), jnp.int32), big, big,
            pltpu.VMEM((rows, cols), f32),
            pltpu.VMEM((names, tall, LANES), f32),
            pltpu.VMEM((names, tall, LANES), f32),
            thin, thin, thin,
            pltpu.SemaphoreType.DMA((pieces, 7)),
            pltpu.SemaphoreType.DMA((1 + 3 * pieces,)),
        ],
        compiler_params=pltpu.CompilerParams(vmem_limit_bytes=52 << 20),
        name="surge_step",
    )


def local(elevation, velocity, wind_forcing, ocean_depth, wet_mask, love_factor, wavenumbers):
    members, rows, cols = elevation.shape
    lat = lax.axis_size("lat")
    lon = lax.axis_size("lon")
    waves = wavenumbers.shape[0]
    assert members == 1 and waves == lat and lat % 16 == 0 and lon % 2 == 0
    bands = lat // 2
    lane_rows = round_up(rows + 4, LANES)
    width = LANES + round_up(cols + 2, LANES)
    steps = round_up((DEGREES + 1) // 2, 8)
    place = (
        lax.axis_index("lat").astype(jnp.int32)[None],
        lax.axis_index("lon").astype(jnp.int32)[None],
    )

    send, top, bottom, side, table = edge_kernel(rows, cols, width, lat, lon, waves, lane_rows)(
        *place, wavenumbers, elevation, velocity, wind_forcing, ocean_depth, wet_mask)
    got = lax.all_to_all(send, ("lat", "lon"), split_axis=0, concat_axis=0, tiled=True)
    values = legendre_kernel(bands, rows, lane_rows, steps)(*place, wavenumbers)
    values, bottom = lax.optimization_barrier((values, bottom))
    low = lax.ppermute(bottom, "lat", [(i, (i + 1) % lat) for i in range(lat)])
    send = synthesis_kernel(bands, rows, lane_rows, steps, lat, lon)(
        *place, wavenumbers, love_factor, got, pltpu.with_memory_space_constraint(values, pltpu.HBM))
    send, top, side = lax.optimization_barrier((send, top, side))
    got = lax.all_to_all(send, ("lat", "lon"), split_axis=0, concat_axis=0, tiled=True)
    high = lax.ppermute(top, "lat", [(i + 1, i) for i in range(lat - 1)])
    low_side = lax.ppermute(side, "lon", [(i, (i + 1) % lon) for i in range(lon)])
    high_side = low_side if lon == 2 else lax.ppermute(
        side, "lon", [(i, (i - 1) % lon) for i in range(lon)])
    got = got.reshape(lat, lon, 2, lane_rows)[:, :2]
    return step_kernel(rows, cols, width, lat, waves, lane_rows)(
        *place, got, table, low, high, low_side, high_side,
        elevation, velocity, wind_forcing, ocean_depth, wet_mask)


def solution(mesh):
    return jax.shard_map(
        local,
        mesh=mesh,
        in_specs=(
            P(None, "lat", "lon"),
            P(None, None, "lat", "lon"),
            P(None, "lat", "lon"),
            P("lat", "lon"),
            P("lat", "lon"),
            P(),
            P(),
        ),
        out_specs=(P(None, "lat", "lon"), P(None, None, "lat", "lon"), P(None, "lat", "lon")),
        check_vma=False,
    )
```
